32 devices in a mesh: seq: 8 (over z, y), head: 4 (over x, core).
Axes of the slice: x: 2, y: 2, z: 4, core: 2. Of those that a mesh axis runs over, the one named last changes fastest.
Arguments:
- frames: bfloat16 [8192, 768], P(('seq', 'head')), may hold values from -6 to 6
- condition: bfloat16 [8, 768], P('seq'), may hold values from -6 to 6
- captions: bfloat16 [8, 256, 768], P('seq'), may hold values from -6 to 6
- caption_lengths: int32 [8], P('seq'), may hold values from 5 to 256, as said below
- modulation_weight: bfloat16 [768, 4608], P('seq'), may hold values from -0.21875 to 0.21875
- modulation_bias: bfloat16 [4608], P('seq'), may hold values from -6 to 6
- self_weight: bfloat16 [768, 2304], P('seq'), may hold values from -0.21875 to 0.21875
- self_out: bfloat16 [768, 768], P('seq'), may hold values from -4 to 4
- self_bias: bfloat16 [768], P('seq'), may hold values from -6 to 6
- cross_gain: bfloat16 [768], P('seq'), may hold values from 0.099609375 to 1.8984375
- cross_query: bfloat16 [768, 768], P('seq'), may hold values from -0.21875 to 0.21875
- cross_pair: bfloat16 [768, 1536], P('seq'), may hold values from -0.21875 to 0.21875
- cross_out: bfloat16 [768, 768], P('seq'), may hold values from -0.75 to 0.75
- cross_bias: bfloat16 [768], P('seq'), may hold values from -6 to 6
- up_weight: bfloat16 [768, 3072], P('seq', 'head'), may hold values from -0.21875 to 0.21875
- up_bias: bfloat16 [3072], P('head'), may hold values from -6 to 6
- down_weight: bfloat16 [3072, 768], P('head', 'seq'), may hold values from -0.109375 to 0.109375
- down_bias: bfloat16 [768], P('seq'), may hold values from -6 to 6
- cotangent: bfloat16 [8192, 768], P(('seq', 'head')), may hold values from -6 to 6
Outputs:
- output_frames: bfloat16 [8192, 768], P(('seq', 'head'))
- grad_frames: float32 [8192, 768], P(('seq', 'head'))
- grad_condition: float32 [8, 768], P('seq', 'head')
- grad_captions: float32 [8, 256, 768], P('seq', None, 'head')
- grad_modulation_weight: float32 [768, 4608], P(('seq', 'head'))
- grad_modulation_bias: float32 [4608], P(('seq', 'head'))
- grad_self_weight: float32 [768, 2304], P(('seq', 'head'))
- grad_self_out: float32 [768, 768], P(('seq', 'head'))
- grad_self_bias: float32 [768], P(('seq', 'head'))
- grad_cross_gain: float32 [768], P(('seq', 'head'))
- grad_cross_query: float32 [768, 768], P(('seq', 'head'))
- grad_cross_pair: float32 [768, 1536], P(('seq', 'head'))
- grad_cross_out: float32 [768, 768], P(('seq', 'head'))
- grad_cross_bias: float32 [768], P(('seq', 'head'))
- grad_up_weight: float32 [768, 3072], P('seq', 'head')
- grad_up_bias: float32 [3072], P('head')
- grad_down_weight: float32 [3072, 768], P('head', 'seq')
- grad_down_bias: float32 [768], P(('seq', 'head'))
The draws below stay inside these ranges and needn't reach their ends.
Inputs may be any that keep to these rules, and one draw needn't show every extreme that they name: `caption_lengths`: every sequence's caption uses between 5 and 256 slots, the first ones; some sequence uses all 256.
All inputs are finite; a program needn't handle non-finite values.
Results may differ from the reference program's by a relative error of at most 0.018.
The reference program's roundings to bfloat16 on the way count: a program that leaves them out, or rounds other values in their place, can miss the bound.
Values may be sent and summed in bfloat16 or wider, within the bound.
No kernel may reach another device: no remote copies, remote signals or barrier semaphores. Data moves between devices by JAX's collectives and lax.ppermute only.
A program may use at most 256 MiB of HBM per device.

```python
from functools import partial
import jax
import jax.numpy as jnp
from jax import lax

D = 768
H = 12
HD = 64
FF = 3072
DT = 768
TL = 256
SEQ_LEN = 1024
SEQUENCES = 8
FRAMES = 8192


def draw_caption_lengths(key, part):
    first, second = jax.random.split(jax.random.fold_in(key, 17))
    lengths = jax.random.randint(first, (SEQUENCES,), 5, TL + 1)
    chosen = jax.random.randint(second, (), 0, SEQUENCES)
    return jnp.where(jnp.arange(SEQUENCES) == chosen, TL, lengths).astype(jnp.int32)


def levels(own_key, dims, cuts, low, largest):
    def one(axis_at, blocks):
        steps = jax.random.uniform(jax.random.fold_in(jax.random.fold_in(own_key, 6), axis_at), (blocks,), jnp.float32, low / len(cuts), largest / len(cuts))
        return jnp.repeat(jnp.exp(steps), dims[axis_at] // blocks).reshape((-1,) + (1,) * (len(dims) - axis_at - 1))

    loudness = one(*cuts[0])
    for cut in cuts[1:]:
        loudness = loudness * one(*cut)
    return loudness


def scatter_about(rng, dims, scale, limit, shards=(), held_as=jnp.bfloat16):
    values = jax.random.normal(rng, dims, jnp.float32) * scale
    if len(shards) > 0:
        values = levels(rng, dims, shards, -0.22, 0.18) * values
    return jnp.clip(values, min=-limit, max=limit).astype(held_as)


def setup_inputs(seed: int = 0) -> dict:
    key_list = jax.random.split(jax.random.key(seed), 20)
    return {
        "frames": scatter_about(key_list[0], (FRAMES, D), 1.0, 6.0, ((0, 32),)),
        "condition": scatter_about(key_list[1], (SEQUENCES, D), 1.0, 6.0, ((0, 8),)),
        "captions": scatter_about(key_list[2], (SEQUENCES, TL, DT), 1.0, 6.0, ((0, 8),)),
        "caption_lengths": draw_caption_lengths(jax.random.fold_in(key_list[19], 71), 0),
        "modulation_weight": scatter_about(key_list[4], (D, 6 * D), D ** -0.5, 0.21875, ((0, 8),)),
        "modulation_bias": scatter_about(key_list[5], (6 * D,), 1.0, 6.0, ((0, 8),)),
        "self_weight": scatter_about(key_list[6], (D, 3 * D), D ** -0.5, 0.21875, ((0, 8),)),
        "self_out": scatter_about(key_list[7], (D, D), (max(1, SEQ_LEN // 512)) ** -0.5, 4.0, ((0, 8),)),
        "self_bias": scatter_about(key_list[8], (D,), 1.0, 6.0, ((0, 8),)),
        "cross_gain": jnp.clip(1.0 + 0.18 * jax.random.normal(key_list[9], (D,), jnp.float32), 0.099609375, 1.8984375).astype(jnp.bfloat16),
        "cross_query": scatter_about(key_list[10], (D, D), D ** -0.5, 0.21875, ((0, 8),)),
        "cross_pair": scatter_about(key_list[11], (DT, 2 * D), DT ** -0.5, 0.21875, ((0, 8),)),
        "cross_out": scatter_about(key_list[12], (D, D), 64 ** -0.5, 0.75, ((0, 8),)),
        "cross_bias": scatter_about(key_list[13], (D,), 1.0, 6.0, ((0, 8),)),
        "up_weight": scatter_about(key_list[14], (D, FF), D ** -0.5, 0.21875, ((0, 8), (1, 4))),
        "up_bias": scatter_about(key_list[15], (FF,), 1.0, 6.0, ((0, 4),)),
        "down_weight": scatter_about(key_list[16], (FF, D), FF ** -0.5, 0.109375, ((0, 4), (1, 8))),
        "down_bias": scatter_about(key_list[17], (D,), 1.0, 6.0, ((0, 8),)),
        "cotangent": scatter_about(key_list[18], (FRAMES, D), 1.0, 6.0, ((0, 32),)),
    }


@jax.custom_vjp
def low(v):
    return lax.optimization_barrier(v.astype(jnp.bfloat16)).astype(jnp.float32)

@jax.custom_vjp
def low_back(v):
    return v

def low_keep(v):
    return (low(v), None)

def low_pass(kept, grad):
    return (grad,)

def back_keep(v):
    return (v, None)

def back_low(kept, grad):
    return (low(grad),)
low.defvjp(low_keep, low_pass)
low_back.defvjp(back_keep, back_low)

def rounded_both(values):
    return low(low_back(values))

def product(left, right):
    return jnp.dot(left, right, precision=lax.Precision.HIGHEST)

def normed(values):
    center = values - lax.optimization_barrier(jnp.mean(values, axis=-1, keepdims=True))
    spread = lax.optimization_barrier(jnp.mean(center * center, axis=-1, keepdims=True))
    return center * lax.rsqrt(spread + 1e-06)

def attend(queries, key_rows, value_rows, visible):
    scores = low_back(jnp.einsum('qhd,khd->hqk', queries, key_rows, precision=lax.Precision.HIGHEST) * 0.125)
    if visible is not None:
        scores = jnp.where(visible[None, None, :], scores, -1e+30)
    weights = jax.nn.softmax(scores, axis=-1)
    mixed = jnp.einsum('hqk,khd->qhd', low(weights), value_rows, precision=lax.Precision.HIGHEST)
    return mixed.reshape(mixed.shape[0], -1)

def layer(params, frames, cond, caption, length):
    modulation_weight, modulation_bias, self_weight, self_out, self_bias, cross_gain, cross_query, cross_pair, cross_out, cross_bias, up_weight, up_bias, down_weight, down_bias = params
    modulation = product(low(jax.nn.silu(cond)), modulation_weight) + modulation_bias
    shift_one, scale_one, gate_one, shift_two, scale_two, gate_two = jnp.split(modulation, 6)
    first_in = low(normed(frames) * (1.0 + scale_one) + shift_one)
    joint = rounded_both(product(first_in, self_weight)).reshape(SEQ_LEN, 3, H, HD)
    self_mixed = rounded_both(attend(joint[:, 0], joint[:, 1], joint[:, 2], None))
    self_proj = low_back(product(self_mixed, self_out) + self_bias)
    after_self = frames + gate_one * self_proj
    second_in = low(normed(after_self) * cross_gain)
    cross_q = rounded_both(product(second_in, cross_query)).reshape(SEQ_LEN, H, HD)
    pair = rounded_both(product(caption, cross_pair)).reshape(TL, 2, H, HD)
    visible = jnp.arange(TL) < length
    cross_mixed = rounded_both(attend(cross_q, pair[:, 0], pair[:, 1], visible))
    cross_proj = low_back(product(cross_mixed, cross_out) + cross_bias)
    after_cross = after_self + cross_proj
    third_in = low(normed(after_cross) * (1.0 + scale_two) + shift_two)
    up_values = low_back(product(third_in, up_weight) + up_bias)
    hidden = low(jax.nn.gelu(up_values, approximate=True))
    feed = low_back(product(hidden, down_weight) + down_bias)
    return after_cross + gate_two * feed

def one_sequence(params, batch_item):
    return layer(params, batch_item[0], batch_item[1], batch_item[2], batch_item[3])

def reference(frames, condition, captions, caption_lengths, modulation_weight, modulation_bias, self_weight, self_out, self_bias, cross_gain, cross_query, cross_pair, cross_out, cross_bias, up_weight, up_bias, down_weight, down_bias, cotangent):
    params = tuple((item.astype(jnp.float32) for item in (modulation_weight, modulation_bias, self_weight, self_out, self_bias, cross_gain, cross_query, cross_pair, cross_out, cross_bias, up_weight, up_bias, down_weight, down_bias)))

    def forward(weights, frame_rows, cond_rows, caption_rows):
        per_sequence = frame_rows.reshape(SEQUENCES, SEQ_LEN, D)
        mapped = lax.map(jax.checkpoint(partial(one_sequence, weights)), (per_sequence, cond_rows, caption_rows, caption_lengths))
        return mapped.reshape(FRAMES, D)
    result, pullback = jax.vjp(forward, params, frames.astype(jnp.float32), condition.astype(jnp.float32), captions.astype(jnp.float32))
    grad_params, grad_frames, grad_condition, grad_captions = pullback(cotangent.astype(jnp.float32))
    grad_mw, grad_mb, grad_sw, grad_so, grad_sb, grad_cg, grad_cq, grad_cp, grad_co, grad_cb, grad_uw, grad_ub, grad_dw, grad_db = grad_params
    return (result.astype(jnp.bfloat16), grad_frames, grad_condition, grad_captions, grad_mw, grad_mb, grad_sw, grad_so, grad_sb, grad_cg, grad_cq, grad_cp, grad_co, grad_cb, grad_uw, grad_ub, grad_dw, grad_db)
```

```python
import jax
import jax.numpy as jnp
from jax import lax
from jax.sharding import PartitionSpec as P

HD = 64
BF = jnp.bfloat16
F32 = jnp.float32


def mm(a, b, ca=1, cb=0):
    return lax.dot_general(a, b, (((ca,), (cb,)), ((), ())), preferred_element_type=F32)


def swap(x, bit):
    return lax.ppermute(x, "head", [(i, i ^ bit) for i in range(4)])


def swap_rows(x, bit):
    blocks = jnp.split(swap(x, bit), 4, axis=0)
    return jnp.concatenate([blocks[i ^ bit] for i in range(4)], axis=0)


def head_rel(x, swap=swap):
    near = swap(x, 1)
    far = swap(x, 2)
    return [x, near, far, swap(far, 1)]


def pick(parts, index):
    low, high = (index & 1) == 1, (index & 2) == 2
    return jnp.where(
        high, jnp.where(low, parts[3], parts[2]), jnp.where(low, parts[1], parts[0])
    )


def head_sum(chunks, swap=swap):
    a, b = swap(chunks[1], 1), swap(chunks[3], 1)
    mine = chunks[0].astype(F32) + a.astype(F32)
    other = (chunks[2].astype(F32) + b.astype(F32)).astype(chunks[0].dtype)
    return mine + swap(other, 2).astype(F32)


def seq_gather(x):
    n = lax.axis_size("seq")
    sent = jnp.broadcast_to(x[None], (n, *x.shape))
    return lax.all_to_all(sent, "seq", split_axis=0, concat_axis=0, tiled=True)


def seq_sum(x):
    return lax.all_to_all(x, "seq", split_axis=0, concat_axis=0, tiled=True).astype(F32).sum(0)


def stats(v):
    mean = jnp.mean(v, axis=-1, keepdims=True)
    center = v - mean
    r = lax.rsqrt(jnp.mean(center * center, axis=-1, keepdims=True) + 1e-6)
    return center * r, r


def normback(n, r, e):
    return r * (
        e - jnp.mean(e, axis=-1, keepdims=True) - n * jnp.mean(e * n, axis=-1, keepdims=True)
    )


def attend(q, k, v, visible):
    rows, width = q.shape
    heads = width // HD
    qh, kh, vh = (t.reshape(t.shape[0], heads, HD) for t in (q, k, v))
    s = jnp.einsum("qhd,khd->hqk", qh, kh, preferred_element_type=F32) * 0.125
    if visible is not None:
        s = jnp.where(visible[None, None, :], s, -1e30)
    w = jnp.exp(s - jnp.max(s, axis=-1, keepdims=True))
    p = (w / jnp.sum(w, axis=-1, keepdims=True)).astype(BF)
    o = jnp.einsum("hqk,khd->qhd", p, vh, preferred_element_type=F32)
    return o.astype(BF).reshape(rows, width), p


def attend_back(q, k, v, p, do):
    rows, width = q.shape
    heads = width // HD
    qh, kh, vh, dh = (t.reshape(t.shape[0], heads, HD) for t in (q, k, v, do))
    dv = jnp.einsum("hqk,qhd->khd", p, dh, preferred_element_type=F32)
    dp = jnp.einsum("qhd,khd->hqk", dh, vh, preferred_element_type=F32)
    pf = p.astype(F32)
    inner = jnp.sum(pf * dp, axis=-1, keepdims=True)
    ds = (pf * (dp - inner)).astype(BF)
    dq = jnp.einsum("hqk,khd->qhd", ds, kh, preferred_element_type=F32) * 0.125
    dk = jnp.einsum("hqk,qhd->khd", ds, qh, preferred_element_type=F32) * 0.125
    return (
        dq.astype(BF).reshape(rows, width),
        dk.astype(BF).reshape(-1, width),
        dv.astype(BF).reshape(-1, width),
    )


def on_device(
    frames,
    condition,
    captions,
    caption_lengths,
    modulation_weight,
    modulation_bias,
    self_weight,
    self_out,
    self_bias,
    cross_gain,
    cross_query,
    cross_pair,
    cross_out,
    cross_bias,
    up_weight,
    up_bias,
    down_weight,
    down_bias,
    cotangent,
):
    n = lax.axis_size("seq")
    h = lax.axis_index("head")
    s = lax.axis_index("seq")
    rows, width = frames.shape
    hw = width // 4
    kr = self_weight.shape[0]
    own = kr // 4
    total = rows * 4

    def cols(w, base):
        return lax.dynamic_slice_in_dim(w, base + h * hw, hw, 1)

    small = jnp.concatenate([self_bias, cross_bias, cross_gain, down_bias])[None]
    sent = jnp.concatenate(
        [condition.reshape(n, kr), jnp.broadcast_to(small, (n, 4 * kr))], axis=1
    )
    got = lax.all_to_all(sent, "seq", split_axis=0, concat_axis=0, tiled=True)
    cond_own = jax.nn.silu(got[:, :kr].astype(F32)).astype(BF)
    vectors = got[:, kr:].astype(F32).reshape(n, 4, kr).transpose(1, 0, 2).reshape(4, width)
    out_bias, co_bias, gain, dn_bias = vectors[0], vectors[1], vectors[2], vectors[3]
    mod_part = mm(cond_own, modulation_weight) + lax.dynamic_update_slice(
        jnp.zeros((n * modulation_bias.shape[0],), F32),
        modulation_bias.astype(F32),
        (s * modulation_bias.shape[0],),
    )
    w_self = seq_gather(
        jnp.concatenate([cols(self_weight, 0), cols(self_weight, width), cols(self_weight, 2 * width)], axis=1)
    ).reshape(width, 3 * hw)
    mod = seq_sum(mod_part[:, None])[0]
    two = seq_gather(
        jnp.concatenate(
            [cols(self_out, 0), cols(cross_query, 0), cols(cross_pair, 0), cols(cross_pair, width)], axis=1
        )
    ).reshape(width, 4 * hw)
    three = lax.all_gather(
        jnp.concatenate([cols(cross_out, 0), up_weight, down_weight.T], axis=1), "seq", axis=0, tiled=True
    )
    x = jnp.concatenate(head_rel(frames), axis=0).astype(F32)
    g = jnp.concatenate(head_rel(cotangent), axis=0).astype(F32)
    w_query, w_pair = two[:, hw : 2 * hw], two[:, 2 * hw :]
    out_parts = head_rel(two[:, :hw])
    w_out = jnp.concatenate([pick(out_parts, h ^ a) for a in range(4)], axis=1)
    cross_parts = head_rel(three[:, :hw])
    w_cross = jnp.concatenate([pick(cross_parts, h ^ a) for a in range(4)], axis=1)
    w_up, w_down = three[:, hw : hw + up_weight.shape[1]], three[:, hw + up_weight.shape[1] :]

    shift1, scale1, gate1, shift2, scale2, gate2 = jnp.split(mod, 6)
    n1, r1 = stats(x)
    first = (n1 * (1.0 + scale1) + shift1).astype(BF)
    joint = mm(first, w_self).astype(BF)
    q, k, v = joint[:, :hw], joint[:, hw : 2 * hw], joint[:, 2 * hw :]
    sm_own, probs = attend(q, k, v, None)
    sm_parts = head_rel(sm_own, swap_rows)
    sm = jnp.concatenate([pick(sm_parts, h ^ a) for a in range(4)], axis=1)
    self_proj = mm(sm, w_out) + out_bias
    after_self = x + gate1 * self_proj
    n2, r2 = stats(after_self)
    second = (n2 * gain).astype(BF)
    cq = mm(second, w_query).astype(BF)
    caption = captions[0]
    pair = mm(caption, w_pair).astype(BF)
    ck, cv = pair[:, :hw], pair[:, hw:]
    visible = jnp.arange(caption.shape[0]) < caption_lengths[0]
    cm_own, cprobs = attend(cq, ck, cv, visible)
    cm_parts = head_rel(cm_own, swap_rows)
    cm = jnp.concatenate([pick(cm_parts, h ^ a) for a in range(4)], axis=1)
    after_cross = after_self + mm(cm, w_cross) + co_bias
    n3, r3 = stats(after_cross)
    third = (n3 * (1.0 + scale2) + shift2).astype(BF)
    up_values = mm(third, w_up) + up_bias.astype(F32)

    def gelu(t):
        return jax.nn.gelu(t, approximate=True)

    hidden, gelu_back = jax.vjp(gelu, up_values)
    hidden = hidden.astype(BF)
    g_feed = (gate2 * g).astype(BF)
    g_up = gelu_back(mm(g_feed, w_down))[0].astype(BF)
    g_third = mm(g_up, w_up, 1, 1)
    ga = normback(n3, r3, (1.0 + scale2) * g_third)
    ga = jnp.concatenate([ga[:rows] + cotangent.astype(F32), ga[rows:]], axis=0)
    ga_low = ga.astype(BF)
    g_cm = mm(ga_low, w_cross, 1, 1).astype(BF)
    g_cm_abs = [g_cm[:, a * hw : (a + 1) * hw] for a in range(4)]
    g_cm_own = head_sum([pick(g_cm_abs, h ^ j) for j in range(4)], swap_rows).astype(BF)
    feed_part = mm(hidden, w_down, 1, 1).astype(BF)
    feed = head_sum([feed_part[j * rows : (j + 1) * rows] for j in range(4)]) + dn_bias
    output_frames = (after_cross[:rows] + gate2 * feed).astype(BF)
    cot = cotangent.astype(F32)
    gv_gate2 = jnp.sum(cot * feed, axis=0)
    gv_down = jnp.sum(g_feed[:rows].astype(F32), axis=0)
    gv_upbias = jnp.sum(g_up.astype(F32), axis=0)
    gv_scale2 = jnp.sum(g_third * n3, axis=0)
    gv_shift2 = jnp.sum(g_third, axis=0)
    gv_cross = jnp.sum(ga, axis=0)
    g_updown = jnp.concatenate([mm(third, g_up, 0, 0).astype(BF), mm(g_feed, hidden, 0, 0).astype(BF)], axis=1)
    sum_updown = seq_sum(g_updown.reshape(n, kr, -1))
    g_cross_part = mm(cm, ga_low, 0, 0).astype(BF).reshape(n, 4, own, width)

    dq, dk, dv = attend_back(cq, ck, cv, cprobs, g_cm_own)
    g_second = mm(dq, w_query, 1, 1)
    gas = ga + normback(n2, r2, gain * g_second)
    g_proj = (gate1 * gas).astype(BF)
    g_sm = mm(g_proj, w_out, 1, 1).astype(BF)
    g_sm_abs = [g_sm[:, a * hw : (a + 1) * hw] for a in range(4)]
    g_sm_own = head_sum([pick(g_sm_abs, h ^ j) for j in range(4)], swap_rows).astype(BF)
    g_pair = jnp.concatenate([dk, dv], axis=1)
    g_cap = mm(g_pair, w_pair, 1, 1).astype(BF)
    g_cap_abs = [g_cap[:, a * hw : (a + 1) * hw] for a in range(4)]
    grad_captions = head_sum([pick(g_cap_abs, h ^ j) for j in range(4)])[None]
    gv_gain = jnp.sum(g_second * n2, axis=0)
    gv_gate1 = jnp.sum(gas * self_proj, axis=0)
    gv_self = jnp.sum(g_proj.astype(F32), axis=0)

    def by_head(part):
        return [lax.dynamic_index_in_dim(part, h ^ j, 1, keepdims=False) for j in range(4)]

    g_cross_out = head_sum(by_head(g_cross_part)).astype(BF).reshape(n, -1)
    g_qp = jnp.concatenate([mm(second, dq, 0, 0), mm(caption, g_pair, 0, 0)], axis=1).astype(BF)
    sum_two = seq_sum(jnp.concatenate([g_cross_out, g_qp.reshape(n, -1)], axis=1)[:, None])[0]
    g_out_part = mm(sm, g_proj, 0, 0).astype(BF).reshape(n, 4, own, width)
    g_self_out = head_sum(by_head(g_out_part)).astype(BF).reshape(n, -1)

    dq, dk, dv = attend_back(q, k, v, probs, g_sm_own)
    g_joint = jnp.concatenate([dq, dk, dv], axis=1)
    g_sw = mm(first, g_joint, 0, 0).astype(BF)
    sum_three = seq_sum(jnp.concatenate([g_self_out, g_sw.reshape(n, -1)], axis=1)[:, None])[0]
    g_first = mm(g_joint, w_self, 1, 1)
    gf = (gas + normback(n1, r1, (1.0 + scale1) * g_first)).astype(BF)
    grad_frames = head_sum([gf[j * rows : (j + 1) * rows] for j in range(4)])
    gv_scale1 = jnp.sum(g_first * n1, axis=0)
    gv_shift1 = jnp.sum(g_first, axis=0)

    vec = jnp.concatenate(
        [gv_shift1, gv_scale1, gv_gate1, gv_shift2, gv_scale2, gv_gate2, gv_self, gv_gain, gv_cross, gv_down]
    )[None]
    vec = vec + swap(vec, 1)
    vec = vec + swap(vec, 2)
    every = seq_gather(jnp.concatenate([vec, gv_upbias[None]], axis=1))[:, 0]
    g_mod = every[:, : 6 * width]
    cond_rows = lax.dynamic_slice_in_dim(cond_own, h * own, own, 1).astype(F32)
    grad_mod_weight = lax.dot_general(
        cond_rows, g_mod, (((0,), (0,)), ((), ())), precision=lax.Precision.HIGHEST, preferred_element_type=F32
    )
    sums = every.sum(0)
    place = s * 4 + h
    mb = 6 * width // (4 * n)
    grad_mod_bias = lax.dynamic_slice_in_dim(sums, place * mb, mb, 0)

    def own_vec(i):
        return lax.dynamic_slice_in_dim(sums, (6 + i) * width + place * own, own, 0)

    g_cond_part = lax.dot_general(
        g_mod,
        modulation_weight.astype(F32),
        (((1,), (1,)), ((), ())),
        precision=lax.Precision.HIGHEST,
        preferred_element_type=F32,
    )
    g_silu = lax.all_to_all(g_cond_part[:, None], "seq", split_axis=0, concat_axis=0, tiled=True).reshape(width)
    g_cond = jax.vjp(jax.nn.silu, condition[0].astype(F32))[1](g_silu)[0]
    grad_condition = lax.dynamic_slice_in_dim(g_cond, h * hw, hw, 0)[None]

    cut = own * width
    sum_cross = sum_two[:cut].reshape(own, width)
    sum_out = sum_three[:cut].reshape(own, width)
    cross_cols = jnp.concatenate([sum_two[cut:].reshape(kr, 3 * hw), sum_three[cut:].reshape(kr, 3 * hw)], axis=1)
    spread = lax.all_to_all(
        cross_cols.astype(BF).reshape(4, own, 6 * hw), "head", split_axis=0, concat_axis=0, tiled=True
    ).astype(F32)
    wide = spread.reshape(4, own, 6, hw).transpose(1, 2, 0, 3).reshape(own, 6 * width)
    grad_query, grad_pair, grad_self = wide[:, :width], wide[:, width : 3 * width], wide[:, 3 * width :]
    return (
        output_frames,
        grad_frames,
        grad_condition,
        grad_captions,
        grad_mod_weight,
        grad_mod_bias,
        grad_self,
        sum_out,
        own_vec(0),
        own_vec(1),
        grad_query,
        grad_pair,
        sum_cross,
        own_vec(2),
        sum_updown[:, : up_weight.shape[1]],
        sums[10 * width :],
        sum_updown[:, up_weight.shape[1] :].T,
        own_vec(3),
    )


def solution(mesh):
    both = ("seq", "head")
    return jax.shard_map(
        on_device,
        mesh=mesh,
        in_specs=(
            P(both, None),
            P("seq", None),
            P("seq", None, None),
            P("seq"),
            P("seq", None),
            P("seq"),
            P("seq", None),
            P("seq", None),
            P("seq"),
            P("seq"),
            P("seq", None),
            P("seq", None),
            P("seq", None),
            P("seq"),
            P("seq", "head"),
            P("head"),
            P("head", "seq"),
            P("seq"),
            P(both, None),
        ),
        out_specs=(
            P(both, None),
            P(both, None),
            P("seq", "head"),
            P("seq", None, "head"),
            P(both, None),
            P(both),
            P(both, None),
            P(both, None),
            P(both),
            P(both),
            P(both, None),
            P(both, None),
            P(both, None),
            P(both),
            P("seq", "head"),
            P("head"),
            P("head", "seq"),
            P(both),
        ),
        check_vma=False,
    )
```

```python
import jax
import jax.numpy as jnp
from jax import lax
from jax.experimental import pallas as pl
from jax.experimental.pallas import tpu as pltpu
from jax.sharding import PartitionSpec as P

HD = 64
BF = jnp.bfloat16
F32 = jnp.float32


def mm(a, b, ca=1, cb=0):
    return lax.dot_general(a, b, (((ca,), (cb,)), ((), ())), preferred_element_type=F32)


def swap(x, bit):
    return lax.ppermute(x, "head", [(i, i ^ bit) for i in range(4)])


def swap_rows(x, bit):
    blocks = jnp.split(swap(x, bit), 4, axis=0)
    return jnp.concatenate([blocks[i ^ bit] for i in range(4)], axis=0)


def head_rel(x, swap=swap):
    near = swap(x, 1)
    far = swap(x, 2)
    return [x, near, far, swap(far, 1)]


def pick(parts, index):
    low, high = (index & 1) == 1, (index & 2) == 2
    return jnp.where(
        high, jnp.where(low, parts[3], parts[2]), jnp.where(low, parts[1], parts[0])
    )


def head_sum(chunks, swap=swap):
    a, b = swap(chunks[1], 1), swap(chunks[3], 1)
    mine = chunks[0].astype(F32) + a.astype(F32)
    other = (chunks[2].astype(F32) + b.astype(F32)).astype(chunks[0].dtype)
    return mine + swap(other, 2).astype(F32)


def after(values, ready):
    return lax.optimization_barrier((values, ready))[0]


def seq_swap(x, bit):
    return lax.ppermute(x, "seq", [(i, i ^ bit) for i in range(lax.axis_size("seq"))])


def seq_bits():
    return [1 << b for b in range(lax.axis_size("seq").bit_length() - 1)]


def seq_gather(x):
    for bit in seq_bits():
        x = jnp.concatenate([x, seq_swap(x, bit)], axis=0)
    return x


def seq_scatter_sum(x):
    for bit in reversed(seq_bits()):
        x = x[:bit] + seq_swap(x[bit:], bit)
    return x


def seq_order(x, s):
    n = x.shape[0]
    at = (s ^ jnp.arange(n))[:, None] == jnp.arange(n)[None, :]
    precision = lax.Precision.HIGHEST if x.dtype == F32 else None
    return lax.dot_general(
        at.astype(x.dtype), x, (((1,), (0,)), ((), ())), precision=precision, preferred_element_type=F32
    )


def exchange(x):
    return lax.all_to_all(x, "seq", split_axis=0, concat_axis=0, tiled=True)


def stats(v):
    mean = jnp.mean(v, axis=-1, keepdims=True)
    center = v - mean
    r = lax.rsqrt(jnp.mean(center * center, axis=-1, keepdims=True) + 1e-6)
    return center * r, r


def normback(n, r, e):
    return r * (
        e - jnp.mean(e, axis=-1, keepdims=True) - n * jnp.mean(e * n, axis=-1, keepdims=True)
    )


def whole(x):
    zeros = (0,) * x.ndim
    return pl.BlockSpec(x.shape, lambda i: zeros)


def rows_of(block, width):
    return pl.BlockSpec((block, width), lambda i: (i, 0))


SCALAR = pl.BlockSpec(memory_space=pltpu.SMEM)


def call(kernel, blocks, ins, outs, scratch=()):
    return pl.pallas_call(
        kernel,
        grid=(blocks,),
        in_specs=[spec for _, spec in ins],
        out_specs=[spec for _, spec in outs],
        out_shape=[shape for shape, _ in outs],
        scratch_shapes=list(scratch),
        compiler_params=pltpu.CompilerParams(
            dimension_semantics=("arbitrary",), vmem_limit_bytes=52 * 1024 * 1024
        ),
    )(*[value for value, _ in ins])


def out(shape, dtype, spec=None):
    struct = jax.ShapeDtypeStruct(shape, dtype)
    return struct, whole(struct) if spec is None else spec


def unpack(ref, block, size):
    slab = ref[pl.ds(pl.multiple_of((block // 2) * size, size), size), :]
    half = slab.shape[1] // 2
    return jnp.where(block % 2 == 0, slab[:, :half], slab[:, half:])


def pack(ref, block, size, value):
    half = ref.shape[1] // 2
    place = pl.ds(pl.multiple_of((block // 2) * size, size), size)

    @pl.when(block % 2 == 0)
    def _():
        ref[place, :half] = value

    @pl.when(block % 2 == 1)
    def _():
        ref[place, half:] = value


def take(ref, parts, index):
    for j, part in enumerate(parts):

        @pl.when(index == j)
        def _():
            ref[...] = part[...]


def assemble(ref, parts, head):
    hw = parts[0].shape[-1]
    for a in range(4):
        ref[:, a * hw : (a + 1) * hw] = pick(parts, head ^ a)


def chunks_by_head(value, head):
    hw = value.shape[1] // 4
    blocks = [value[:, a * hw : (a + 1) * hw] for a in range(4)]
    return [pick(blocks, head ^ j) for j in range(4)]


def softmax_columns(keys, queries, values_t, p_ref, inv_ref, visible=None):
    lane = lax.broadcasted_iota(jnp.int32, (1, keys.shape[1]), 1) // HD
    outs = []
    for hd in range(keys.shape[1] // HD):
        st = mm(jnp.where(lane == hd, keys, 0), queries, 1, 1)
        if visible is not None:
            st = jnp.where(visible, st, -1e30)
        e = jnp.exp(st - jnp.max(st, axis=0, keepdims=True))
        inv = 1.0 / jnp.sum(e, axis=0, keepdims=True)
        low = e.astype(BF)
        p_ref[hd] = low
        inv_ref[hd : hd + 1, :] = inv
        outs.append(mm(values_t[hd * HD : (hd + 1) * HD, :], low) * inv)
    return jnp.concatenate(outs, axis=0).T.astype(BF)


def softmax_back(keys, keys_t, values, queries, p_ref, inv_ref, out_low, grad_out, dk_acc, dv_acc):
    width = keys.shape[1]
    lane = lax.broadcasted_iota(jnp.int32, (1, width), 1) // HD
    go_t, o_t = grad_out.T, out_low.astype(F32).T
    heads = width // HD
    scaled, inner = [], []
    for hd in range(heads):
        part = go_t[hd * HD : (hd + 1) * HD, :] * inv_ref[hd : hd + 1, :]
        scaled.append(part)
        inner.append(jnp.sum(part * o_t[hd * HD : (hd + 1) * HD, :], axis=0, keepdims=True))
    go = jnp.concatenate(scaled, axis=0).T.astype(BF)
    grads = []
    dk, dv = 0.0, 0.0
    for hd in range(heads):
        mine = lane == hd
        low = p_ref[hd]
        dp = mm(jnp.where(mine, values, 0), go, 1, 1)
        ds = (low.astype(F32) * (dp - inner[hd])).astype(BF)
        dv = dv + jnp.where(mine, mm(low, go), 0.0)
        dk = dk + jnp.where(mine, mm(ds, queries), 0.0)
        grads.append(mm(keys_t[hd * HD : (hd + 1) * HD, :], ds))
    dk_acc[...] += dk
    dv_acc[...] += dv
    return (jnp.concatenate(grads, axis=0).T * 0.125).astype(BF)


def self_forward(x0, x1, x2, x3, mod, w, first_ref, qkv_ref, sm_ref, p_ref, inv_ref, vt):
    i = pl.program_id(0)
    size, width = x0.shape
    hw = sm_ref.shape[1] // 2

    @pl.when(i == 0)
    def _():
        weights = w[:, : 3 * hw]
        for b, x in enumerate((x0, x1, x2, x3)):
            at = slice(b * size, (b + 1) * size)
            n, _ = stats(x[...].astype(F32))
            first = (n * (1.0 + mod[:, width : 2 * width]) + mod[:, :width]).astype(BF)
            first_ref[at, :] = first
            joint = mm(first, weights)
            qkv_ref[0, at, :] = (joint[:, :hw] * 0.125).astype(BF)
            qkv_ref[1, at, :] = joint[:, hw : 2 * hw].astype(BF)
            qkv_ref[2, at, :] = joint[:, 2 * hw :].astype(BF)
            vt[:, at] = joint[:, 2 * hw :].T.astype(BF)

    queries = qkv_ref[0, pl.ds(pl.multiple_of(i * size, size), size), :]
    pack(sm_ref, i, size, softmax_columns(qkv_ref[1], queries, vt, p_ref, inv_ref))


def cross_forward(
    head, length, x0, x1, x2, x3, sm0, sm1, sm2, sm3, mod, w0, w1, w2, w3, out_bias, gain, w_query, w_pair, caption,
    sm_abs, wout_ref, proj_ref, after_ref, second_ref, cq_ref, pair_ref, cm_ref, p_ref, inv_ref, vt, x,
):
    i, h = pl.program_id(0), head[0]
    size, width = x0.shape
    hw = cq_ref.shape[1]
    take(x, (x0, x1, x2, x3), i)

    @pl.when(i == 0)
    def _():
        assemble(wout_ref, [w[:, :hw] for w in (w0, w1, w2, w3)], h)
        pair = mm(caption[...], w_pair[:, : 2 * hw])
        pair_ref[0] = pair[:, :hw].astype(BF)
        pair_ref[1] = pair[:, hw:].astype(BF)
        vt[...] = pair[:, hw:].T.astype(BF)

    assemble(sm_abs, [unpack(p, i ^ j, size) for j, p in enumerate((sm0, sm1, sm2, sm3))], h)
    proj = mm(sm_abs[...], wout_ref[...]) + out_bias[...]
    proj_ref[...] = proj.astype(BF)
    after = x[...].astype(F32) + mod[:, 2 * width : 3 * width] * proj
    after_ref[...] = after
    n, _ = stats(after)
    second = (n * gain[...]).astype(BF)
    second_ref[...] = second
    queries = (mm(second, w_query[:, 3 * hw :]) * 0.125).astype(BF)
    cq_ref[...] = queries
    slots = lax.broadcasted_iota(jnp.int32, (caption.shape[0], 1), 0)
    pack(cm_ref, i, size, softmax_columns(pair_ref[0], queries, vt, p_ref, inv_ref, slots < length[0]))


def feed_both(
    head, after, cm0, cm1, cm2, cm3, mod, w0, w1, w2, w3, co_bias, w_up, w_down, up_bias, g0, g1, g2, g3,
    cm_abs, wc_ref, across_ref, third_ref, hidden_ref, gup_ref, gfeed_ref, ga_ref, c0, c1, c2, c3, vec_ref, g,
):
    i, h = pl.program_id(0), head[0]
    size, width = after.shape
    hw = width // 4
    take(g, (g0, g1, g2, g3), i)

    @pl.when(i == 0)
    def _():
        assemble(wc_ref, [w[:, hw:] for w in (w0, w1, w2, w3)], h)
        vec_ref[...] = jnp.zeros_like(vec_ref)

    assemble(cm_abs, [unpack(p, i ^ j, size) for j, p in enumerate((cm0, cm1, cm2, cm3))], h)
    across = after[...] + mm(cm_abs[...], wc_ref[...]) + co_bias[...]
    n, r = stats(across)
    scale = 1.0 + mod[:, 4 * width : 5 * width]
    third = (n * scale + mod[:, 3 * width : 4 * width]).astype(BF)
    third_ref[...] = third
    v = mm(third, w_up[...]) + up_bias[...].astype(F32)
    t = jnp.tanh(0.7978845608028654 * (v + 0.044715 * v * v * v))
    hidden_ref[...] = (0.5 * v * (1.0 + t)).astype(BF)
    slope = 0.5 * (1.0 + t) + 0.5 * v * (1.0 - t * t) * (0.7978845608028654 * (1.0 + 0.134145 * v * v))
    grad = g[...].astype(F32)
    gfeed = (mod[:, 5 * width :] * grad).astype(BF)
    gfeed_ref[...] = gfeed
    gup = (mm(gfeed, w_down[...]) * slope).astype(BF)
    gup_ref[...] = gup
    gthird = mm(gup, w_up[...], 1, 1)
    ga = normback(n, r, scale * gthird) + jnp.where(i == 0, grad, 0.0)
    low = ga.astype(BF)
    ga_ref[...] = low
    for j, (ref, chunk) in enumerate(zip((c0, c1, c2, c3), chunks_by_head(mm(low, wc_ref[...], 1, 1).astype(BF), h))):
        pack(ref, i ^ j, size, chunk)

    @pl.when(i == 0)
    def _():
        across_ref[...] = across
        vec_ref[4:5, :] = jnp.sum(gfeed.astype(F32), axis=0, keepdims=True)

    vec_ref[0:1, :] += jnp.sum(gthird, axis=0, keepdims=True)
    vec_ref[1:2, :] += jnp.sum(gthird * n, axis=0, keepdims=True)
    vec_ref[2:3, :] += jnp.sum(ga, axis=0, keepdims=True)
    vec_ref[3:4, :] += jnp.sum(gup.astype(F32), axis=0, keepdims=True)


def cross_back(
    head, a0, a1, a2, cq, p, inv, pair, cm, w_query, ga, after, proj, mod, gain, wout,
    dq_ref, dpair_ref, gas_ref, gproj_ref, c0, c1, c2, c3, vec_ref, kt, dk, dv,
):
    i, h = pl.program_id(0), head[0]
    size, width = after.shape

    @pl.when(i == 0)
    def _():
        vec_ref[...] = jnp.zeros_like(vec_ref)
        dk[...] = jnp.zeros_like(dk)
        dv[...] = jnp.zeros_like(dv)
        kt[...] = pair[0].astype(F32).T.astype(BF)

    grad = sum(unpack(a, i, size).astype(F32) for a in (a0, a1, a2))
    dq = softmax_back(pair[0], kt, pair[1], cq[...], p, inv, unpack(cm, i, size), grad, dk, dv)
    dq_ref[...] = dq
    gsecond = mm(dq, w_query[:, 3 * dq.shape[1] :], 1, 1)
    n, r = stats(after[...])
    gas = ga[...].astype(F32) + normback(n, r, gain[...] * gsecond)
    gas_ref[...] = gas.astype(BF)
    gproj = (mod[:, 2 * width : 3 * width] * gas).astype(BF)
    gproj_ref[...] = gproj
    for j, (ref, chunk) in enumerate(zip((c0, c1, c2, c3), chunks_by_head(mm(gproj, wout[...], 1, 1).astype(BF), h))):
        pack(ref, i ^ j, size, chunk)
    vec_ref[0:1, :] += jnp.sum(gas * proj[...].astype(F32), axis=0, keepdims=True)
    vec_ref[1:2, :] += jnp.sum(gsecond * n, axis=0, keepdims=True)
    vec_ref[2:3, :] += jnp.sum(gproj.astype(F32), axis=0, keepdims=True)

    @pl.when(i == pl.num_programs(0) - 1)
    def _():
        dpair_ref[0] = dk[...].astype(BF)
        dpair_ref[1] = dv[...].astype(BF)


def self_back(a0, a1, a2, qkv, p, inv, sm, grads_ref, kt, dk, dv):
    i = pl.program_id(0)
    size = p.shape[2]
    hw = qkv.shape[2]

    @pl.when(i == 0)
    def _():
        dk[...] = jnp.zeros_like(dk)
        dv[...] = jnp.zeros_like(dv)
        kt[...] = qkv[1].astype(F32).T.astype(BF)

    at = pl.ds(pl.multiple_of(i * size, size), size)
    grad = sum(unpack(a, i, size).astype(F32) for a in (a0, a1, a2))
    grads_ref[at, :hw] = softmax_back(
        qkv[1], kt, qkv[2], qkv[0, at, :], p, inv, unpack(sm, i, size), grad, dk, dv
    )

    @pl.when(i == pl.num_programs(0) - 1)
    def _():
        grads_ref[:, hw : 2 * hw] = dk[...].astype(BF)
        grads_ref[:, 2 * hw :] = dv[...].astype(BF)


def first_back(x0, x1, x2, x3, grads, w, mod, gas, gf_ref, vec_ref, x):
    i = pl.program_id(0)
    width = x0.shape[1]
    take(x, (x0, x1, x2, x3), i)

    @pl.when(i == 0)
    def _():
        vec_ref[...] = jnp.zeros_like(vec_ref)

    gfirst = mm(grads[...], w[:, : grads.shape[1]], 1, 1)
    n, r = stats(x[...].astype(F32))
    scale = 1.0 + mod[:, width : 2 * width]
    gf_ref[...] = (gas[...].astype(F32) + normback(n, r, scale * gfirst)).astype(BF)
    vec_ref[0:1, :] += jnp.sum(gfirst, axis=0, keepdims=True)
    vec_ref[1:2, :] += jnp.sum(gfirst * n, axis=0, keepdims=True)


def own_columns(head, w_self, w_out, w_query, w_pair, w_cross, own_ref):
    h = head[0]
    width = w_out.shape[1]
    hw = width // 4
    places = [(w_self, t * width) for t in range(3)] + [(w_query, 0), (w_pair, 0), (w_pair, width), (w_out, 0), (w_cross, 0)]
    for t, (ref, base) in enumerate(places):
        parts = [ref[:, base + a * hw : base + (a + 1) * hw] for a in range(4)]
        own_ref[:, t * hw : (t + 1) * hw] = pick(parts, h)


def feed_weights(head, third, gup, gfeed, hidden, cm, ga, w_down, both_ref, c0, c1, c2, c3):
    i = pl.program_id(0)
    width = ga.shape[1]
    hw = width // 4
    rows = hidden.shape[0] // 4
    both_ref[:, : gup.shape[1]] = mm(third[...], gup[...], 0, 0).astype(BF)
    both_ref[:, gup.shape[1] :] = mm(gfeed[...], hidden[...], 0, 0).astype(BF)
    chunks = chunks_by_head(mm(cm[...], ga[...], 0, 0).astype(BF), head[0])
    for j, ref in enumerate((c0, c1, c2, c3)):
        for k in range(3):

            @pl.when(i == k)
            def _():
                ref[:, width + k * hw : width + (k + 1) * hw] = chunks[j]

        @pl.when(i == 0)
        def _():
            ref[:, width + 3 * hw :] = jnp.zeros((rows, ref.shape[1] - width - 3 * hw), BF)
            ref[:, :width] = mm(hidden[j * rows : (j + 1) * rows, :], w_down[...], 1, 1).astype(BF)


def mid_weights(head, sm, gproj, second, dq, caption, dpair, w_pair, gcross, mid_ref, c0, c1, c2, c3):
    i = pl.program_id(0)
    hw = dq.shape[1]
    out_chunks = chunks_by_head(mm(sm[...], gproj[...], 0, 0).astype(BF), head[0])
    mid_ref[:, hw : 2 * hw] = mm(second[...], dq[...], 0, 0).astype(BF)
    for t in range(2):
        mid_ref[:, (2 + t) * hw : (3 + t) * hw] = mm(caption[...], dpair[t], 0, 0).astype(BF)
    for k in range(3):

        @pl.when(i == k)
        def _():
            mid_ref[:, :hw] = gcross[:, k * hw : (k + 1) * hw]
            for j, ref in enumerate((c0, c1, c2, c3)):
                ref[:, k * hw : (k + 1) * hw] = out_chunks[j]

    @pl.when(i == 0)
    def _():
        cap = mm(dpair[0], w_pair[:, :hw], 1, 1) + mm(dpair[1], w_pair[:, hw : 2 * hw], 1, 1)
        for ref, chunk in zip((c0, c1, c2, c3), chunks_by_head(cap.astype(BF), head[0])):
            ref[:, 3 * hw :] = chunk


def last_weights(first, gjoint, gout, last_ref):
    i = pl.program_id(0)
    hw = gjoint.shape[1] // 3
    last_ref[:, hw:] = mm(first[...], gjoint[...], 0, 0).astype(BF)
    for k in range(3):

        @pl.when(i == k)
        def _():
            last_ref[:, :hw] = gout[:, k * hw : (k + 1) * hw]


def spread_columns(got, cross_ref, query_ref, pair_ref, out_ref, self_ref):
    hw = got.shape[2] // 8
    for t, (ref, base) in enumerate(
        ((cross_ref, 0), (query_ref, 0), (pair_ref, 0), (pair_ref, 4), (out_ref, 0), (self_ref, 0), (self_ref, 4), (self_ref, 8))
    ):
        for a in range(4):
            ref[:, (base + a) * hw : (base + a + 1) * hw] = got[a, :, t * hw : (t + 1) * hw].astype(F32)


def on_device(
    frames,
    condition,
    captions,
    caption_lengths,
    modulation_weight,
    modulation_bias,
    self_weight,
    self_out,
    self_bias,
    cross_gain,
    cross_query,
    cross_pair,
    cross_out,
    cross_bias,
    up_weight,
    up_bias,
    down_weight,
    down_bias,
    cotangent,
):
    n = lax.axis_size("seq")
    h = lax.axis_index("head")
    s = lax.axis_index("seq")
    rows, width = frames.shape
    hw = width // 4
    kr = self_weight.shape[0]
    own = kr // 4
    total = rows * 4

    ff = up_weight.shape[1]
    head = h.astype(jnp.int32)[None]

    def full(v):
        return v, whole(v)

    (w_own,) = call(
        own_columns,
        1,
        [(head, SCALAR)] + [full(v) for v in (self_weight, self_out, cross_query, cross_pair, cross_out)],
        [out((kr, 8 * hw), BF)],
    )
    w_own = lax.all_gather(w_own, "seq", axis=0, tiled=True)
    small = jnp.concatenate([self_bias, cross_bias, cross_gain, down_bias])[None]
    got = exchange(jnp.concatenate([condition.reshape(n, kr), jnp.broadcast_to(small, (n, 4 * kr))], axis=1))
    cond_own = jax.nn.silu(got[:, :kr].astype(F32)).astype(BF)
    vectors = got[:, kr:].astype(F32).reshape(n, 4, kr).transpose(1, 0, 2).reshape(4, width)
    out_bias, co_bias, gain, dn_bias = vectors[0], vectors[1], vectors[2], vectors[3]
    mod_part = mm(cond_own, modulation_weight) + lax.dynamic_update_slice(
        jnp.zeros((n * modulation_bias.shape[0],), F32),
        modulation_bias.astype(F32),
        (s * modulation_bias.shape[0],),
    )
    mod = exchange(mod_part).sum(0, keepdims=True)
    updown = jnp.concatenate([up_weight, down_weight.T], axis=1)
    updown = jnp.broadcast_to(updown[None], (n, *updown.shape))
    updown = exchange(after(updown, (mod, w_own))).reshape(width, 2 * ff)
    x = head_rel(frames)
    w_parts = head_rel(w_own[:, 6 * hw :])
    g = head_rel(after(cotangent, x[3]))
    two = pl.BlockSpec((width, width), lambda i: (0, 1))
    one = pl.BlockSpec((width, width), lambda i: (0, 0))
    caption = captions[0]
    slots = caption.shape[0]
    heads = hw // HD
    grid, block = 4, rows
    packed = (total // 2, 2 * hw)

    p_spec = pl.BlockSpec((heads, total, block), lambda i: (0, 0, i))
    cp_spec = pl.BlockSpec((heads, slots, block), lambda i: (0, 0, i))
    inv_spec = pl.BlockSpec((heads, block), lambda i: (0, i))
    wide = rows_of(block, width)
    thin = rows_of(block, hw)

    first, qkv, sm_own, probs, inv = call(
        self_forward,
        grid,
        [full(v) for v in (*x, mod)] + [(w_own, one)],
        [
            out((total, width), BF),
            out((3, total, hw), BF),
            out(packed, BF),
            out((heads, total, total), BF, p_spec),
            out((heads, total), F32, inv_spec),
        ],
        [pltpu.VMEM((hw, total), BF)],
    )
    sm_parts = head_rel(sm_own)
    sm, w_out, proj, after_self, second, cq, pair, cm_own, cprobs, cinv = call(
        cross_forward,
        grid,
        [(head, SCALAR), (caption_lengths, SCALAR)]
        + [full(v) for v in (*x, *sm_parts, mod, *w_parts, out_bias[None], gain[None])]
        + [(w_own, one), (w_own, two), full(caption)],
        [
            out((total, width), BF, wide),
            out((width, width), BF),
            out((total, width), BF, wide),
            out((total, width), F32, wide),
            out((total, width), BF, wide),
            out((total, hw), BF, thin),
            out((2, slots, hw), BF),
            out(packed, BF),
            out((heads, slots, total), BF, cp_spec),
            out((heads, total), F32, inv_spec),
        ],
        [pltpu.VMEM((hw, slots), BF), pltpu.VMEM((rows, width), BF)],
    )
    cm_parts = head_rel(cm_own)
    cm, w_cross, across, third, hidden, g_up, g_feed, ga, *chunks, vec_c = call(
        feed_both,
        grid,
        [(head, SCALAR), (after_self, wide)]
        + [full(v) for v in (*cm_parts, mod, *w_parts, co_bias[None])]
        + [(updown, one), (updown, two)]
        + [full(v) for v in (up_bias[None], *g)],
        [
            out((total, width), BF, wide),
            out((width, width), BF),
            out((rows, width), F32),
            out((total, width), BF, wide),
            out((total, ff), BF, rows_of(block, ff)),
            out((total, ff), BF, rows_of(block, ff)),
            out((total, width), BF, wide),
            out((total, width), BF, wide),
            *[out(packed, BF) for _ in range(4)],
            out((8, width), F32),
        ],
        [pltpu.VMEM((rows, width), BF)],
    )

    def near_terms(chunks):
        a, b = swap(chunks[1], 1), swap(chunks[3], 1)
        return chunks[0], a, (chunks[2].astype(F32) + b.astype(F32)).astype(BF)

    mine, near, other = near_terms(chunks)
    far = swap(other, 2)
    third_rows = width // 3
    pad = -3 * hw % 128
    col = pl.BlockSpec((total, third_rows), lambda i: (0, i))
    both, *feed_chunks = call(
        feed_weights,
        3,
        [(head, SCALAR), (after(third, other), col), full(g_up), (g_feed, col), full(hidden), (cm, col), full(ga), (updown, two)],
        [out((width, 2 * ff), BF, rows_of(third_rows, 2 * ff))] + [out((rows, width + 3 * hw + pad), BF) for _ in range(4)],
    )
    both = exchange(both.reshape(n, kr, 2 * ff))
    feed_mine, feed_near, feed_other = near_terms(after(tuple(feed_chunks), far))
    far, feed_other = lax.optimization_barrier((far, feed_other))
    dq, dpair, gas, g_proj, *chunks, vec_d = call(
        cross_back,
        grid,
        [(head, SCALAR)]
        + [full(v) for v in (mine, near, far)]
        + [(cq, thin), (cprobs, cp_spec), (cinv, inv_spec), full(pair), full(cm_own), (w_own, one)]
        + [(ga, wide), (after_self, wide), (proj, wide), full(mod), full(gain[None]), full(w_out)],
        [
            out((total, hw), BF, thin),
            out((2, slots, hw), BF),
            out((total, width), BF, wide),
            out((total, width), BF, wide),
            *[out(packed, BF) for _ in range(4)],
            out((8, width), F32),
        ],
        [pltpu.VMEM((hw, slots), BF), pltpu.VMEM((slots, hw), F32), pltpu.VMEM((slots, hw), F32)],
    )
    feed_sum = feed_mine.astype(F32) + feed_near.astype(F32) + swap(feed_other, 2).astype(F32)
    feed, g_cross = feed_sum[:, :width] + dn_bias, feed_sum[:, width : width + 3 * hw].astype(BF)
    output_frames = (across + mod[:, 5 * width :] * feed).astype(BF)
    gv_gate2 = jnp.sum(cotangent.astype(F32) * feed, axis=0, keepdims=True)
    mine, near, other = near_terms(chunks)
    far = swap(other, 2)
    mid, *out_chunks = call(
        mid_weights,
        3,
        [(head, SCALAR), (after(sm, other), col), full(g_proj), (second, col), full(dq)]
        + [(caption, pl.BlockSpec((slots, third_rows), lambda i: (0, i))), full(dpair), (w_own, two)]
        + [(g_cross, pl.BlockSpec((rows, 3 * hw), lambda i: (0, 0)))],
        [out((width, 4 * hw), BF, rows_of(third_rows, 4 * hw))] + [out((rows, 4 * hw), BF) for _ in range(4)],
    )
    out_mine, out_near, out_other = near_terms(after(tuple(out_chunks), far))
    far, mid, both, out_other = lax.optimization_barrier((far, mid, both, out_other))
    mid = exchange(mid.reshape(n, kr, 4 * hw))
    (g_joint,) = call(
        self_back,
        grid,
        [full(v) for v in (mine, near, far, qkv)]
        + [(probs, p_spec), (inv, inv_spec), full(sm_own)],
        [out((total, 3 * hw), BF)],
        [pltpu.VMEM((hw, total), BF), pltpu.VMEM((total, hw), F32), pltpu.VMEM((total, hw), F32)],
    )
    out_sum = out_mine.astype(F32) + out_near.astype(F32) + swap(out_other, 2).astype(F32)
    grad_captions = out_sum[None, :, 3 * hw :]
    (last,) = call(
        last_weights,
        3,
        [(first, col), full(g_joint), full(out_sum[:, : 3 * hw].astype(BF))],
        [out((width, 4 * hw), BF, rows_of(third_rows, 4 * hw))],
    )
    gas, last = lax.optimization_barrier((gas, last))
    last = exchange(after(last, mid).reshape(n, kr, 4 * hw))
    gf, vec_e = call(
        first_back,
        grid,
        [full(v) for v in x] + [(g_joint, rows_of(block, 3 * hw)), (w_own, one), full(mod), (gas, wide)],
        [out((total, width), BF, wide), out((8, width), F32)],
        [pltpu.VMEM((rows, width), BF)],
    )
    grad_frames = head_sum([gf[j * rows : (j + 1) * rows] for j in range(4)])

    def over_heads(v):
        v = v + swap(v, 1)
        return v + swap(v, 2)

    vec = [vec_e[:2], vec_d[:1], vec_c[:2], gv_gate2, vec_d[2:3], vec_d[1:2], vec_c[2:3], vec_c[4:5]]
    vec = seq_gather(jnp.concatenate([over_heads(jnp.concatenate(vec, axis=0)), vec_c[3:4]], axis=0)[None])
    g_mod = vec[:, :6].reshape(n, 6 * width)
    g_cond = lax.dot_general(
        g_mod,
        modulation_weight.astype(F32),
        (((1,), (1,)), ((), ())),
        precision=lax.Precision.HIGHEST,
        preferred_element_type=F32,
    )
    g_silu = exchange(seq_order(g_cond, s)).reshape(width)
    g_cond = jax.vjp(jax.nn.silu, condition[0].astype(F32))[1](g_silu)[0]
    grad_condition = lax.dynamic_slice_in_dim(g_cond, h * hw, hw, 0)[None]
    cond_rows = seq_order(lax.dynamic_slice_in_dim(cond_own, h * own, own, 1), s)
    grad_mod_weight = lax.dot_general(
        cond_rows, g_mod, (((0,), (0,)), ((), ())), precision=lax.Precision.HIGHEST, preferred_element_type=F32
    )
    sums = vec.sum(0)
    place = s * 4 + h
    mb = 6 * width // (4 * n)
    grad_mod_bias = lax.dynamic_slice_in_dim(sums[:6].reshape(6 * width), place * mb, mb, 0)

    def own_vec(i):
        return lax.dynamic_slice_in_dim(sums[6 + i], place * own, own, 0)

    both = both.astype(F32).sum(0)
    cols = jnp.concatenate([mid.astype(F32).sum(0).astype(BF), last.astype(F32).sum(0).astype(BF)], axis=1)
    cols = lax.all_to_all(cols.reshape(4, own, 8 * hw), "head", split_axis=0, concat_axis=0, tiled=True)
    grad_cross, grad_query, grad_pair, grad_out, grad_self = call(
        spread_columns,
        1,
        [full(cols)],
        [out((own, k * width), F32) for k in (1, 1, 2, 1, 3)],
    )
    return (
        output_frames,
        grad_frames,
        grad_condition,
        grad_captions,
        grad_mod_weight,
        grad_mod_bias,
        grad_self,
        grad_out,
        own_vec(0),
        own_vec(1),
        grad_query,
        grad_pair,
        grad_cross,
        own_vec(2),
        both[:, :ff],
        sums[10],
        both[:, ff:].T,
        own_vec(3),
    )


def solution(mesh):
    both = ("seq", "head")
    return jax.shard_map(
        on_device,
        mesh=mesh,
        in_specs=(
            P(both, None),
            P("seq", None),
            P("seq", None, None),
            P("seq"),
            P("seq", None),
            P("seq"),
            P("seq", None),
            P("seq", None),
            P("seq"),
            P("seq"),
            P("seq", None),
            P("seq", None),
            P("seq", None),
            P("seq"),
            P("seq", "head"),
            P("head"),
            P("head", "seq"),
            P("seq"),
            P(both, None),
        ),
        out_specs=(
            P(both, None),
            P(both, None),
            P("seq", "head"),
            P("seq", None, "head"),
            P(both, None),
            P(both),
            P(both, None),
            P(both, None),
            P(both),
            P(both),
            P(both, None),
            P(both, None),
            P(both, None),
            P(both),
            P("seq", "head"),
            P("head"),
            P("head", "seq"),
            P(both),
        ),
        check_vma=False,
    )
```

```python
from functools import partial

import jax
import jax.numpy as jnp
from jax import lax
from jax.experimental import pallas as pl
from jax.experimental.pallas import tpu as pltpu
from jax.sharding import PartitionSpec as P

HD = 64
BF = jnp.bfloat16
F32 = jnp.float32


def mm(a, b, ca=1, cb=0):
    return lax.dot_general(a, b, (((ca,), (cb,)), ((), ())), preferred_element_type=F32)


def swap(x, bit):
    return lax.ppermute(x, "head", [(i, i ^ bit) for i in range(4)])


def swap_rows(x, bit):
    blocks = jnp.split(swap(x, bit), 4, axis=0)
    return jnp.concatenate([blocks[i ^ bit] for i in range(4)], axis=0)


def head_rel(x, swap=swap):
    near = swap(x, 1)
    far = swap(x, 2)
    return [x, near, far, swap(far, 1)]


def pick(parts, index):
    low, high = (index & 1) == 1, (index & 2) == 2
    return jnp.where(
        high, jnp.where(low, parts[3], parts[2]), jnp.where(low, parts[1], parts[0])
    )


def head_sum(chunks, swap=swap):
    a, b = swap(chunks[1], 1), swap(chunks[3], 1)
    mine = chunks[0].astype(F32) + a.astype(F32)
    other = (chunks[2].astype(F32) + b.astype(F32)).astype(chunks[0].dtype)
    return mine + swap(other, 2).astype(F32)


def after(values, ready):
    return lax.optimization_barrier((values, ready))[0]


def seq_swap(x, bit):
    return lax.ppermute(x, "seq", [(i, i ^ bit) for i in range(lax.axis_size("seq"))])


def seq_bits():
    return [1 << b for b in range(lax.axis_size("seq").bit_length() - 1)]


def seq_gather(x):
    for bit in seq_bits():
        x = jnp.concatenate([x, seq_swap(x, bit)], axis=0)
    return x


def seq_scatter_sum(x):
    for bit in reversed(seq_bits()):
        x = x[:bit] + seq_swap(x[bit:], bit)
    return x


def seq_order(x, s):
    n = x.shape[0]
    at = (s ^ jnp.arange(n))[:, None] == jnp.arange(n)[None, :]
    precision = lax.Precision.HIGHEST if x.dtype == F32 else None
    return lax.dot_general(
        at.astype(x.dtype), x, (((1,), (0,)), ((), ())), precision=precision, preferred_element_type=F32
    )


def exchange(x):
    return lax.all_to_all(x, "seq", split_axis=0, concat_axis=0, tiled=True)


def alike():
    n = lax.axis_size("seq")
    return [list(range(odd, n, 2)) for odd in (0, 1)]


def half_reduce(near, far):
    return (near.astype(F32) + seq_swap(far, 1).astype(F32)).astype(BF)


def rest_reduce(part):
    return lax.all_to_all(part, "seq", split_axis=0, concat_axis=0, axis_index_groups=alike(), tiled=True)


def stats(v):
    mean = jnp.mean(v, axis=-1, keepdims=True)
    center = v - mean
    r = lax.rsqrt(jnp.mean(center * center, axis=-1, keepdims=True) + 1e-6)
    return center * r, r


def normback(n, r, e):
    return r * (
        e - jnp.mean(e, axis=-1, keepdims=True) - n * jnp.mean(e * n, axis=-1, keepdims=True)
    )


def whole(x):
    zeros = (0,) * x.ndim
    return pl.BlockSpec(x.shape, lambda i: zeros)


def rows_of(block, width):
    return pl.BlockSpec((block, width), lambda i: (i, 0))


SCALAR = pl.BlockSpec(memory_space=pltpu.SMEM)


def call(kernel, blocks, ins, outs, scratch=()):
    return pl.pallas_call(
        kernel,
        grid=(blocks,),
        in_specs=[spec for _, spec in ins],
        out_specs=[spec for _, spec in outs],
        out_shape=[shape for shape, _ in outs],
        scratch_shapes=list(scratch),
        compiler_params=pltpu.CompilerParams(
            dimension_semantics=("arbitrary",), vmem_limit_bytes=52 * 1024 * 1024
        ),
    )(*[value for value, _ in ins])


def out(shape, dtype, spec=None):
    struct = jax.ShapeDtypeStruct(shape, dtype)
    return struct, whole(struct) if spec is None else spec


def unpack(ref, block, size):
    slab = ref[pl.ds(pl.multiple_of((block // 2) * size, size), size), :]
    half = slab.shape[1] // 2
    return jnp.where(block % 2 == 0, slab[:, :half], slab[:, half:])


def pack(ref, block, size, value):
    half = ref.shape[1] // 2
    place = pl.ds(pl.multiple_of((block // 2) * size, size), size)

    @pl.when(block % 2 == 0)
    def _():
        ref[place, :half] = value

    @pl.when(block % 2 == 1)
    def _():
        ref[place, half:] = value


def take(ref, parts, index):
    for j, part in enumerate(parts):

        @pl.when(index == j)
        def _():
            ref[...] = part[...]


def assemble(ref, parts, head):
    hw = parts[0].shape[-1]
    for a in range(4):
        ref[:, a * hw : (a + 1) * hw] = pick(parts, head ^ a)


def chunks_by_head(value, head):
    hw = value.shape[1] // 4
    blocks = [value[:, a * hw : (a + 1) * hw] for a in range(4)]
    return [pick(blocks, head ^ j) for j in range(4)]


def softmax_columns(keys, queries, values_t, p_ref, inv_ref, visible=None):
    lane = lax.broadcasted_iota(jnp.int32, (1, keys.shape[1]), 1) // HD
    outs = []
    for hd in range(keys.shape[1] // HD):
        st = mm(jnp.where(lane == hd, keys, 0), queries, 1, 1)
        if visible is not None:
            st = jnp.where(visible, st, -1e30)
        e = jnp.exp(st - jnp.max(st, axis=0, keepdims=True))
        inv = 1.0 / jnp.sum(e, axis=0, keepdims=True)
        low = e.astype(BF)
        p_ref[hd] = low
        inv_ref[hd : hd + 1, :] = inv
        outs.append(mm(values_t[hd * HD : (hd + 1) * HD, :], low) * inv)
    return jnp.concatenate(outs, axis=0).T.astype(BF)


def softmax_back(keys, keys_t, values, queries, p_ref, inv_ref, out_low, grad_out, dk_acc, dv_acc):
    width = keys.shape[1]
    lane = lax.broadcasted_iota(jnp.int32, (1, width), 1) // HD
    go_t, o_t = grad_out.T, out_low.astype(F32).T
    heads = width // HD
    scaled, inner = [], []
    for hd in range(heads):
        part = go_t[hd * HD : (hd + 1) * HD, :] * inv_ref[hd : hd + 1, :]
        scaled.append(part)
        inner.append(jnp.sum(part * o_t[hd * HD : (hd + 1) * HD, :], axis=0, keepdims=True))
    go = jnp.concatenate(scaled, axis=0).T.astype(BF)
    grads = []
    dk, dv = 0.0, 0.0
    for hd in range(heads):
        mine = lane == hd
        low = p_ref[hd]
        dp = mm(jnp.where(mine, values, 0), go, 1, 1)
        ds = (low.astype(F32) * (dp - inner[hd])).astype(BF)
        dv = dv + jnp.where(mine, mm(low, go), 0.0)
        dk = dk + jnp.where(mine, mm(ds, queries), 0.0)
        grads.append(mm(keys_t[hd * HD : (hd + 1) * HD, :], ds))
    dk_acc[...] += dk
    dv_acc[...] += dv
    return (jnp.concatenate(grads, axis=0).T * 0.125).astype(BF)


def self_forward(x0, x1, x2, x3, mod, w, first_ref, qkv_ref, sm_ref, p_ref, inv_ref, vt):
    i = pl.program_id(0)
    size, width = x0.shape
    hw = sm_ref.shape[1] // 2

    @pl.when(i == 0)
    def _():
        weights = w[:, : 3 * hw]
        for b, x in enumerate((x0, x1, x2, x3)):
            at = slice(b * size, (b + 1) * size)
            n, _ = stats(x[...].astype(F32))
            first = (n * (1.0 + mod[:, width : 2 * width]) + mod[:, :width]).astype(BF)
            first_ref[at, :] = first
            joint = mm(first, weights)
            qkv_ref[0, at, :] = (joint[:, :hw] * 0.125).astype(BF)
            qkv_ref[1, at, :] = joint[:, hw : 2 * hw].astype(BF)
            qkv_ref[2, at, :] = joint[:, 2 * hw :].astype(BF)
            vt[:, at] = joint[:, 2 * hw :].T.astype(BF)

    queries = qkv_ref[0, pl.ds(pl.multiple_of(i * size, size), size), :]
    pack(sm_ref, i, size, softmax_columns(qkv_ref[1], queries, vt, p_ref, inv_ref))


def cross_forward(
    head, length, x0, x1, x2, x3, sm0, sm1, sm2, sm3, mod, w0, w1, w2, w3, out_bias, gain, w_query, w_rest, caption,
    sm_abs, wout_ref, proj_ref, after_ref, second_ref, cq_ref, pair_ref, cm_ref, p_ref, inv_ref, vt, x,
):
    i, h = pl.program_id(0), head[0]
    size, width = x0.shape
    hw = cq_ref.shape[1]
    take(x, (x0, x1, x2, x3), i)

    @pl.when(i == 0)
    def _():
        assemble(wout_ref, [w[:, :hw] for w in (w0, w1, w2, w3)], h)
        pair = mm(caption[...], w_rest[:, 2 * hw :])
        pair_ref[0] = pair[:, :hw].astype(BF)
        pair_ref[1] = pair[:, hw:].astype(BF)
        vt[...] = pair[:, hw:].T.astype(BF)

    assemble(sm_abs, [unpack(p, i ^ j, size) for j, p in enumerate((sm0, sm1, sm2, sm3))], h)
    proj = mm(sm_abs[...], wout_ref[...]) + out_bias[...]
    proj_ref[...] = proj.astype(BF)
    after = x[...].astype(F32) + mod[:, 2 * width : 3 * width] * proj
    after_ref[...] = after
    n, _ = stats(after)
    second = (n * gain[...]).astype(BF)
    second_ref[...] = second
    queries = (mm(second, w_query[:, 3 * hw :]) * 0.125).astype(BF)
    cq_ref[...] = queries
    slots = lax.broadcasted_iota(jnp.int32, (caption.shape[0], 1), 0)
    pack(cm_ref, i, size, softmax_columns(pair_ref[0], queries, vt, p_ref, inv_ref, slots < length[0]))


def feed_both(
    head, after, cm0, cm1, cm2, cm3, mod, w0, w1, w2, w3, co_bias, w_up, w_down, up_bias, g0, g1, g2, g3,
    cm_abs, wc_ref, across_ref, third_ref, hidden_ref, gup_ref, gfeed_ref, ga_ref, c0, c1, c2, c3, vec_ref, g,
):
    i, h = pl.program_id(0), head[0]
    size, width = after.shape
    hw = width // 4
    take(g, (g0, g1, g2, g3), i)

    @pl.when(i == 0)
    def _():
        assemble(wc_ref, [w[:, hw:] for w in (w0, w1, w2, w3)], h)
        vec_ref[...] = jnp.zeros_like(vec_ref)

    assemble(cm_abs, [unpack(p, i ^ j, size) for j, p in enumerate((cm0, cm1, cm2, cm3))], h)
    across = after[...] + mm(cm_abs[...], wc_ref[...]) + co_bias[...]
    n, r = stats(across)
    scale = 1.0 + mod[:, 4 * width : 5 * width]
    third = (n * scale + mod[:, 3 * width : 4 * width]).astype(BF)
    third_ref[...] = third
    v = mm(third, w_up[...]) + up_bias[...].astype(F32)
    t = jnp.tanh(0.7978845608028654 * (v + 0.044715 * v * v * v))
    hidden_ref[...] = (0.5 * v * (1.0 + t)).astype(BF)
    slope = 0.5 * (1.0 + t) + 0.5 * v * (1.0 - t * t) * (0.7978845608028654 * (1.0 + 0.134145 * v * v))
    grad = g[...].astype(F32)
    gfeed = (mod[:, 5 * width :] * grad).astype(BF)
    gfeed_ref[...] = gfeed
    gup = (mm(gfeed, w_down[...]) * slope).astype(BF)
    gup_ref[...] = gup
    gthird = mm(gup, w_up[...], 1, 1)
    ga = normback(n, r, scale * gthird) + jnp.where(i == 0, grad, 0.0)
    low = ga.astype(BF)
    ga_ref[...] = low
    for j, (ref, chunk) in enumerate(zip((c0, c1, c2, c3), chunks_by_head(mm(low, wc_ref[...], 1, 1).astype(BF), h))):
        pack(ref, i ^ j, size, chunk)

    @pl.when(i == 0)
    def _():
        across_ref[...] = across
        vec_ref[4:5, :] = jnp.sum(gfeed.astype(F32), axis=0, keepdims=True)

    vec_ref[0:1, :] += jnp.sum(gthird, axis=0, keepdims=True)
    vec_ref[1:2, :] += jnp.sum(gthird * n, axis=0, keepdims=True)
    vec_ref[2:3, :] += jnp.sum(ga, axis=0, keepdims=True)
    vec_ref[3:4, :] += jnp.sum(gup.astype(F32), axis=0, keepdims=True)


def cross_back(
    head, a0, a1, a2, cq, p, inv, pair, cm, w_query, ga, after, proj, mod, gain, wout,
    dq_ref, dpair_ref, gas_ref, gproj_ref, c0, c1, c2, c3, vec_ref, kt, dk, dv,
):
    i, h = pl.program_id(0), head[0]
    size, width = after.shape

    @pl.when(i == 0)
    def _():
        vec_ref[...] = jnp.zeros_like(vec_ref)
        dk[...] = jnp.zeros_like(dk)
        dv[...] = jnp.zeros_like(dv)
        kt[...] = pair[0].astype(F32).T.astype(BF)

    grad = sum(unpack(a, i, size).astype(F32) for a in (a0, a1, a2))
    dq = softmax_back(pair[0], kt, pair[1], cq[...], p, inv, unpack(cm, i, size), grad, dk, dv)
    dq_ref[...] = dq
    gsecond = mm(dq, w_query[:, 3 * dq.shape[1] :], 1, 1)
    n, r = stats(after[...])
    gas = ga[...].astype(F32) + normback(n, r, gain[...] * gsecond)
    gas_ref[...] = gas.astype(BF)
    gproj = (mod[:, 2 * width : 3 * width] * gas).astype(BF)
    gproj_ref[...] = gproj
    for j, (ref, chunk) in enumerate(zip((c0, c1, c2, c3), chunks_by_head(mm(gproj, wout[...], 1, 1).astype(BF), h))):
        pack(ref, i ^ j, size, chunk)
    vec_ref[0:1, :] += jnp.sum(gas * proj[...].astype(F32), axis=0, keepdims=True)
    vec_ref[1:2, :] += jnp.sum(gsecond * n, axis=0, keepdims=True)
    vec_ref[2:3, :] += jnp.sum(gproj.astype(F32), axis=0, keepdims=True)

    @pl.when(i == pl.num_programs(0) - 1)
    def _():
        dpair_ref[0] = dk[...].astype(BF)
        dpair_ref[1] = dv[...].astype(BF)


def self_back(a0, a1, a2, qkv, p, inv, sm, grads_ref, kt, dk, dv):
    i = pl.program_id(0)
    size = p.shape[2]
    hw = qkv.shape[2]

    @pl.when(i == 0)
    def _():
        dk[...] = jnp.zeros_like(dk)
        dv[...] = jnp.zeros_like(dv)
        kt[...] = qkv[1].astype(F32).T.astype(BF)

    at = pl.ds(pl.multiple_of(i * size, size), size)
    grad = sum(unpack(a, i, size).astype(F32) for a in (a0, a1, a2))
    grads_ref[at, :hw] = softmax_back(
        qkv[1], kt, qkv[2], qkv[0, at, :], p, inv, unpack(sm, i, size), grad, dk, dv
    )

    @pl.when(i == pl.num_programs(0) - 1)
    def _():
        grads_ref[:, hw : 2 * hw] = dk[...].astype(BF)
        grads_ref[:, 2 * hw :] = dv[...].astype(BF)


def first_back(x0, x1, x2, x3, grads, w, mod, gas, gf_ref, vec_ref, x):
    i = pl.program_id(0)
    width = x0.shape[1]
    take(x, (x0, x1, x2, x3), i)

    @pl.when(i == 0)
    def _():
        vec_ref[...] = jnp.zeros_like(vec_ref)

    gfirst = mm(grads[...], w[:, : grads.shape[1]], 1, 1)
    n, r = stats(x[...].astype(F32))
    scale = 1.0 + mod[:, width : 2 * width]
    gf_ref[...] = (gas[...].astype(F32) + normback(n, r, scale * gfirst)).astype(BF)
    vec_ref[0:1, :] += jnp.sum(gfirst, axis=0, keepdims=True)
    vec_ref[1:2, :] += jnp.sum(gfirst * n, axis=0, keepdims=True)


def own_columns(head, *refs, hw):
    count = len(refs) // 2 - 1
    sources, target, held, sems = refs[:count], refs[count], refs[count + 1 : -1], refs[-1]
    copies = [pltpu.make_async_copy(source, place, sems.at[k]) for k, (source, place) in enumerate(zip(sources, held))]
    for copy in copies:
        copy.start()
    t = 0
    for copy, ref in zip(copies, held):
        copy.wait()
        for base in range(0, ref.shape[1], 4 * hw):
            part = pick([ref[:, base + a * hw : base + (a + 1) * hw] for a in range(4)], head[0])
            if len(target.shape) == 2:
                target[:, t * hw : (t + 1) * hw] = part
            else:
                for d in range(target.shape[0]):
                    target[d, :, t * hw : (t + 1) * hw] = part
            t += 1


def feed_weights(head, third, gup, gfeed, hidden, cm, ga, w_down, both_ref, c0, c1, c2, c3):
    width = ga.shape[1]
    hw = width // 4
    rows = hidden.shape[0] // 4
    both_ref[:, : gup.shape[1]] = mm(third[...], gup[...], 0, 0).astype(BF)
    both_ref[:, gup.shape[1] :] = mm(gfeed[...], hidden[...], 0, 0).astype(BF)
    chunks = chunks_by_head(mm(cm[...], ga[...], 0, 0).astype(BF), head[0])
    for j, ref in enumerate((c0, c1, c2, c3)):
        ref[:, :width] = mm(hidden[j * rows : (j + 1) * rows, :], w_down[...], 1, 1).astype(BF)
        for k in range(3):
            ref[:, width + k * hw : width + (k + 1) * hw] = chunks[j][k * rows : (k + 1) * rows]
        ref[:, width + 3 * hw :] = jnp.zeros((rows, ref.shape[1] - width - 3 * hw), BF)


def part_rows(value, odd, near_ref, far_ref, kr):
    if kr % 16:
        near_ref[...] = value
        far_ref[...] = value
        return
    for z in range(value.shape[0] // (2 * kr)):
        even_rows = value[2 * z * kr : (2 * z + 1) * kr]
        odd_rows = value[(2 * z + 1) * kr : (2 * z + 2) * kr]
        near_ref[z] = jnp.where(odd == 1, odd_rows, even_rows)
        far_ref[z] = jnp.where(odd == 1, even_rows, odd_rows)


def mid_weights(place, sm, gproj, second, dq, caption, dpair, w_rest, gcross, near_ref, far_ref, c0, c1, c2, c3, *, kr):
    hw = dq.shape[1]
    rows = gcross.shape[0]
    out_chunks = chunks_by_head(mm(sm[...], gproj[...], 0, 0).astype(BF), place[0])
    cap = mm(dpair[0], w_rest[:, 2 * hw : 3 * hw], 1, 1) + mm(dpair[1], w_rest[:, 3 * hw :], 1, 1)
    cap_chunks = chunks_by_head(cap.astype(BF), place[0])
    for ref, out_chunk, cap_chunk in zip((c0, c1, c2, c3), out_chunks, cap_chunks):
        for k in range(3):
            ref[:, k * hw : (k + 1) * hw] = out_chunk[k * rows : (k + 1) * rows]
        ref[:, 3 * hw :] = cap_chunk
    cross = jnp.concatenate([gcross[:, k * hw : (k + 1) * hw] for k in range(3)], axis=0)
    parts = [mm(second[...], dq[...], 0, 0)] + [mm(caption[...], dpair[t], 0, 0) for t in range(2)]
    part_rows(jnp.concatenate([cross] + [p.astype(BF) for p in parts], axis=1), place[1], near_ref, far_ref, kr)


def last_weights(place, first, gjoint, gout, near_ref, far_ref, *, kr):
    hw = gjoint.shape[1] // 3
    rows = gout.shape[0]
    cross = jnp.concatenate([gout[:, k * hw : (k + 1) * hw] for k in range(3)], axis=0)
    value = jnp.concatenate([cross, mm(first[...], gjoint[...], 0, 0).astype(BF)], axis=1)
    part_rows(value, place[1], near_ref, far_ref, kr)


def column_chunks(head, mid, last, *refs):
    own = refs[0].shape[0]
    value = jnp.concatenate([jnp.sum(v[...].astype(F32), axis=0) for v in (mid, last)], axis=1)
    for j, ref in enumerate(refs):
        ref[...] = pick([value[a * own : (a + 1) * own] for a in range(4)], head[0] ^ j).astype(BF)


def spread_columns(head, p0, p1, p2, p3, cross_ref, query_ref, pair_ref, out_ref, self_ref):
    hw = p0.shape[1] // 8
    got = [p[...].astype(F32) for p in (p0, p1, p2, p3)]
    for a in range(4):
        rows = pick(got, head[0] ^ a)
        for t, (ref, base) in enumerate(
            ((cross_ref, 0), (query_ref, 0), (pair_ref, 0), (pair_ref, 4), (out_ref, 0), (self_ref, 0), (self_ref, 4), (self_ref, 8))
        ):
            ref[:, (base + a) * hw : (base + a + 1) * hw] = rows[:, t * hw : (t + 1) * hw]


def on_device(
    frames,
    condition,
    captions,
    caption_lengths,
    modulation_weight,
    modulation_bias,
    self_weight,
    self_out,
    self_bias,
    cross_gain,
    cross_query,
    cross_pair,
    cross_out,
    cross_bias,
    up_weight,
    up_bias,
    down_weight,
    down_bias,
    cotangent,
):
    n = lax.axis_size("seq")
    h = lax.axis_index("head")
    s = lax.axis_index("seq")
    rows, width = frames.shape
    hw = width // 4
    kr = self_weight.shape[0]
    own = kr // 4
    total = rows * 4

    ff = up_weight.shape[1]
    head = h.astype(jnp.int32)[None]

    def full(v):
        return v, whole(v)

    def columns(weights, shape):
        (own_cols,) = call(
            partial(own_columns, hw=hw),
            1,
            [(head, SCALAR)] + [(v, pl.BlockSpec(memory_space=pltpu.HBM)) for v in weights],
            [out(shape, BF)],
            [pltpu.VMEM(v.shape, BF) for v in weights] + [pltpu.SemaphoreType.DMA((len(weights),))],
        )
        return own_cols

    w_own = columns((self_weight, cross_query, self_out, cross_out, cross_pair), (kr, 8 * hw))
    updown = jnp.concatenate([up_weight, down_weight.T], axis=1)
    condition, updown, w_own = lax.optimization_barrier((condition, updown, w_own))
    w_own = lax.all_gather(w_own, "seq", axis=0, tiled=True)
    one = pl.BlockSpec((width, width), lambda i: (0, 0))
    two = pl.BlockSpec((width, width), lambda i: (0, 1))
    x = head_rel(frames)
    biases = jnp.concatenate([self_bias, cross_bias, cross_gain, down_bias])[None]
    got = exchange(jnp.concatenate([condition.reshape(n, kr), jnp.broadcast_to(biases, (n, 4 * kr))], axis=1))
    cond_own = jax.nn.silu(got[:, :kr].astype(F32)).astype(BF)
    vectors = got[:, kr:].astype(F32).reshape(n, 4, kr).transpose(1, 0, 2).reshape(4, width)
    out_bias, co_bias, gain, dn_bias = vectors[0], vectors[1], vectors[2], vectors[3]
    mod_part = mm(cond_own, modulation_weight) + lax.dynamic_update_slice(
        jnp.zeros((n * modulation_bias.shape[0],), F32),
        modulation_bias.astype(F32),
        (s * modulation_bias.shape[0],),
    )
    g = head_rel(cotangent)
    mod_part, x, g = lax.optimization_barrier((mod_part, x, g))
    mod = exchange(mod_part).sum(0, keepdims=True)
    updown, w_own = after((updown, w_own), mod)
    updown = lax.all_gather(updown, "seq", axis=0, tiled=True)
    w_parts = w_own[:, 4 * hw : 6 * hw]
    mod, w_parts = lax.optimization_barrier((mod, w_parts))
    w_parts = head_rel(w_parts)
    caption = captions[0]
    slots = caption.shape[0]
    heads = hw // HD
    grid, block = 4, rows
    packed = (total // 2, 2 * hw)

    p_spec = pl.BlockSpec((heads, total, block), lambda i: (0, 0, i))
    cp_spec = pl.BlockSpec((heads, slots, block), lambda i: (0, 0, i))
    inv_spec = pl.BlockSpec((heads, block), lambda i: (0, i))
    wide = rows_of(block, width)
    thin = rows_of(block, hw)
    up_spec = pl.BlockSpec((width, ff), lambda i: (0, 0))
    down_spec = pl.BlockSpec((width, ff), lambda i: (0, 1))

    first, qkv, sm_own, probs, inv = call(
        self_forward,
        grid,
        [full(v) for v in (*x, mod)] + [(w_own, one)],
        [
            out((total, width), BF),
            out((3, total, hw), BF),
            out(packed, BF),
            out((heads, total, total), BF, p_spec),
            out((heads, total), F32, inv_spec),
        ],
        [pltpu.VMEM((hw, total), BF)],
    )
    sm_parts = head_rel(sm_own)
    sm, w_out, proj, after_self, second, cq, pair, cm_own, cprobs, cinv = call(
        cross_forward,
        grid,
        [(head, SCALAR), (caption_lengths, SCALAR)]
        + [full(v) for v in (*x, *sm_parts, mod, *w_parts, out_bias[None], gain[None])]
        + [(w_own, one), (w_own, two), full(caption)],
        [
            out((total, width), BF, wide),
            out((width, width), BF),
            out((total, width), BF, wide),
            out((total, width), F32, wide),
            out((total, width), BF, wide),
            out((total, hw), BF, thin),
            out((2, slots, hw), BF),
            out(packed, BF),
            out((heads, slots, total), BF, cp_spec),
            out((heads, total), F32, inv_spec),
        ],
        [pltpu.VMEM((hw, slots), BF), pltpu.VMEM((rows, width), BF)],
    )
    cm_parts = head_rel(cm_own)
    cm, w_cross, across, third, hidden, g_up, g_feed, ga, *chunks, vec_c = call(
        feed_both,
        grid,
        [(head, SCALAR), (after_self, wide)]
        + [full(v) for v in (*cm_parts, mod, *w_parts, co_bias[None])]
        + [(updown, up_spec), (updown, down_spec)]
        + [full(v) for v in (up_bias[None], *g)],
        [
            out((total, width), BF, wide),
            out((width, width), BF),
            out((rows, width), F32),
            out((total, width), BF, wide),
            out((total, ff), BF, rows_of(block, ff)),
            out((total, ff), BF, rows_of(block, ff)),
            out((total, width), BF, wide),
            out((total, width), BF, wide),
            *[out(packed, BF) for _ in range(4)],
            out((8, width), F32),
        ],
        [pltpu.VMEM((rows, width), BF)],
    )

    def near_terms(chunks):
        a, b = swap(chunks[1], 1), swap(chunks[3], 1)
        return chunks[0], a, (chunks[2].astype(F32) + b.astype(F32)).astype(BF)

    mine, near, other = near_terms(chunks)
    far = swap(other, 2)
    pad = -3 * hw % 128
    place = jnp.stack([h, s & 1]).astype(jnp.int32)

    def halves(columns):
        shape = (width, columns) if kr % 16 else (n // 2, kr, columns)
        return [out(shape, BF) for _ in range(2)]

    def parted(near_rows, far_rows):
        if kr % 16 == 0:
            return near_rows, far_rows
        near_rows, far_rows = (v.reshape(n // 2, 2, kr, -1) for v in (near_rows, far_rows))
        return (
            lax.dynamic_index_in_dim(near_rows, s & 1, 1, keepdims=False),
            lax.dynamic_index_in_dim(far_rows, 1 - (s & 1), 1, keepdims=False),
        )

    both, *feed_chunks = call(
        feed_weights,
        1,
        [(head, SCALAR)]
        + [full(v) for v in (after(third, other), g_up, g_feed, hidden, cm, ga)]
        + [(updown, down_spec)],
        [out((width, 2 * ff), BF)] + [out((rows, width + 3 * hw + pad), BF) for _ in range(4)],
    )
    both = exchange(after(both, far).reshape(n, kr, 2 * ff))
    feed_mine, feed_near, feed_other = near_terms(after(tuple(feed_chunks), far))
    far, feed_other = lax.optimization_barrier((far, feed_other))
    dq, dpair, gas, g_proj, *chunks, vec_d = call(
        cross_back,
        grid,
        [(head, SCALAR)]
        + [full(v) for v in (mine, near, far)]
        + [(cq, thin), (cprobs, cp_spec), (cinv, inv_spec), full(pair), full(cm_own), (w_own, one)]
        + [(ga, wide), (after_self, wide), (proj, wide), full(mod), full(gain[None]), full(w_out)],
        [
            out((total, hw), BF, thin),
            out((2, slots, hw), BF),
            out((total, width), BF, wide),
            out((total, width), BF, wide),
            *[out(packed, BF) for _ in range(4)],
            out((8, width), F32),
        ],
        [pltpu.VMEM((hw, slots), BF), pltpu.VMEM((slots, hw), F32), pltpu.VMEM((slots, hw), F32)],
    )
    feed_sum = feed_mine.astype(F32) + feed_near.astype(F32) + swap(feed_other, 2).astype(F32)
    chunks, feed_sum = lax.optimization_barrier((chunks, feed_sum))
    g_cross = feed_sum[:, width : width + 3 * hw].astype(BF)
    mine, near, other = near_terms(chunks)
    far = swap(other, 2)
    *mid, out0, out1, out2, out3 = call(
        partial(mid_weights, kr=kr),
        1,
        [(place, SCALAR)]
        + [full(v) for v in (after(sm, other), g_proj, second, dq, caption, dpair)]
        + [(w_own, two), full(g_cross)],
        halves(4 * hw) + [out((rows, 4 * hw), BF) for _ in range(4)],
    )
    out_chunks = (out0, out1, out2, out3)
    out_mine, out_near, out_other = near_terms(after(tuple(out_chunks), far))
    far, mid, out_other = lax.optimization_barrier((far, mid, out_other))
    mid = half_reduce(*parted(*mid))
    (g_joint,) = call(
        self_back,
        grid,
        [full(v) for v in (mine, near, far, qkv)]
        + [(probs, p_spec), (inv, inv_spec), full(sm_own)],
        [out((total, 3 * hw), BF)],
        [pltpu.VMEM((hw, total), BF), pltpu.VMEM((total, hw), F32), pltpu.VMEM((total, hw), F32)],
    )
    feed_sum = after(feed_sum, g_joint)
    feed = feed_sum[:, :width] + dn_bias
    output_frames = (across + mod[:, 5 * width :] * feed).astype(BF)
    gv_gate2 = jnp.sum(cotangent.astype(F32) * feed, axis=0, keepdims=True)
    out_sum = out_mine.astype(F32) + out_near.astype(F32) + swap(out_other, 2).astype(F32)
    grad_captions = out_sum[None, :, 3 * hw :]
    last = call(
        partial(last_weights, kr=kr),
        1,
        [(place, SCALAR)] + [full(v) for v in (first, after(g_joint, mid), out_sum[:, : 3 * hw].astype(BF))],
        halves(4 * hw),
    )
    gas, last, both = lax.optimization_barrier((gas, last, both))
    last = half_reduce(*parted(*last))
    mid = rest_reduce(after(mid, both))
    gf, vec_e = call(
        first_back,
        grid,
        [full(v) for v in x] + [(g_joint, rows_of(block, 3 * hw)), (w_own, one), full(mod), (gas, wide)],
        [out((total, width), BF, wide), out((8, width), F32)],
        [pltpu.VMEM((rows, width), BF)],
    )
    vec_e, gf, last = lax.optimization_barrier((vec_e, gf, last))
    last = rest_reduce(after(last, mid))
    grad_frames = head_sum([gf[j * rows : (j + 1) * rows] for j in range(4)])

    def over_heads(v):
        v = v + swap(v, 1)
        return v + swap(v, 2)

    vec = [vec_e[:2], vec_d[:1], vec_c[:2], gv_gate2, vec_d[2:3], vec_d[1:2], vec_c[2:3], vec_c[4:5]]
    vec = seq_gather(jnp.concatenate([over_heads(jnp.concatenate(vec, axis=0)), vec_c[3:4]], axis=0)[None])
    g_mod = vec[:, :6].reshape(n, 6 * width)
    g_cond = lax.dot_general(
        g_mod,
        modulation_weight.astype(F32),
        (((1,), (1,)), ((), ())),
        precision=lax.Precision.HIGHEST,
        preferred_element_type=F32,
    )
    g_silu = exchange(after(seq_order(g_cond, s), last)).reshape(width)
    g_cond = jax.vjp(jax.nn.silu, condition[0].astype(F32))[1](g_silu)[0]
    grad_condition = lax.dynamic_slice_in_dim(g_cond, h * hw, hw, 0)[None]
    cond_rows = seq_order(lax.dynamic_slice_in_dim(cond_own, h * own, own, 1), s)
    grad_mod_weight = lax.dot_general(
        cond_rows, g_mod, (((0,), (0,)), ((), ())), precision=lax.Precision.HIGHEST, preferred_element_type=F32
    )
    sums = vec.sum(0)
    index = s * 4 + h
    mb = 6 * width // (4 * n)
    grad_mod_bias = lax.dynamic_slice_in_dim(sums[:6].reshape(6 * width), index * mb, mb, 0)

    def own_vec(i):
        return lax.dynamic_slice_in_dim(sums[6 + i], index * own, own, 0)

    both = both.astype(F32).sum(0)
    cols = call(
        column_chunks, 1, [(head, SCALAR), full(mid), full(last)], [out((own, 8 * hw), BF) for _ in range(4)]
    )
    cols = [cols[0]] + [
        lax.ppermute(cols[j], "head", [(i, i ^ j) for i in range(4)]) for j in range(1, 4)
    ]
    grad_cross, grad_query, grad_pair, grad_out, grad_self = call(
        spread_columns,
        1,
        [(head, SCALAR)] + [full(v) for v in cols],
        [out((own, k * width), F32) for k in (1, 1, 2, 1, 3)],
    )
    return (
        output_frames,
        grad_frames,
        grad_condition,
        grad_captions,
        grad_mod_weight,
        grad_mod_bias,
        grad_self,
        grad_out,
        own_vec(0),
        own_vec(1),
        grad_query,
        grad_pair,
        grad_cross,
        own_vec(2),
        both[:, :ff],
        sums[10],
        both[:, ff:].T,
        own_vec(3),
    )


def solution(mesh):
    both = ("seq", "head")
    return jax.shard_map(
        on_device,
        mesh=mesh,
        in_specs=(
            P(both, None),
            P("seq", None),
            P("seq", None, None),
            P("seq"),
            P("seq", None),
            P("seq"),
            P("seq", None),
            P("seq", None),
            P("seq"),
            P("seq"),
            P("seq", None),
            P("seq", None),
            P("seq", None),
            P("seq"),
            P("seq", "head"),
            P("head"),
            P("head", "seq"),
            P("seq"),
            P(both, None),
        ),
        out_specs=(
            P(both, None),
            P(both, None),
            P("seq", "head"),
            P("seq", None, "head"),
            P(both, None),
            P(both),
            P(both, None),
            P(both, None),
            P(both),
            P(both),
            P(both, None),
            P(both, None),
            P(both, None),
            P(both),
            P("seq", "head"),
            P("head"),
            P("head", "seq"),
            P(both),
        ),
        check_vma=False,
    )
```

```python
from functools import partial

import jax
import jax.numpy as jnp
from jax import lax
from jax.experimental import pallas as pl
from jax.experimental.pallas import tpu as pltpu
from jax.sharding import PartitionSpec as P

HD = 64
BF = jnp.bfloat16
F32 = jnp.float32


def mm(a, b, ca=1, cb=0):
    return lax.dot_general(a, b, (((ca,), (cb,)), ((), ())), preferred_element_type=F32)


def swap(x, bit):
    return lax.ppermute(x, "head", [(i, i ^ bit) for i in range(4)])


def swap_rows(x, bit):
    blocks = jnp.split(swap(x, bit), 4, axis=0)
    return jnp.concatenate([blocks[i ^ bit] for i in range(4)], axis=0)


def head_rel(x, swap=swap):
    near = swap(x, 1)
    far = swap(x, 2)
    return [x, near, far, swap(far, 1)]


def pick(parts, index):
    low, high = (index & 1) == 1, (index & 2) == 2
    return jnp.where(
        high, jnp.where(low, parts[3], parts[2]), jnp.where(low, parts[1], parts[0])
    )


def head_sum(chunks, swap=swap):
    a, b = swap(chunks[1], 1), swap(chunks[3], 1)
    mine = chunks[0].astype(F32) + a.astype(F32)
    other = (chunks[2].astype(F32) + b.astype(F32)).astype(chunks[0].dtype)
    return mine + swap(other, 2).astype(F32)


def after(values, ready):
    return lax.optimization_barrier((values, ready))[0]


def seq_swap(x, bit):
    return lax.ppermute(x, "seq", [(i, i ^ bit) for i in range(lax.axis_size("seq"))])


def seq_bits():
    return [1 << b for b in range(lax.axis_size("seq").bit_length() - 1)]


def seq_gather(x):
    for bit in seq_bits():
        x = jnp.concatenate([x, seq_swap(x, bit)], axis=0)
    return x


def seq_scatter_sum(x):
    for bit in reversed(seq_bits()):
        x = x[:bit] + seq_swap(x[bit:], bit)
    return x


def seq_order(x, s):
    n = x.shape[0]
    at = (s ^ jnp.arange(n))[:, None] == jnp.arange(n)[None, :]
    precision = lax.Precision.HIGHEST if x.dtype == F32 else None
    return lax.dot_general(
        at.astype(x.dtype), x, (((1,), (0,)), ((), ())), precision=precision, preferred_element_type=F32
    )


def exchange(x):
    return lax.all_to_all(x, "seq", split_axis=0, concat_axis=0, tiled=True)


def alike():
    n = lax.axis_size("seq")
    return [list(range(odd, n, 2)) for odd in (0, 1)]


def half_reduce(near, far):
    return (near.astype(F32) + seq_swap(far, 1).astype(F32)).astype(BF)


def rest_reduce(part):
    return lax.all_to_all(part, "seq", split_axis=0, concat_axis=0, axis_index_groups=alike(), tiled=True)


def stats(v):
    mean = jnp.mean(v, axis=-1, keepdims=True)
    center = v - mean
    r = lax.rsqrt(jnp.mean(center * center, axis=-1, keepdims=True) + 1e-6)
    return center * r, r


def normback(n, r, e):
    return r * (
        e - jnp.mean(e, axis=-1, keepdims=True) - n * jnp.mean(e * n, axis=-1, keepdims=True)
    )


class Held:
    def __init__(self, outside, inside, sems, count):
        self.outside, self.inside, self.sems, self.count = outside, inside, sems, count
        self.pending = []
        self.shape, self.dtype = inside.shape, inside.dtype

    def copy(self, source, target):
        copy = pltpu.make_async_copy(source, target, self.sems.at[self.count[0]])
        self.count[0] += 1
        copy.start()
        self.pending.append(copy)

    def send(self, at=...):
        if self.outside is not None:
            self.copy(self.inside.at[at], self.outside.at[at])

    def wait(self):
        for copy in self.pending:
            copy.wait()
        self.pending = []

    def __getitem__(self, at):
        self.wait()
        return self.inside[at]

    def __setitem__(self, at, value):
        self.inside[at] = value


class Result(Held):
    def __getitem__(self, at):
        return self.inside[at]


def call(kernel, scalars, ins, outs, scratch=(), sends=0, small=0, limit=58):
    ins = [v if isinstance(v, tuple) else (v, ...) for v in ins]
    parts = [v if at is ... else jax.eval_shape(lambda x, at=at: x[at], v) for v, at in ins]

    def is_small(v):
        return v.size * v.dtype.itemsize <= small

    plain = [is_small(v) and at is ... for v, at in ins] + [is_small(v) for v in outs]
    kept = [v for v, p in zip((*parts, *outs), plain) if not p]

    def body(*refs):
        refs = list(refs)
        numbers = [refs.pop(0) for _ in scalars]
        outside = [refs.pop(0) for _ in plain]
        inside = [refs.pop(0) for _ in kept]
        sems, rest, count = refs[-1], refs[:-1], [0]
        arrays = []
        for k, (ref, p) in enumerate(zip(outside, plain)):
            kind = Held if k < len(ins) else Result
            arrays.append(kind(None, ref, sems, count) if p else kind(ref, inside.pop(0), sems, count))
        held, results = arrays[: len(ins)], arrays[len(ins) :]
        for v, (_, at) in zip(held, ins):
            if v.outside is not None:
                v.copy(v.outside.at[at], v.inside)
        kernel(*numbers, *held, *results, *rest)
        for v in results:
            if not v.pending:
                v.send()
        for v in arrays:
            v.wait()

    specs = [pl.BlockSpec(memory_space=pltpu.VMEM if p else pl.ANY) for p in plain]
    return pl.pallas_call(
        body,
        in_specs=[pl.BlockSpec(memory_space=pltpu.SMEM)] * len(scalars) + specs[: len(ins)],
        out_specs=specs[len(ins) :],
        out_shape=list(outs),
        scratch_shapes=[pltpu.VMEM(v.shape, v.dtype) for v in kept]
        + list(scratch)
        + [pltpu.SemaphoreType.DMA((len(kept) + sends + 1,))],
        compiler_params=pltpu.CompilerParams(vmem_limit_bytes=limit * 1024 * 1024),
    )(*scalars, *[v for v, _ in ins])


def out(shape, dtype):
    return jax.ShapeDtypeStruct(shape, dtype)


def block(b, size=256):
    return slice(b * size, (b + 1) * size)


def packed_at(shape, b):
    size, half = shape[0] // 2, shape[1] // 2
    return (block(b // 2, size), slice(half * (b % 2), half * (b % 2 + 1)))


def unpack(ref, b):
    return ref[packed_at(ref.shape, b)]


def pack(ref, b, value):
    ref[packed_at(ref.shape, b)] = value


def by_head(parts, head):
    return jnp.concatenate([pick(parts, head ^ a) for a in range(4)], axis=1)


def chunks_by_head(value, head):
    hw = value.shape[1] // 4
    blocks = [value[:, a * hw : (a + 1) * hw] for a in range(4)]
    return [pick(blocks, head ^ j) for j in range(4)]


def staggered(stages, tasks):
    done = [None] * len(tasks)
    for t in range(len(tasks) + len(stages) - 1):
        for k, stage in enumerate(stages):
            if 0 <= t - k < len(tasks):
                done[t - k] = stage(*tasks[t - k]) if k == 0 else stage(*tasks[t - k], done[t - k])
    return done


def of_head(values, hd):
    lane = lax.broadcasted_iota(jnp.int32, (1, values.shape[1]), 1) // HD
    return jnp.where(lane == hd, values, 0)


def softmax_columns(keys, queries, values_t, p_ref, inv_ref, visible=None):
    heads = keys.shape[1] // HD
    own_keys = [of_head(keys, hd) for hd in range(heads)]

    def scores(b, hd):
        return mm(own_keys[hd], queries[b], 1, 1)

    def weights(b, hd, st):
        if visible is not None:
            st = jnp.where(visible, st, -1e30)
        e = jnp.exp(st - jnp.max(st, axis=0, keepdims=True))
        inv = 1.0 / jnp.sum(e, axis=0, keepdims=True)
        low = e.astype(BF)
        p_ref[hd, :, block(b)] = low
        inv_ref[hd : hd + 1, block(b)] = inv
        return low, inv

    def mixed(b, hd, done):
        result = mm(values_t[hd * HD : (hd + 1) * HD, :], done[0]) * done[1]
        if hd == heads - 1:
            p_ref.send((slice(None), slice(None), block(b)))
        return result

    parts = staggered((scores, weights, mixed), [(b, hd) for b in range(len(queries)) for hd in range(heads)])
    return [
        jnp.concatenate(parts[b * heads : (b + 1) * heads], axis=0).T.astype(BF) for b in range(len(queries))
    ]


def softmax_back(keys, values, queries, p_ref, inv_ref, results, grads, ds_ref):
    heads = keys.shape[1] // HD
    keys_t = keys.astype(F32).T.astype(BF)
    own_values = [of_head(values, hd) for hd in range(heads)]
    count = len(grads)
    scaled, inner = [], []
    for b in range(count):
        go_t, o_t = grads[b].T, results[b].astype(F32).T
        parts = []
        for hd in range(heads):
            at = slice(hd * HD, (hd + 1) * HD)
            parts.append(go_t[at, :] * inv_ref[hd : hd + 1, block(b)])
            inner.append(jnp.sum(parts[-1] * o_t[at, :], axis=0, keepdims=True))
        scaled.append(jnp.concatenate(parts, axis=0).T.astype(BF))

    def dprob(b, hd):
        return mm(own_values[hd], scaled[b], 1, 1)

    def dscore(b, hd, dp):
        ds = (p_ref[hd, :, block(b)].astype(F32) * (dp - inner[b * heads + hd])).astype(BF)
        ds_ref[hd, :, block(b)] = ds
        return ds

    def dquery(b, hd, ds):
        return mm(keys_t[hd * HD : (hd + 1) * HD, :], ds)

    parts = staggered((dprob, dscore, dquery), [(b, hd) for b in range(count) for hd in range(heads)])
    dq = [
        (jnp.concatenate(parts[b * heads : (b + 1) * heads], axis=0).T * 0.125).astype(BF) for b in range(count)
    ]
    everything = jnp.concatenate(scaled, axis=0)
    dk = sum(of_head(mm(ds_ref[hd], queries), hd) for hd in range(heads))
    dv = sum(of_head(mm(p_ref[hd], everything), hd) for hd in range(heads))
    return dq, dk.astype(BF), dv.astype(BF)


BLOCKS = range(4)


def self_forward(x0, x1, x2, x3, mod, w, n_ref, qkv_ref, sm_ref, p_ref, inv_ref):
    width = x0.shape[1]
    hw = sm_ref.shape[1] // 2
    norms = [stats(x[...].astype(F32))[0] for x in (x0, x1, x2, x3)]
    scale, shift = 1.0 + mod[:, width : 2 * width], mod[:, :width]
    firsts = [(n * scale + shift).astype(BF) for n in norms]
    weights = w[:, 2 * hw :]
    joints = [mm(first, weights) for first in firsts]
    for b in BLOCKS:
        n_ref[block(b), :] = norms[b].astype(BF)
    n_ref.send()
    queries = [(joint[:, :hw] * 0.125).astype(BF) for joint in joints]
    keys = jnp.concatenate([joint[:, hw : 2 * hw].astype(BF) for joint in joints], axis=0)
    for b in BLOCKS:
        qkv_ref[0, block(b), :] = queries[b]
        qkv_ref[2, block(b), :] = joints[b][:, 2 * hw :].astype(BF)
    qkv_ref[1] = keys
    qkv_ref.send()
    values_t = jnp.concatenate([joint[:, 2 * hw :].T.astype(BF) for joint in joints], axis=1)
    for b, result in enumerate(softmax_columns(keys, queries, values_t, p_ref, inv_ref)):
        pack(sm_ref, b, result)


def cross_forward(
    head, length, x0, x1, x2, x3, w0, w1, w2, w3, sm0, sm1, sm2, sm3, mod, out_bias, gain, w_later, caption,
    sm_ref, wout_ref, proj_ref, after_ref, second_ref, cq_ref, pair_ref, cm_ref, p_ref, inv_ref,
):
    h = head[0]
    width = x0.shape[1]
    hw = cq_ref.shape[1]
    w_out = by_head([w[:, :hw] for w in (w0, w1, w2, w3)], h)
    wout_ref[...] = w_out
    wout_ref.send()
    mixed = [by_head([unpack(p, b ^ j) for j, p in enumerate((sm0, sm1, sm2, sm3))], h) for b in BLOCKS]
    projs = [mm(m, w_out) + out_bias[...] for m in mixed]
    pair = mm(caption[...], w_later[:, hw:])
    keys, values = pair[:, :hw].astype(BF), pair[:, hw:]
    pair_ref[0] = keys
    pair_ref[1] = values.astype(BF)
    afters, seconds = [], []
    for b, x in enumerate((x0, x1, x2, x3)):
        sm_ref[block(b), :] = mixed[b]
        proj_ref[block(b), :] = projs[b].astype(BF)
        after = x[...].astype(F32) + mod[:, 2 * width : 3 * width] * projs[b]
        after_ref[block(b), :] = after
        seconds.append((stats(after)[0] * gain[...]).astype(BF))
        second_ref[block(b), :] = seconds[b]
    for ref in (sm_ref, proj_ref, after_ref, second_ref):
        ref.send()
    queries = [(mm(second, w_later[:, :hw]) * 0.125).astype(BF) for second in seconds]
    for b in BLOCKS:
        cq_ref[block(b), :] = queries[b]
    slots = lax.broadcasted_iota(jnp.int32, (caption.shape[0], 1), 0)
    results = softmax_columns(keys, queries, values.T.astype(BF), p_ref, inv_ref, slots < length[0])
    for b, result in enumerate(results):
        pack(cm_ref, b, result)


def feed_both(
    head, cm0, w0, w1, w2, w3, cm1, cm2, cm3, after, co_bias, mod, w_up, up_bias, w_down, g0, g1, g2, g3,
    cm_ref, wc_ref, across_ref, third_ref, hidden_ref, gup_ref, gfeed_ref, ga_ref, c0, c1, c2, c3, vec_ref,
):
    h = head[0]
    width = after.shape[1]
    hw = width // 4
    ff = w_up.shape[1]
    w_cross = by_head([w[:, hw:] for w in (w0, w1, w2, w3)], h)
    wc_ref[...] = w_cross
    wc_ref.send()
    mixed = [by_head([unpack(p, b ^ j) for j, p in enumerate((cm0, cm1, cm2, cm3))], h) for b in BLOCKS]
    across = [after[block(b), :] + mm(mixed[b], w_cross) + co_bias[...] for b in BLOCKS]
    across_ref[...] = across[0]
    across_ref.send()
    scale, shift = 1.0 + mod[:, 4 * width : 5 * width], mod[:, 3 * width : 4 * width]
    norms = [stats(v) for v in across]
    thirds = [(n * scale + shift).astype(BF) for n, _ in norms]
    for b in BLOCKS:
        cm_ref[block(b), :] = mixed[b]
        third_ref[block(b), :] = thirds[b]
    cm_ref.send()
    third_ref.send()
    ups = [mm(third, w_up[...]) + up_bias[...].astype(F32) for third in thirds]
    cots = [g[...].astype(F32) for g in (g0, g1, g2, g3)]
    feeds = [(mod[:, 5 * width :] * cot).astype(BF) for cot in cots]
    hiddens = [mm(feed, w_down[...]) for feed in feeds]
    gups = []
    for b in BLOCKS:
        v = ups[b]
        t = jnp.tanh(0.7978845608028654 * (v + 0.044715 * v * v * v))
        hidden_ref[block(b), :] = (0.5 * v * (1.0 + t)).astype(BF)
        slope = 0.5 * (1.0 + t) + 0.5 * v * (1.0 - t * t) * (0.7978845608028654 * (1.0 + 0.134145 * v * v))
        gups.append((hiddens[b] * slope).astype(BF))
        gup_ref[block(b), :] = gups[b]
        gfeed_ref[block(b), :] = feeds[b]
    for ref in (hidden_ref, gup_ref, gfeed_ref):
        ref.send()
    gthirds = [mm(gup, w_up[...], 1, 1) for gup in gups]
    gas = [normback(*norms[b], scale * gthirds[b]) for b in BLOCKS]
    gas[0] = gas[0] + cots[0]
    lows = [ga.astype(BF) for ga in gas]
    for b in BLOCKS:
        ga_ref[block(b), :] = lows[b]
    ga_ref.send()
    for b in BLOCKS:
        chunks = chunks_by_head(mm(lows[b], w_cross, 1, 1).astype(BF), h)
        for j, (ref, chunk) in enumerate(zip((c0, c1, c2, c3), chunks)):
            pack(ref, b ^ j, chunk)

    def over_rows(values):
        return sum(jnp.sum(v, axis=0, keepdims=True) for v in values)

    vec_ref[...] = jnp.concatenate(
        [
            over_rows(gthirds),
            over_rows([gthirds[b] * norms[b][0] for b in BLOCKS]),
            over_rows(gas),
            over_rows([gup.astype(F32) for gup in gups]),
            over_rows([feeds[0].astype(F32)]),
            jnp.zeros((3, width), F32),
        ],
        axis=0,
    )


def cross_back(
    head, a0, a1, a2, cm, inv, pair, cq, p, w_later, ga, after, gain, mod, proj, wout,
    dq_ref, dpair_ref, gas_ref, gproj_ref, c0, c1, c2, c3, vec_ref, ds_ref,
):
    h = head[0]
    width = after.shape[1]
    hw = cq.shape[1]
    grads = [sum(unpack(a, b).astype(F32) for a in (a0, a1, a2)) for b in BLOCKS]
    results = [unpack(cm, b) for b in BLOCKS]
    dqs, dk, dv = softmax_back(pair[0], pair[1], cq[...], p, inv, results, grads, ds_ref)
    dpair_ref[0] = dk
    dpair_ref[1] = dv
    for b in BLOCKS:
        dq_ref[block(b), :] = dqs[b]
    gseconds = [mm(dq, w_later[:, :hw], 1, 1) for dq in dqs]
    norms = [stats(after[block(b), :]) for b in BLOCKS]
    gas = [ga[block(b), :].astype(F32) + normback(*norms[b], gain[...] * gseconds[b]) for b in BLOCKS]
    gprojs = [(mod[:, 2 * width : 3 * width] * v).astype(BF) for v in gas]
    for b in BLOCKS:
        gas_ref[block(b), :] = gas[b].astype(BF)
        gproj_ref[block(b), :] = gprojs[b]
    gas_ref.send()
    gproj_ref.send()
    for b in BLOCKS:
        chunks = chunks_by_head(mm(gprojs[b], wout[...], 1, 1).astype(BF), h)
        for j, (ref, chunk) in enumerate(zip((c0, c1, c2, c3), chunks)):
            pack(ref, b ^ j, chunk)

    def over_rows(values):
        return sum(jnp.sum(v, axis=0, keepdims=True) for v in values)

    vec_ref[...] = jnp.concatenate(
        [
            over_rows([gas[b] * proj[block(b), :].astype(F32) for b in BLOCKS]),
            over_rows([gseconds[b] * norms[b][0] for b in BLOCKS]),
            over_rows([gproj.astype(F32) for gproj in gprojs]),
            jnp.zeros((5, width), F32),
        ],
        axis=0,
    )


def self_back(a0, a1, a2, sm, inv, qkv, p, grads_ref, ds_ref):
    hw = qkv.shape[2]
    grads = [sum(unpack(a, b).astype(F32) for a in (a0, a1, a2)) for b in BLOCKS]
    results = [unpack(sm, b) for b in BLOCKS]
    dqs, dk, dv = softmax_back(qkv[1], qkv[2], qkv[0], p, inv, results, grads, ds_ref)
    for b in BLOCKS:
        grads_ref[block(b), :hw] = dqs[b]
    grads_ref[:, hw : 2 * hw] = dk
    grads_ref[:, 2 * hw :] = dv


def first_back(x0, x1, x2, x3, grads, w, mod, gas, gf_ref):
    width = x0.shape[1]
    weights = w[:, w.shape[1] - grads.shape[1] :]
    gfirsts = [mm(grads[block(b), :], weights, 1, 1) for b in BLOCKS]
    scale = 1.0 + mod[:, width : 2 * width]
    for b, x in enumerate((x0, x1, x2, x3)):
        ga = normback(*stats(x[...].astype(F32)), scale * gfirsts[b])
        gf_ref[block(b), :] = (gas[block(b), :].astype(F32) + ga).astype(BF)


def own_columns(head, *refs, hw):
    sources, target = refs[:-1], refs[-1]
    t = 0
    for ref in sources:
        for base in range(0, ref.shape[1], 4 * hw):
            part = pick([ref[:, base + a * hw : base + (a + 1) * hw] for a in range(4)], head[0])
            if len(target.shape) == 2:
                target[:, t * hw : (t + 1) * hw] = part
            else:
                for d in range(target.shape[0]):
                    target[d, :, t * hw : (t + 1) * hw] = part
            t += 1


def feed_weights(head, cm, ga, hidden, w_down, third, gup, gfeed, c0, c1, c2, c3, both_ref):
    width = ga.shape[1]
    hw = width // 4
    rows = hidden.shape[0] // 4
    chunks = chunks_by_head(mm(cm[...], ga[...], 0, 0).astype(BF), head[0])
    for j, ref in enumerate((c0, c1, c2, c3)):
        ref[:, :width] = mm(hidden[block(j, rows), :], w_down[...], 1, 1).astype(BF)
        for k in range(3):
            ref[:, width + k * hw : width + (k + 1) * hw] = chunks[j][k * rows : (k + 1) * rows]
        ref[:, width + 3 * hw :] = jnp.zeros((rows, ref.shape[1] - width - 3 * hw), BF)
        ref.send()
    both_ref[:, : gup.shape[1]] = mm(third[...], gup[...], 0, 0).astype(BF)
    both_ref[:, gup.shape[1] :] = mm(gfeed[...], hidden[...], 0, 0).astype(BF)


def part_rows(value, odd, near_ref, far_ref, kr):
    if kr % 16:
        near_ref[...] = value
        far_ref[...] = value
        return
    for z in range(value.shape[0] // (2 * kr)):
        even_rows = value[2 * z * kr : (2 * z + 1) * kr]
        odd_rows = value[(2 * z + 1) * kr : (2 * z + 2) * kr]
        near_ref[z] = jnp.where(odd == 1, odd_rows, even_rows)
        far_ref[z] = jnp.where(odd == 1, even_rows, odd_rows)


def mid_weights(
    place, f0, f1, f2, across, cot, mod, dn_bias, sm, gproj, caption, dpair, w_later, second, dq,
    near_ref, far_ref, c0, c1, c2, c3, output_ref, gate_ref, *, kr,
):
    hw, width = dq.shape[1], sm.shape[1]
    rows = f0.shape[0]
    total = sum(f[...].astype(F32) for f in (f0, f1, f2))
    feed = total[:, :width] + dn_bias[...]
    output_ref[...] = (across[...] + mod[:, 5 * width :] * feed).astype(BF)
    gate_ref[...] = jnp.sum(cot[...].astype(F32) * feed, axis=0, keepdims=True)
    out_chunks = chunks_by_head(mm(sm[...], gproj[...], 0, 0).astype(BF), place[0])
    cap = mm(dpair[0], w_later[:, hw : 2 * hw], 1, 1) + mm(dpair[1], w_later[:, 2 * hw :], 1, 1)
    cap_chunks = chunks_by_head(cap.astype(BF), place[0])
    for ref, out_chunk, cap_chunk in zip((c0, c1, c2, c3), out_chunks, cap_chunks):
        for k in range(3):
            ref[:, k * hw : (k + 1) * hw] = out_chunk[k * rows : (k + 1) * rows]
        ref[:, 3 * hw :] = cap_chunk
    low = total[:, width:].astype(BF)
    cross = jnp.concatenate([low[:, k * hw : (k + 1) * hw] for k in range(3)], axis=0)
    parts = [mm(second[...], dq[...], 0, 0)] + [mm(caption[...], dpair[t], 0, 0) for t in range(2)]
    part_rows(jnp.concatenate([cross] + [p.astype(BF) for p in parts], axis=1), place[1], near_ref, far_ref, kr)


def last_weights(place, n_one, gjoint, mod, w, o0, o1, o2, vec_c, vec_d, gate, near_ref, far_ref, cap_ref, vec_ref, *, kr):
    hw = gjoint.shape[1] // 3
    rows, width = o0.shape[0], w.shape[0]
    product = mm(n_one[...], gjoint[...], 0, 0)
    sums = jnp.sum(gjoint[...].astype(F32), axis=0, keepdims=True)
    weights = w[:, 2 * hw :].astype(F32)
    vec_ref[0:1, :] = jnp.sum(weights * sums, axis=1, keepdims=True).T
    vec_ref[1:2, :] = jnp.sum(weights * product, axis=1, keepdims=True).T
    grad = (1.0 + mod[:, width : 2 * width]).T * product + mod[:, :width].T * sums
    total = sum(o[...].astype(F32) for o in (o0, o1, o2))
    cap_ref[0] = total[:, 3 * hw :]
    low = total[:, : 3 * hw].astype(BF)
    cross = jnp.concatenate([low[:, k * hw : (k + 1) * hw] for k in range(3)], axis=0)
    part_rows(jnp.concatenate([cross, grad.astype(BF)], axis=1), place[1], near_ref, far_ref, kr)
    rest = (vec_d[0:1], vec_c[0:1], vec_c[1:2], gate[...], vec_d[2:3], vec_d[1:2], vec_c[2:3], vec_c[4:5], vec_c[3:4])
    for t, row in enumerate(rest):
        vec_ref[2 + t : 3 + t, :] = row
    vec_ref[2 + len(rest) :, :] = jnp.zeros((vec_ref.shape[0] - 2 - len(rest), width), F32)


def column_chunks(head, mid, last, *refs):
    own = refs[0].shape[0]
    parts = mid[...], last[:, : mid.shape[1], :]
    value = jnp.concatenate([jnp.sum(v.astype(F32), axis=0) for v in parts], axis=1)
    for j, ref in enumerate(refs):
        ref[...] = pick([value[a * own : (a + 1) * own] for a in range(4)], head[0] ^ j).astype(BF)


def spread_columns(head, p0, p1, p2, p3, cross_ref, query_ref, pair_ref, out_ref, self_ref):
    hw = p0.shape[1] // 8
    got = [p[...].astype(F32) for p in (p0, p1, p2, p3)]
    for a in range(4):
        rows = pick(got, head[0] ^ a)
        for t, (ref, base) in enumerate(
            ((cross_ref, 0), (query_ref, 0), (pair_ref, 0), (pair_ref, 4), (out_ref, 0), (self_ref, 0), (self_ref, 4), (self_ref, 8))
        ):
            ref[:, (base + a) * hw : (base + a + 1) * hw] = rows[:, t * hw : (t + 1) * hw]


def on_device(
    frames,
    condition,
    captions,
    caption_lengths,
    modulation_weight,
    modulation_bias,
    self_weight,
    self_out,
    self_bias,
    cross_gain,
    cross_query,
    cross_pair,
    cross_out,
    cross_bias,
    up_weight,
    up_bias,
    down_weight,
    down_bias,
    cotangent,
):
    n = lax.axis_size("seq")
    h = lax.axis_index("head")
    s = lax.axis_index("seq")
    rows, width = frames.shape
    hw = width // 4
    kr = self_weight.shape[0]
    own = kr // 4
    total = rows * 4

    ff = up_weight.shape[1]
    head = h.astype(jnp.int32)[None]

    def columns(weights, shape):
        return call(partial(own_columns, hw=hw), [head], weights, [out(shape, BF)])[0]

    w_own = columns((self_out, cross_out, self_weight), (kr, 5 * hw))
    condition, w_own, later = lax.optimization_barrier((condition, w_own, (cross_query, cross_pair)))
    w_later = columns(later, (n, kr, 3 * hw))
    w_own = lax.all_gather(w_own, "seq", axis=0, tiled=True)
    x = head_rel(frames)
    biases = jnp.concatenate([self_bias, cross_bias, cross_gain, down_bias])[None]
    got = exchange(jnp.concatenate([condition.reshape(n, kr), jnp.broadcast_to(biases, (n, 4 * kr))], axis=1))
    cond_own = jax.nn.silu(got[:, :kr].astype(F32)).astype(BF)
    vectors = got[:, kr:].astype(F32).reshape(n, 4, kr).transpose(1, 0, 2).reshape(4, width)
    out_bias, co_bias, gain, dn_bias = vectors[0], vectors[1], vectors[2], vectors[3]
    mod_part = mm(cond_own, modulation_weight) + lax.dynamic_update_slice(
        jnp.zeros((n * modulation_bias.shape[0],), F32),
        modulation_bias.astype(F32),
        (s * modulation_bias.shape[0],),
    )
    g = head_rel(cotangent)
    mod_part, x = lax.optimization_barrier((mod_part, x))
    mod = exchange(mod_part).sum(0, keepdims=True)
    w_own = after(w_own, (mod, w_later, g))
    updown = after((up_weight, down_weight), (mod, g))
    updown = jnp.concatenate([updown[0], updown[1].T], axis=1)
    updown = lax.all_gather(updown, "seq", axis=0, tiled=True)
    w_up = (updown, (slice(None), slice(0, ff)))
    w_down = (updown, (slice(None), slice(ff, 2 * ff)))
    w_later = exchange(after(w_later, mod)).reshape(width, 3 * hw)
    w_parts = w_own[:, : 2 * hw]
    mod, w_parts = lax.optimization_barrier((mod, w_parts))
    w_parts = head_rel(w_parts)
    caption = captions[0]
    slots = caption.shape[0]
    heads = hw // HD
    packed = (total // 2, 2 * hw)
    pad = -3 * hw % 128
    deep = out((total, width), BF)
    n_one, qkv, sm_own, probs, inv = call(
        self_forward,
        [],
        [*x, mod, w_own],
        [deep, out((3, total, hw), BF), out(packed, BF), out((heads, total, total), BF), out((heads, total), F32)],
        sends=4,
    )
    sm_parts = head_rel(sm_own)
    sm, w_out, proj, after_self, second, cq, pair, cm_own, cprobs, cinv = call(
        cross_forward,
        [head, caption_lengths],
        [*x, *w_parts, *sm_parts, mod, out_bias[None], gain[None], w_later, caption],
        [
            deep,
            out((width, width), BF),
            deep,
            out((total, width), F32),
            deep,
            out((total, hw), BF),
            out((2, slots, hw), BF),
            out(packed, BF),
            out((heads, slots, total), BF),
            out((heads, total), F32),
        ],
        sends=4,
    )
    cm_parts = head_rel(cm_own)
    cm, w_cross, across, third, hidden, g_up, g_feed, ga, *chunks, vec_c = call(
        feed_both,
        [head],
        [cm_parts[0], *w_parts, *cm_parts[1:], after_self, co_bias[None], mod]
        + [w_up, up_bias[None], w_down, *g],
        [deep, out((width, width), BF), out((rows, width), F32), deep]
        + [out((total, ff), BF), out((total, ff), BF), deep, deep]
        + [out(packed, BF) for _ in range(4)]
        + [out((8, width), F32)],
    )

    def near_terms(chunks):
        a, b = swap(chunks[1], 1), swap(chunks[3], 1)
        return chunks[0], a, (chunks[2].astype(F32) + b.astype(F32)).astype(BF)

    mine, near, other = near_terms(chunks)
    far = swap(other, 2)
    place = jnp.stack([h, s & 1]).astype(jnp.int32)

    def halves(columns):
        shape = (width, columns) if kr % 16 else (n // 2, kr, columns)
        return [out(shape, BF) for _ in range(2)]

    def parted(near_rows, far_rows):
        if kr % 16 == 0:
            return near_rows, far_rows
        near_rows, far_rows = (v.reshape(n // 2, 2, kr, -1) for v in (near_rows, far_rows))
        return (
            lax.dynamic_index_in_dim(near_rows, s & 1, 1, keepdims=False),
            lax.dynamic_index_in_dim(far_rows, 1 - (s & 1), 1, keepdims=False),
        )

    *feed_chunks, both = call(
        feed_weights,
        [head],
        [after(cm, other), ga, hidden, w_down, third, g_up, g_feed],
        [out((rows, width + 3 * hw + pad), BF) for _ in range(4)] + [out((width, 2 * ff), BF)],
    )
    both = exchange(after(both, far).reshape(n, kr, 2 * ff))
    feed_mine, feed_near, feed_other = near_terms(after(tuple(feed_chunks), far))
    far, feed_other = lax.optimization_barrier((far, feed_other))
    feed_far = swap(feed_other, 2)
    dq, dpair, gas, g_proj, *chunks, vec_d = call(
        cross_back,
        [head],
        [mine, near, far, cm_own, cinv, pair, cq, cprobs, w_later, ga, after_self, gain[None], mod, proj, w_out],
        [out((total, hw), BF), out((2, slots, hw), BF), deep, deep]
        + [out(packed, BF) for _ in range(4)]
        + [out((8, width), F32)],
        [pltpu.VMEM((heads, slots, total), BF)],
    )
    mine, near, other = near_terms(chunks)
    other, feed_far = lax.optimization_barrier((other, feed_far))
    far = swap(other, 2)
    *mid, out0, out1, out2, out3, output_frames, gv_gate2 = call(
        partial(mid_weights, kr=kr),
        [place],
        [feed_mine, feed_near, feed_far, across, cotangent, mod, dn_bias[None]]
        + [after(sm, other), g_proj, caption, dpair, w_later, second, dq],
        halves(4 * hw)
        + [out((rows, 4 * hw), BF) for _ in range(4)]
        + [out((rows, width), BF), out((1, width), F32)],
    )
    out_mine, out_near, out_other = near_terms(after((out0, out1, out2, out3), far))
    far, mid, out_other = lax.optimization_barrier((far, mid, out_other))
    mid = half_reduce(*parted(*mid))
    out_far = swap(out_other, 2)
    (g_joint,) = call(
        self_back,
        [],
        [mine, near, far, sm_own, inv, qkv, probs],
        [out((total, 3 * hw), BF)],
        [pltpu.VMEM((heads, total, total), BF)],
    )
    n_one, out_far, mid, both = after((n_one, out_far, mid, both), g_joint)
    *last, grad_captions, vec = call(
        partial(last_weights, kr=kr),
        [place],
        [n_one, g_joint, mod, w_own, out_mine, out_near, out_far, vec_c, vec_d, gv_gate2],
        halves(4 * hw) + [out((1, slots, hw), F32), out((16, width), F32)],
    )
    mid = rest_reduce(after(mid, both))
    gas, last, vec = lax.optimization_barrier((gas, last, vec))
    shared = vec + swap(vec, 1)
    shared = shared + swap(shared, 2)
    vec = jnp.where(jnp.arange(16)[:, None] == 10, vec, shared).astype(BF)
    last = half_reduce(*parted(*last))
    vec = jnp.concatenate([vec, seq_swap(vec, 1)], axis=0)
    (gf,) = call(first_back, [], [*x, g_joint, w_own, mod, gas], [deep])
    gf, last, vec, mid = lax.optimization_barrier((gf, last, vec, mid))
    last = jnp.concatenate([last, jnp.broadcast_to(vec[None], (n // 2, *vec.shape))], axis=1)
    last = rest_reduce(last)
    vec = last[:, kr:].reshape(n, 16, width).astype(F32)
    if kr % 16:
        last = last[:, :kr]
    grad_frames = head_sum([gf[j * rows : (j + 1) * rows] for j in range(4)])

    def pairs(v):
        v = v.reshape(n // 2, 2, -1)
        return jnp.where((s & 1) == 1, v[:, ::-1], v).reshape(n, -1)

    g_mod = vec[:, :6].reshape(n, 6 * width)
    g_cond = lax.dot_general(
        g_mod,
        modulation_weight.astype(F32),
        (((1,), (1,)), ((), ())),
        precision=lax.Precision.HIGHEST,
        preferred_element_type=F32,
    )
    g_silu = exchange(pairs(g_cond)).reshape(width)
    g_cond = jax.vjp(jax.nn.silu, condition[0].astype(F32))[1](g_silu)[0]
    grad_condition = lax.dynamic_slice_in_dim(g_cond, h * hw, hw, 0)[None]
    cond_rows = pairs(lax.dynamic_slice_in_dim(cond_own, h * own, own, 1).astype(F32))
    grad_mod_weight = lax.dot_general(
        cond_rows, g_mod, (((0,), (0,)), ((), ())), precision=lax.Precision.HIGHEST, preferred_element_type=F32
    )
    sums = vec.sum(0)
    index = s * 4 + h
    mb = 6 * width // (4 * n)
    grad_mod_bias = lax.dynamic_slice_in_dim(sums[:6].reshape(6 * width), index * mb, mb, 0)

    def own_vec(i):
        return lax.dynamic_slice_in_dim(sums[6 + i], index * own, own, 0)

    both = both.astype(F32).sum(0)
    tiny = dict(small=1 << 20, limit=8)
    cols = call(column_chunks, [head], [mid, last], [out((own, 8 * hw), BF) for _ in range(4)], **tiny)
    cols = [cols[0]] + [
        lax.ppermute(cols[j], "head", [(i, i ^ j) for i in range(4)]) for j in range(1, 4)
    ]
    grad_cross, grad_query, grad_pair, grad_out, grad_self = call(
        spread_columns, [head], cols, [out((own, k * width), F32) for k in (1, 1, 2, 1, 3)], **tiny
    )
    return (
        output_frames,
        grad_frames,
        grad_condition,
        grad_captions,
        grad_mod_weight,
        grad_mod_bias,
        grad_self,
        grad_out,
        own_vec(0),
        own_vec(1),
        grad_query,
        grad_pair,
        grad_cross,
        own_vec(2),
        both[:, :ff],
        sums[10],
        both[:, ff:].T,
        own_vec(3),
    )


def solution(mesh):
    both = ("seq", "head")
    return jax.shard_map(
        on_device,
        mesh=mesh,
        in_specs=(
            P(both, None),
            P("seq", None),
            P("seq", None, None),
            P("seq"),
            P("seq", None),
            P("seq"),
            P("seq", None),
            P("seq", None),
            P("seq"),
            P("seq"),
            P("seq", None),
            P("seq", None),
            P("seq", None),
            P("seq"),
            P("seq", "head"),
            P("head"),
            P("head", "seq"),
            P("seq"),
            P(both, None),
        ),
        out_specs=(
            P(both, None),
            P(both, None),
            P("seq", "head"),
            P("seq", None, "head"),
            P(both, None),
            P(both),
            P(both, None),
            P(both, None),
            P(both),
            P(both),
            P(both, None),
            P(both, None),
            P(both, None),
            P(both),
            P("seq", "head"),
            P("head"),
            P("head", "seq"),
            P(both),
        ),
        check_vma=False,
    )
```

```python
from functools import partial

import jax
import jax.numpy as jnp
from jax import lax
from jax.experimental import pallas as pl
from jax.experimental.pallas import tpu as pltpu
from jax.sharding import PartitionSpec as P

HD = 64
BF = jnp.bfloat16
F32 = jnp.float32


def mm(a, b, ca=1, cb=0):
    return lax.dot_general(a, b, (((ca,), (cb,)), ((), ())), preferred_element_type=F32)


def swap(x, bit):
    return lax.ppermute(x, "head", [(i, i ^ bit) for i in range(4)])


def swap_rows(x, bit):
    blocks = jnp.split(swap(x, bit), 4, axis=0)
    return jnp.concatenate([blocks[i ^ bit] for i in range(4)], axis=0)


def head_rel(x, swap=swap):
    near = swap(x, 1)
    far = swap(x, 2)
    return [x, near, far, swap(far, 1)]


def pick(parts, index):
    low, high = (index & 1) == 1, (index & 2) == 2
    return jnp.where(
        high, jnp.where(low, parts[3], parts[2]), jnp.where(low, parts[1], parts[0])
    )


def after(values, ready):
    return lax.optimization_barrier((values, ready))[0]


def seq_swap(x, bit):
    return lax.ppermute(x, "seq", [(i, i ^ bit) for i in range(lax.axis_size("seq"))])


def exchange(x):
    return lax.all_to_all(x, "seq", split_axis=0, concat_axis=0, tiled=True)


def half_reduce(near, far):
    return (near.astype(F32) + seq_swap(far, 1).astype(F32)).astype(BF)


def rest_reduce(x, sent=None):
    x, bit = x.astype(F32), 2
    while x.shape[0] > 1:
        send = x[1::2].astype(BF)
        if sent is not None:
            sent.append(send)
        x, bit = x[0::2] + seq_swap(send, bit).astype(F32), 2 * bit
    return x[0]


def stats(v):
    mean = jnp.mean(v, axis=-1, keepdims=True)
    center = v - mean
    r = lax.rsqrt(jnp.mean(center * center, axis=-1, keepdims=True) + 1e-6)
    return center * r, r


def normback(n, r, e):
    return r * (
        e - jnp.mean(e, axis=-1, keepdims=True) - n * jnp.mean(e * n, axis=-1, keepdims=True)
    )


class Held:
    def __init__(self, outside, inside, sems, count):
        self.outside, self.inside, self.sems, self.count = outside, inside, sems, count
        self.pending = []
        self.shape, self.dtype = inside.shape, inside.dtype

    def copy(self, source, target):
        copy = pltpu.make_async_copy(source, target, self.sems.at[self.count[0]])
        self.count[0] += 1
        copy.start()
        self.pending.append(copy)

    def send(self, at=...):
        if self.outside is not None:
            self.copy(self.inside.at[at], self.outside.at[at])

    def wait(self):
        for copy in self.pending:
            copy.wait()
        self.pending = []

    def __getitem__(self, at):
        self.wait()
        return self.inside[at]

    def __setitem__(self, at, value):
        self.inside[at] = value


class Result(Held):
    def __getitem__(self, at):
        return self.inside[at]


def call(kernel, scalars, ins, outs, scratch=(), sends=0, small=0, limit=58):
    ins = [v if isinstance(v, tuple) else (v, ...) for v in ins]
    parts = [v if at is ... else jax.eval_shape(lambda x, at=at: x[at], v) for v, at in ins]

    def is_small(v):
        return v.size * v.dtype.itemsize <= small

    plain = [is_small(v) and at is ... for v, at in ins] + [is_small(v) for v in outs]
    kept = [v for v, p in zip((*parts, *outs), plain) if not p]

    def body(*refs):
        refs = list(refs)
        numbers = [refs.pop(0) for _ in scalars]
        outside = [refs.pop(0) for _ in plain]
        inside = [refs.pop(0) for _ in kept]
        sems, rest, count = refs[-1], refs[:-1], [0]
        arrays = []
        for k, (ref, p) in enumerate(zip(outside, plain)):
            kind = Held if k < len(ins) else Result
            arrays.append(kind(None, ref, sems, count) if p else kind(ref, inside.pop(0), sems, count))
        held, results = arrays[: len(ins)], arrays[len(ins) :]
        for v, (_, at) in zip(held, ins):
            if v.outside is not None:
                v.copy(v.outside.at[at], v.inside)
        kernel(*numbers, *held, *results, *rest)
        for v in results:
            if not v.pending:
                v.send()
        for v in arrays:
            v.wait()

    specs = [pl.BlockSpec(memory_space=pltpu.VMEM if p else pl.ANY) for p in plain]
    return pl.pallas_call(
        body,
        in_specs=[pl.BlockSpec(memory_space=pltpu.SMEM)] * len(scalars) + specs[: len(ins)],
        out_specs=specs[len(ins) :],
        out_shape=list(outs),
        scratch_shapes=[pltpu.VMEM(v.shape, v.dtype) for v in kept]
        + list(scratch)
        + [pltpu.SemaphoreType.DMA((len(kept) + sends + 1,))],
        compiler_params=pltpu.CompilerParams(vmem_limit_bytes=limit * 1024 * 1024),
    )(*scalars, *[v for v, _ in ins])


def out(shape, dtype):
    return jax.ShapeDtypeStruct(shape, dtype)


def block(b, size=256):
    return slice(b * size, (b + 1) * size)


def packed_at(shape, b):
    size, half = shape[0] // 2, shape[1] // 2
    return (block(b // 2, size), slice(half * (b % 2), half * (b % 2 + 1)))


def unpack(ref, b):
    return ref[packed_at(ref.shape, b)]


def pack(ref, b, value):
    ref[packed_at(ref.shape, b)] = value


def by_head(parts, head):
    return jnp.concatenate([pick(parts, head ^ a) for a in range(4)], axis=1)


def chunks_by_head(value, head):
    hw = value.shape[1] // 4
    blocks = [value[:, a * hw : (a + 1) * hw] for a in range(4)]
    return [pick(blocks, head ^ j) for j in range(4)]


def staggered(stages, tasks):
    done = [None] * len(tasks)
    for t in range(len(tasks) + len(stages) - 1):
        for k, stage in enumerate(stages):
            if 0 <= t - k < len(tasks):
                done[t - k] = stage(*tasks[t - k]) if k == 0 else stage(*tasks[t - k], done[t - k])
    return done


def of_head(values, hd):
    lane = lax.broadcasted_iota(jnp.int32, (1, values.shape[1]), 1) // HD
    return jnp.where(lane == hd, values, 0)


def softmax_columns(keys, queries, values_t, p_ref, inv_ref, visible=None):
    heads = keys.shape[1] // HD
    own_keys = [of_head(keys, hd) for hd in range(heads)]

    def scores(b, hd):
        return mm(own_keys[hd], queries[b], 1, 1)

    def weights(b, hd, st):
        if visible is not None:
            st = jnp.where(visible, st, -1e30)
        e = jnp.exp(st - jnp.max(st, axis=0, keepdims=True))
        inv = 1.0 / jnp.sum(e, axis=0, keepdims=True)
        low = e.astype(BF)
        p_ref[hd, :, block(b)] = low
        inv_ref[hd : hd + 1, block(b)] = inv
        return low, inv

    def mixed(b, hd, done):
        result = mm(values_t[hd * HD : (hd + 1) * HD, :], done[0]) * done[1]
        if hd == heads - 1:
            p_ref.send((slice(None), slice(None), block(b)))
        return result

    parts = staggered((scores, weights, mixed), [(b, hd) for b in range(len(queries)) for hd in range(heads)])
    return [
        jnp.concatenate(parts[b * heads : (b + 1) * heads], axis=0).T.astype(BF) for b in range(len(queries))
    ]


def softmax_back(keys, values, queries, p_ref, inv_ref, results, grads, ds_ref):
    heads = keys.shape[1] // HD
    keys_t = keys.astype(F32).T.astype(BF)
    own_values = [of_head(values, hd) for hd in range(heads)]
    count = len(grads)
    scaled, inner = [], []
    for b in range(count):
        go_t, o_t = grads[b].T, results[b].astype(F32).T
        parts = []
        for hd in range(heads):
            at = slice(hd * HD, (hd + 1) * HD)
            parts.append(go_t[at, :] * inv_ref[hd : hd + 1, block(b)])
            inner.append(jnp.sum(parts[-1] * o_t[at, :], axis=0, keepdims=True))
        scaled.append(jnp.concatenate(parts, axis=0).T.astype(BF))

    def dprob(b, hd):
        return mm(own_values[hd], scaled[b], 1, 1)

    def dscore(b, hd, dp):
        ds = (p_ref[hd, :, block(b)].astype(F32) * (dp - inner[b * heads + hd])).astype(BF)
        ds_ref[hd, :, block(b)] = ds
        return ds

    def dquery(b, hd, ds):
        return mm(keys_t[hd * HD : (hd + 1) * HD, :], ds)

    parts = staggered((dprob, dscore, dquery), [(b, hd) for b in range(count) for hd in range(heads)])
    dq = [
        (jnp.concatenate(parts[b * heads : (b + 1) * heads], axis=0).T * 0.125).astype(BF) for b in range(count)
    ]
    everything = jnp.concatenate(scaled, axis=0)
    dk = sum(of_head(mm(ds_ref[hd], queries), hd) for hd in range(heads))
    dv = sum(of_head(mm(p_ref[hd], everything), hd) for hd in range(heads))
    return dq, dk.astype(BF), dv.astype(BF)


BLOCKS = range(4)


def self_forward(x0, x1, x2, x3, mod, w, n_ref, qkv_ref, sm_ref, p_ref, inv_ref):
    width = x0.shape[1]
    hw = sm_ref.shape[1] // 2
    norms = [stats(x[...].astype(F32))[0] for x in (x0, x1, x2, x3)]
    scale, shift = 1.0 + mod[:, width : 2 * width], mod[:, :width]
    firsts = [(n * scale + shift).astype(BF) for n in norms]
    weights = w[:, 2 * hw :]
    joints = [mm(first, weights) for first in firsts]
    for b in BLOCKS:
        n_ref[block(b), :] = norms[b].astype(BF)
    n_ref.send()
    queries = [(joint[:, :hw] * 0.125).astype(BF) for joint in joints]
    keys = jnp.concatenate([joint[:, hw : 2 * hw].astype(BF) for joint in joints], axis=0)
    for b in BLOCKS:
        qkv_ref[0, block(b), :] = queries[b]
        qkv_ref[2, block(b), :] = joints[b][:, 2 * hw :].astype(BF)
    qkv_ref[1] = keys
    qkv_ref.send()
    values_t = jnp.concatenate([joint[:, 2 * hw :].T.astype(BF) for joint in joints], axis=1)
    for b, result in enumerate(softmax_columns(keys, queries, values_t, p_ref, inv_ref)):
        pack(sm_ref, b, result)


def cross_forward(
    head, length, x0, x1, x2, x3, w0, w1, w2, w3, sm0, sm1, sm2, sm3, mod, out_bias, gain, w_later, caption,
    sm_ref, wout_ref, proj_ref, after_ref, second_ref, cq_ref, pair_ref, cm_ref, p_ref, inv_ref,
):
    h = head[0]
    width = x0.shape[1]
    hw = cq_ref.shape[1]
    w_out = by_head([w[:, :hw] for w in (w0, w1, w2, w3)], h)
    wout_ref[...] = w_out
    wout_ref.send()
    mixed = [by_head([unpack(p, b ^ j) for j, p in enumerate((sm0, sm1, sm2, sm3))], h) for b in BLOCKS]
    projs = [mm(m, w_out) + out_bias[...] for m in mixed]
    pair = mm(caption[...], w_later[:, hw:])
    keys, values = pair[:, :hw].astype(BF), pair[:, hw:]
    pair_ref[0] = keys
    pair_ref[1] = values.astype(BF)
    afters, seconds = [], []
    for b, x in enumerate((x0, x1, x2, x3)):
        sm_ref[block(b), :] = mixed[b]
        proj_ref[block(b), :] = projs[b].astype(BF)
        after = x[...].astype(F32) + mod[:, 2 * width : 3 * width] * projs[b]
        after_ref[block(b), :] = after
        seconds.append((stats(after)[0] * gain[...]).astype(BF))
        second_ref[block(b), :] = seconds[b]
    for ref in (sm_ref, proj_ref, after_ref, second_ref):
        ref.send()
    queries = [(mm(second, w_later[:, :hw]) * 0.125).astype(BF) for second in seconds]
    for b in BLOCKS:
        cq_ref[block(b), :] = queries[b]
    slots = lax.broadcasted_iota(jnp.int32, (caption.shape[0], 1), 0)
    results = softmax_columns(keys, queries, values.T.astype(BF), p_ref, inv_ref, slots < length[0])
    for b, result in enumerate(results):
        pack(cm_ref, b, result)


def feed_both(
    head, cm0, w0, w1, w2, w3, cm1, cm2, cm3, after, co_bias, mod, w_up, up_bias, w_down, g0, g1, g2, g3,
    cm_ref, wc_ref, across_ref, third_ref, hidden_ref, gup_ref, gfeed_ref, ga_ref, c0, c1, c2, c3, vec_ref,
):
    h = head[0]
    width = after.shape[1]
    hw = width // 4
    ff = w_up.shape[1]
    w_cross = by_head([w[:, hw:] for w in (w0, w1, w2, w3)], h)
    wc_ref[...] = w_cross
    wc_ref.send()
    mixed = [by_head([unpack(p, b ^ j) for j, p in enumerate((cm0, cm1, cm2, cm3))], h) for b in BLOCKS]
    across = [after[block(b), :] + mm(mixed[b], w_cross) + co_bias[...] for b in BLOCKS]
    across_ref[...] = across[0]
    across_ref.send()
    scale, shift = 1.0 + mod[:, 4 * width : 5 * width], mod[:, 3 * width : 4 * width]
    norms = [stats(v) for v in across]
    thirds = [(n * scale + shift).astype(BF) for n, _ in norms]
    for b in BLOCKS:
        cm_ref[block(b), :] = mixed[b]
        third_ref[block(b), :] = thirds[b]
    cm_ref.send()
    third_ref.send()
    ups = [mm(third, w_up[...]) + up_bias[...].astype(F32) for third in thirds]
    cots = [g[...].astype(F32) for g in (g0, g1, g2, g3)]
    feeds = [(mod[:, 5 * width :] * cot).astype(BF) for cot in cots]
    hiddens = [mm(feed, w_down[...]) for feed in feeds]
    gups = []
    for b in BLOCKS:
        v = ups[b]
        t = jnp.tanh(0.7978845608028654 * (v + 0.044715 * v * v * v))
        hidden_ref[block(b), :] = (0.5 * v * (1.0 + t)).astype(BF)
        slope = 0.5 * (1.0 + t) + 0.5 * v * (1.0 - t * t) * (0.7978845608028654 * (1.0 + 0.134145 * v * v))
        gups.append((hiddens[b] * slope).astype(BF))
        gup_ref[block(b), :] = gups[b]
        gfeed_ref[block(b), :] = feeds[b]
    for ref in (hidden_ref, gup_ref, gfeed_ref):
        ref.send()
    gthirds = [mm(gup, w_up[...], 1, 1) for gup in gups]
    gas = [normback(*norms[b], scale * gthirds[b]) for b in BLOCKS]
    gas[0] = gas[0] + cots[0]
    lows = [ga.astype(BF) for ga in gas]
    for b in BLOCKS:
        ga_ref[block(b), :] = lows[b]
    ga_ref.send()
    for b in BLOCKS:
        chunks = chunks_by_head(mm(lows[b], w_cross, 1, 1).astype(BF), h)
        for j, (ref, chunk) in enumerate(zip((c0, c1, c2, c3), chunks)):
            pack(ref, b ^ j, chunk)

    def over_rows(values):
        return sum(jnp.sum(v, axis=0, keepdims=True) for v in values)

    vec_ref[...] = jnp.concatenate(
        [
            over_rows(gthirds),
            over_rows([gthirds[b] * norms[b][0] for b in BLOCKS]),
            over_rows(gas),
            over_rows([gup.astype(F32) for gup in gups]),
            over_rows([feeds[0].astype(F32)]),
            jnp.zeros((3, width), F32),
        ],
        axis=0,
    )


def cross_back(
    head, a0, a1, a2, cm, inv, pair, cq, p, w_later, ga, after, gain, mod, proj, wout,
    dq_ref, dpair_ref, gas_ref, gproj_ref, c0, c1, c2, c3, vec_ref, ds_ref,
):
    h = head[0]
    width = after.shape[1]
    hw = cq.shape[1]
    grads = [sum(unpack(a, b).astype(F32) for a in (a0, a1, a2)) for b in BLOCKS]
    results = [unpack(cm, b) for b in BLOCKS]
    dqs, dk, dv = softmax_back(pair[0], pair[1], cq[...], p, inv, results, grads, ds_ref)
    dpair_ref[0] = dk
    dpair_ref[1] = dv
    for b in BLOCKS:
        dq_ref[block(b), :] = dqs[b]
    gseconds = [mm(dq, w_later[:, :hw], 1, 1) for dq in dqs]
    norms = [stats(after[block(b), :]) for b in BLOCKS]
    gas = [ga[block(b), :].astype(F32) + normback(*norms[b], gain[...] * gseconds[b]) for b in BLOCKS]
    gprojs = [(mod[:, 2 * width : 3 * width] * v).astype(BF) for v in gas]
    for b in BLOCKS:
        gas_ref[block(b), :] = gas[b].astype(BF)
        gproj_ref[block(b), :] = gprojs[b]
    gas_ref.send()
    gproj_ref.send()
    for b in BLOCKS:
        chunks = chunks_by_head(mm(gprojs[b], wout[...], 1, 1).astype(BF), h)
        for j, (ref, chunk) in enumerate(zip((c0, c1, c2, c3), chunks)):
            pack(ref, b ^ j, chunk)

    def over_rows(values):
        return sum(jnp.sum(v, axis=0, keepdims=True) for v in values)

    vec_ref[...] = jnp.concatenate(
        [
            over_rows([gas[b] * proj[block(b), :].astype(F32) for b in BLOCKS]),
            over_rows([gseconds[b] * norms[b][0] for b in BLOCKS]),
            over_rows([gproj.astype(F32) for gproj in gprojs]),
            jnp.zeros((5, width), F32),
        ],
        axis=0,
    )


def self_back(
    place, a0, a1, a2, sm, inv, qkv, p, n_one, w, mod, vec_c, vec_d, gate, grads_ref, near_ref, far_ref, vec_ref, ds_ref, whole_ref,
    *, kr,
):
    hw = qkv.shape[2]
    width = w.shape[0]
    grads = [sum(unpack(a, b).astype(F32) for a in (a0, a1, a2)) for b in BLOCKS]
    results = [unpack(sm, b) for b in BLOCKS]
    dqs, dk, dv = softmax_back(qkv[1], qkv[2], qkv[0], p, inv, results, grads, ds_ref)
    joint = jnp.concatenate([jnp.concatenate(dqs, axis=0), dk, dv], axis=1)
    grads_ref[...] = joint
    grads_ref.send()
    product = mm(n_one[...], joint, 0, 0)
    sums = jnp.sum(joint.astype(F32), axis=0, keepdims=True)
    weights = w[...].astype(F32)
    grad = (1.0 + mod[:, width : 2 * width]).T * product + mod[:, :width].T * sums
    empty = jnp.zeros((width, near_ref.shape[-1] - 3 * hw), BF)
    whole_ref[...] = jnp.concatenate([grad.astype(BF), empty], axis=1)
    part_rows(whole_ref, place, near_ref, far_ref, kr)
    shift_one = jnp.sum(weights * sums, axis=1, keepdims=True).T
    scale_one = jnp.sum(weights * product, axis=1, keepdims=True).T
    rows = [shift_one, scale_one, vec_d[0:1], vec_c[0:1], vec_c[1:2], gate[...], vec_d[2:3], vec_d[1:2]]
    rows += [vec_c[2:3], vec_c[4:5], vec_c[3:4], jnp.zeros((5, width), F32)]
    vec_ref[...] = jnp.concatenate(rows, axis=0)


def out_rows(place, o0, o1, o2, near_ref, far_ref, cap_ref, whole_ref, *, kr):
    hw = o0.shape[1] // 4
    rows = o0.shape[0]
    total = sum(o[...].astype(F32) for o in (o0, o1, o2))
    cap_ref[0] = total[:, 3 * hw :]
    low = total[:, : 3 * hw].astype(BF)
    for k in range(3):
        whole_ref[block(k, rows), :] = low[:, k * hw : (k + 1) * hw]
    part_rows(whole_ref, place, near_ref, far_ref, kr, out_third=kr // 3)


def first_back(x0, x1, x2, x3, grads, w, mod, gas, *frame_refs):
    width = x0.shape[1]
    weights = w[:, w.shape[1] - grads.shape[1] :]
    gfirsts = [mm(grads[block(b), :], weights, 1, 1) for b in BLOCKS]
    scale = 1.0 + mod[:, width : 2 * width]
    for b, x in enumerate((x0, x1, x2, x3)):
        ga = normback(*stats(x[...].astype(F32)), scale * gfirsts[b])
        frame_refs[b][...] = (gas[block(b), :].astype(F32) + ga).astype(BF)


def own_columns(head, *refs, hw):
    sources, target = refs[:-1], refs[-1]
    t = 0
    for ref in sources:
        for base in range(0, ref.shape[1], 4 * hw):
            part = pick([ref[:, base + a * hw : base + (a + 1) * hw] for a in range(4)], head[0])
            if len(target.shape) == 2:
                target[:, t * hw : (t + 1) * hw] = part
            else:
                for d in range(target.shape[0]):
                    target[d, :, t * hw : (t + 1) * hw] = part
            t += 1


def feed_weights(head, cm, ga, hidden, w_down, third, gup, gfeed, c0, c1, c2, c3, both_ref):
    width = ga.shape[1]
    hw = width // 4
    rows = hidden.shape[0] // 4
    chunks = chunks_by_head(mm(cm[...], ga[...], 0, 0).astype(BF), head[0])
    for j, ref in enumerate((c0, c1, c2, c3)):
        ref[:, :width] = mm(hidden[block(j, rows), :], w_down[...], 1, 1).astype(BF)
        for k in range(3):
            ref[:, width + k * hw : width + (k + 1) * hw] = chunks[j][k * rows : (k + 1) * rows]
        ref[:, width + 3 * hw :] = jnp.zeros((rows, ref.shape[1] - width - 3 * hw), BF)
        ref.send()
    both_ref[:, : gup.shape[1]] = mm(third[...], gup[...], 0, 0).astype(BF)
    both_ref[:, gup.shape[1] :] = mm(gfeed[...], hidden[...], 0, 0).astype(BF)


def part_rows(value, place, near_ref, far_ref, kr, out_third=0):
    if kr % 16:
        near_ref[...] = value[...]
        far_ref[...] = value[...]
        return
    for j in range(near_ref.shape[0]):
        first = ((place[1] >> 1) ^ j) * 2
        for ref, index in ((near_ref, first + (place[1] & 1)), (far_ref, first + 1 - (place[1] & 1))):
            block_rows = value[pl.ds(pl.multiple_of(index * kr, kr), kr), :]
            if out_third:
                hw = block_rows.shape[1]
                for k in range(3):
                    ref[j, :, k * hw : (k + 1) * hw] = block_rows[k * out_third : (k + 1) * out_third]
                ref[j, :, 3 * hw :] = jnp.zeros((out_third, ref.shape[2] - 3 * hw), BF)
            else:
                ref[j] = block_rows


def mid_weights(
    place, f0, f1, f2, across, cot, mod, dn_bias, sm, gproj, caption, dpair, w_later, second, dq,
    near_ref, far_ref, c0, c1, c2, c3, output_ref, gate_ref, whole_ref, *, kr,
):
    hw, width = dq.shape[1], sm.shape[1]
    rows = f0.shape[0]
    total = sum(f[...].astype(F32) for f in (f0, f1, f2))
    feed = total[:, :width] + dn_bias[...]
    output_ref[...] = (across[...] + mod[:, 5 * width :] * feed).astype(BF)
    gate_ref[...] = jnp.sum(cot[...].astype(F32) * feed, axis=0, keepdims=True)
    out_chunks = chunks_by_head(mm(sm[...], gproj[...], 0, 0).astype(BF), place[0])
    cap = mm(dpair[0], w_later[:, hw : 2 * hw], 1, 1) + mm(dpair[1], w_later[:, 2 * hw :], 1, 1)
    cap_chunks = chunks_by_head(cap.astype(BF), place[0])
    for ref, out_chunk, cap_chunk in zip((c0, c1, c2, c3), out_chunks, cap_chunks):
        for k in range(3):
            ref[:, k * hw : (k + 1) * hw] = out_chunk[k * rows : (k + 1) * rows]
        ref[:, 3 * hw :] = cap_chunk
    low = total[:, width:].astype(BF)
    cross = jnp.concatenate([low[:, k * hw : (k + 1) * hw] for k in range(3)], axis=0)
    parts = [mm(second[...], dq[...], 0, 0)] + [mm(caption[...], dpair[t], 0, 0) for t in range(2)]
    whole_ref[...] = jnp.concatenate([cross] + [p.astype(BF) for p in parts], axis=1)
    part_rows(whole_ref, place, near_ref, far_ref, kr)


def column_chunks(head, mid, last, third_rows, *refs):
    own = refs[0].shape[0]
    hw = mid.shape[1] // 4
    kr = 4 * own

    outs = third_rows[...]
    if outs.shape[1] > hw:
        outs = jnp.concatenate([outs[:, k * hw : (k + 1) * hw] for k in range(3)], axis=0)
    value = jnp.concatenate([mid[...], outs, last[:kr, : 3 * hw]], axis=1)
    for j, ref in enumerate(refs):
        ref[...] = pick([value[a * own : (a + 1) * own] for a in range(4)], head[0] ^ j).astype(BF)


def spread_columns(head, p0, p1, p2, p3, cross_ref, query_ref, pair_ref, out_ref, self_ref):
    hw = p0.shape[1] // 8
    got = [p[...].astype(F32) for p in (p0, p1, p2, p3)]
    for a in range(4):
        rows = pick(got, head[0] ^ a)
        for t, (ref, base) in enumerate(
            ((cross_ref, 0), (query_ref, 0), (pair_ref, 0), (pair_ref, 4), (out_ref, 0), (self_ref, 0), (self_ref, 4), (self_ref, 8))
        ):
            ref[:, (base + a) * hw : (base + a + 1) * hw] = rows[:, t * hw : (t + 1) * hw]


def on_device(
    frames,
    condition,
    captions,
    caption_lengths,
    modulation_weight,
    modulation_bias,
    self_weight,
    self_out,
    self_bias,
    cross_gain,
    cross_query,
    cross_pair,
    cross_out,
    cross_bias,
    up_weight,
    up_bias,
    down_weight,
    down_bias,
    cotangent,
):
    n = lax.axis_size("seq")
    h = lax.axis_index("head")
    s = lax.axis_index("seq")
    rows, width = frames.shape
    hw = width // 4
    kr = self_weight.shape[0]
    own = kr // 4
    total = rows * 4

    ff = up_weight.shape[1]
    head = h.astype(jnp.int32)[None]

    def columns(weights, shape):
        return call(partial(own_columns, hw=hw), [head], weights, [out(shape, BF)])[0]

    w_own = columns((self_out, cross_out, self_weight), (kr, 5 * hw))
    condition, w_own, later = lax.optimization_barrier((condition, w_own, (cross_query, cross_pair)))
    w_later = columns(later, (n, kr, 3 * hw))
    w_own = lax.all_gather(w_own, "seq", axis=0, tiled=True)
    x = head_rel(frames)
    biases = jnp.concatenate([self_bias, cross_bias, cross_gain, down_bias])[None]
    got = exchange(jnp.concatenate([condition.reshape(n, kr), jnp.broadcast_to(biases, (n, 4 * kr))], axis=1))
    cond_own = jax.nn.silu(got[:, :kr].astype(F32)).astype(BF)
    vectors = got[:, kr:].astype(F32).reshape(n, 4, kr).transpose(1, 0, 2).reshape(4, width)
    out_bias, co_bias, gain, dn_bias = vectors[0], vectors[1], vectors[2], vectors[3]
    mod_part = mm(cond_own, modulation_weight) + lax.dynamic_update_slice(
        jnp.zeros((n * modulation_bias.shape[0],), F32),
        modulation_bias.astype(F32),
        (s * modulation_bias.shape[0],),
    )
    g = head_rel(cotangent)
    mod_part, x = lax.optimization_barrier((mod_part, x))
    mod = exchange(mod_part).sum(0, keepdims=True)
    w_own = after(w_own, (mod, w_later, g))
    updown = after((up_weight, down_weight), (mod, g))
    updown = jnp.concatenate([updown[0], updown[1].T], axis=1)
    updown = lax.all_gather(updown, "seq", axis=0, tiled=True)
    w_up = (updown, (slice(None), slice(0, ff)))
    w_down = (updown, (slice(None), slice(ff, 2 * ff)))
    w_later = exchange(after(w_later, mod)).reshape(width, 3 * hw)
    w_parts = w_own[:, : 2 * hw]
    mod, w_parts = lax.optimization_barrier((mod, w_parts))
    w_parts = head_rel(w_parts)
    caption = captions[0]
    slots = caption.shape[0]
    heads = hw // HD
    packed = (total // 2, 2 * hw)
    pad = -3 * hw % 128
    deep = out((total, width), BF)
    n_one, qkv, sm_own, probs, inv = call(
        self_forward,
        [],
        [*x, mod, w_own],
        [deep, out((3, total, hw), BF), out(packed, BF), out((heads, total, total), BF), out((heads, total), F32)],
        sends=4,
    )
    sm_parts = head_rel(sm_own)
    sm, w_out, proj, after_self, second, cq, pair, cm_own, cprobs, cinv = call(
        cross_forward,
        [head, caption_lengths],
        [*x, *w_parts, *sm_parts, mod, out_bias[None], gain[None], w_later, caption],
        [
            deep,
            out((width, width), BF),
            deep,
            out((total, width), F32),
            deep,
            out((total, hw), BF),
            out((2, slots, hw), BF),
            out(packed, BF),
            out((heads, slots, total), BF),
            out((heads, total), F32),
        ],
        sends=4,
    )
    cm_parts = head_rel(cm_own)
    cm, w_cross, across, third, hidden, g_up, g_feed, ga, *chunks, vec_c = call(
        feed_both,
        [head],
        [cm_parts[0], *w_parts, *cm_parts[1:], after_self, co_bias[None], mod]
        + [w_up, up_bias[None], w_down, *g],
        [deep, out((width, width), BF), out((rows, width), F32), deep]
        + [out((total, ff), BF), out((total, ff), BF), deep, deep]
        + [out(packed, BF) for _ in range(4)]
        + [out((8, width), F32)],
    )

    def near_terms(chunks):
        a, b = swap(chunks[1], 1), swap(chunks[3], 1)
        return chunks[0], a, (chunks[2].astype(F32) + b.astype(F32)).astype(BF)

    mine, near, other = near_terms(chunks)
    far = swap(other, 2)
    place = jnp.stack([h, s]).astype(jnp.int32)

    def halves(columns):
        shape = (width, columns) if kr % 16 else (n // 2, kr, columns)
        return [out(shape, BF) for _ in range(2)]

    def parted(near_rows, far_rows):
        if kr % 16 == 0:
            return near_rows, far_rows
        v = near_rows.reshape(n, kr, -1)
        for bit in (1 << b for b in range(n.bit_length() - 1)):
            pairs = v.reshape(n // (2 * bit), 2, bit, kr, -1)
            v = jnp.where((s & bit) != 0, pairs[:, ::-1], pairs).reshape(n, kr, -1)
        return v[0::2], v[1::2]

    *feed_chunks, both = call(
        feed_weights,
        [head],
        [after(cm, other), ga, hidden, w_down, third, g_up, g_feed],
        [out((rows, width + 3 * hw + pad), BF) for _ in range(4)] + [out((width, 2 * ff), BF)],
    )
    both = exchange(after(both, far).reshape(n, kr, 2 * ff))
    feed_mine, feed_near, feed_other = near_terms(after(tuple(feed_chunks), far))
    far, feed_other = lax.optimization_barrier((far, feed_other))
    feed_far = swap(feed_other, 2)
    dq, dpair, gas, g_proj, *chunks, vec_d = call(
        cross_back,
        [head],
        [mine, near, far, cm_own, cinv, pair, cq, cprobs, w_later, ga, after_self, gain[None], mod, proj, w_out],
        [out((total, hw), BF), out((2, slots, hw), BF), deep, deep]
        + [out(packed, BF) for _ in range(4)]
        + [out((8, width), F32)],
        [pltpu.VMEM((heads, slots, total), BF)],
    )
    mine, near, other = near_terms(chunks)
    other, feed_far = lax.optimization_barrier((other, feed_far))
    far = swap(other, 2)
    *mid, out0, out1, out2, out3, output_frames, gv_gate2 = call(
        partial(mid_weights, kr=kr),
        [place],
        [feed_mine, feed_near, feed_far, across, cotangent, mod, dn_bias[None]]
        + [after(sm, other), g_proj, caption, dpair, w_later, second, dq],
        halves(4 * hw)
        + [out((rows, 4 * hw), BF) for _ in range(4)]
        + [out((rows, width), BF), out((1, width), F32)],
        [pltpu.VMEM((width, 4 * hw), BF)],
    )
    out_mine, out_near, out_other = near_terms(after((out0, out1, out2, out3), far))
    far, mid, out_other = lax.optimization_barrier((far, mid, out_other))
    out_far = swap(out_other, 2)
    mid = half_reduce(*parted(*mid))
    g_joint, *last, vec = call(
        partial(self_back, kr=kr),
        [place],
        [mine, near, far, sm_own, inv, qkv, probs, n_one, (w_own, (slice(None), slice(2 * hw, 5 * hw)))]
        + [mod, vec_c, vec_d, gv_gate2],
        [out((total, 3 * hw), BF)] + halves(3 * hw + pad) + [out((16, width), F32)],
        [pltpu.VMEM((heads, total, total), BF), pltpu.VMEM((width, 3 * hw + pad), BF)],
    )
    vec, mid, both, out_far = lax.optimization_barrier((vec, mid, both, out_far))
    near_rows, far_rows = parted(*last)
    last = half_reduce(near_rows, after(far_rows, mid))
    last_y = last
    shared = vec + swap(vec, 1)
    shared = shared + swap(shared, 2)
    vec = jnp.where(jnp.arange(16)[:, None] == 10, vec, shared).astype(BF)
    mid_y = mid
    mid = rest_reduce(mid)
    third_shape = (width, hw) if kr % 16 else (n // 2, kr // 3, 3 * hw + pad)
    *outs, grad_captions = call(
        partial(out_rows, kr=kr),
        [place],
        [out_mine, out_near, out_far],
        [out(third_shape, BF) for _ in range(2)] + [out((1, slots, hw), F32)],
        [pltpu.VMEM((width, hw), BF)],
    )
    near_rows, far_rows = parted(*outs)
    if kr % 16:
        near_rows, far_rows = (
            jnp.pad(
                v.reshape(n // 2, 3, kr // 3, hw).transpose(0, 2, 1, 3).reshape(n // 2, kr // 3, 3 * hw),
                ((0, 0), (0, 0), (0, pad)),
            )
            for v in (near_rows, far_rows)
        )
    outs = half_reduce(near_rows, far_rows)
    vec = exchange(jnp.broadcast_to(after(vec, last_y)[None], (n, *vec.shape))).astype(F32)
    sent = []
    last = rest_reduce(jnp.concatenate([last, outs], axis=1), sent)
    outs = last[kr:]
    gf = call(first_back, [], [*x, g_joint, w_own, mod, after(gas, sent[-1])], [out((rows, width), BF)] * 4)
    if kr % 16:
        outs = outs[:, : 3 * hw].reshape(own * 4 // 3, 3, hw).transpose(1, 0, 2).reshape(kr, hw)
    frame_mine, frame_near, frame_other = near_terms(gf)

    g_mod = vec[:, :6].reshape(n, 6 * width)
    g_cond = lax.dot_general(
        g_mod,
        modulation_weight.astype(F32),
        (((1,), (1,)), ((), ())),
        precision=lax.Precision.HIGHEST,
        preferred_element_type=F32,
    )
    g_silu = exchange(after(g_cond, frame_other)).reshape(width)
    g_cond = jax.vjp(jax.nn.silu, condition[0].astype(F32))[1](g_silu)[0]
    grad_condition = lax.dynamic_slice_in_dim(g_cond, h * hw, hw, 0)[None]
    cond_rows = lax.dynamic_slice_in_dim(cond_own, h * own, own, 1).astype(F32)
    grad_mod_weight = lax.dot_general(
        cond_rows, g_mod, (((0,), (0,)), ((), ())), precision=lax.Precision.HIGHEST, preferred_element_type=F32
    )
    sums = vec.sum(0)
    index = s * 4 + h
    mb = 6 * width // (4 * n)
    grad_mod_bias = lax.dynamic_slice_in_dim(sums[:6].reshape(6 * width), index * mb, mb, 0)

    def own_vec(i):
        return lax.dynamic_slice_in_dim(sums[6 + i], index * own, own, 0)

    both = both.astype(F32).sum(0)
    tiny = dict(small=1 << 20, limit=8)
    cols = call(column_chunks, [head], [mid, last, outs], [out((own, 8 * hw), BF) for _ in range(4)], **tiny)
    frame_far = swap(frame_other, 2)
    grad_frames = frame_mine.astype(F32) + frame_near.astype(F32) + frame_far.astype(F32)
    cols = [cols[0]] + [
        lax.ppermute(cols[j], "head", [(i, i ^ j) for i in range(4)]) for j in range(1, 4)
    ]
    grad_cross, grad_query, grad_pair, grad_out, grad_self = call(
        spread_columns, [head], cols, [out((own, k * width), F32) for k in (1, 1, 2, 1, 3)], **tiny
    )
    return (
        output_frames,
        grad_frames,
        grad_condition,
        grad_captions,
        grad_mod_weight,
        grad_mod_bias,
        grad_self,
        grad_out,
        own_vec(0),
        own_vec(1),
        grad_query,
        grad_pair,
        grad_cross,
        own_vec(2),
        both[:, :ff],
        sums[10],
        both[:, ff:].T,
        own_vec(3),
    )


def solution(mesh):
    both = ("seq", "head")
    return jax.shard_map(
        on_device,
        mesh=mesh,
        in_specs=(
            P(both, None),
            P("seq", None),
            P("seq", None, None),
            P("seq"),
            P("seq", None),
            P("seq"),
            P("seq", None),
            P("seq", None),
            P("seq"),
            P("seq"),
            P("seq", None),
            P("seq", None),
            P("seq", None),
            P("seq"),
            P("seq", "head"),
            P("head"),
            P("head", "seq"),
            P("seq"),
            P(both, None),
        ),
        out_specs=(
            P(both, None),
            P(both, None),
            P("seq", "head"),
            P("seq", None, "head"),
            P(both, None),
            P(both),
            P(both, None),
            P(both, None),
            P(both),
            P(both),
            P(both, None),
            P(both, None),
            P(both, None),
            P(both),
            P("seq", "head"),
            P("head"),
            P("head", "seq"),
            P(both),
        ),
        check_vma=False,
    )
```

```python
from functools import partial

import jax
import jax.numpy as jnp
from jax import lax
from jax.experimental import pallas as pl
from jax.experimental.pallas import tpu as pltpu
from jax.sharding import PartitionSpec as P

HD = 64
BF = jnp.bfloat16
F32 = jnp.float32


def mm(a, b, ca=1, cb=0):
    return lax.dot_general(a, b, (((ca,), (cb,)), ((), ())), preferred_element_type=F32)


def swap(x, bit):
    return lax.ppermute(x, "head", [(i, i ^ bit) for i in range(4)])


def swap_rows(x, bit):
    blocks = jnp.split(swap(x, bit), 4, axis=0)
    return jnp.concatenate([blocks[i ^ bit] for i in range(4)], axis=0)


def head_rel(x, swap=swap):
    near = swap(x, 1)
    far = swap(x, 2)
    return [x, near, far, swap(far, 1)]


def pick(parts, index):
    low, high = (index & 1) == 1, (index & 2) == 2
    return jnp.where(
        high, jnp.where(low, parts[3], parts[2]), jnp.where(low, parts[1], parts[0])
    )


def after(values, ready):
    return lax.optimization_barrier((values, ready))[0]


def seq_swap(x, bit):
    return lax.ppermute(x, "seq", [(i, i ^ bit) for i in range(lax.axis_size("seq"))])


def exchange(x):
    return lax.all_to_all(x, "seq", split_axis=0, concat_axis=0, tiled=True)


def half_reduce(near, far):
    return (near.astype(F32) + seq_swap(far, 1).astype(F32)).astype(BF)


def rest_reduce(x, sent=None):
    x, bit = x.astype(F32), 2
    while x.shape[0] > 1:
        send = x[1::2].astype(BF)
        if sent is not None:
            sent.append(send)
        x, bit = x[0::2] + seq_swap(send, bit).astype(F32), 2 * bit
    return x[0]


def stats(v):
    mean = jnp.mean(v, axis=-1, keepdims=True)
    center = v - mean
    r = lax.rsqrt(jnp.mean(center * center, axis=-1, keepdims=True) + 1e-6)
    return center * r, r


def normback(n, r, e):
    return r * (
        e - jnp.mean(e, axis=-1, keepdims=True) - n * jnp.mean(e * n, axis=-1, keepdims=True)
    )


class Held:
    def __init__(self, outside, inside, sems, count):
        self.outside, self.inside, self.sems, self.count = outside, inside, sems, count
        self.pending = []
        self.shape, self.dtype = inside.shape, inside.dtype

    def copy(self, source, target):
        copy = pltpu.make_async_copy(source, target, self.sems.at[self.count[0]])
        self.count[0] += 1
        copy.start()
        self.pending.append(copy)

    def send(self, at=...):
        if self.outside is not None:
            self.copy(self.inside.at[at], self.outside.at[at])

    def wait(self):
        for copy in self.pending:
            copy.wait()
        self.pending = []

    def __getitem__(self, at):
        self.wait()
        return self.inside[at]

    def __setitem__(self, at, value):
        self.inside[at] = value


class Result(Held):
    def __getitem__(self, at):
        return self.inside[at]


def call(kernel, scalars, ins, outs, scratch=(), sends=0, small=0, limit=58):
    ins = [v if isinstance(v, tuple) else (v, ...) for v in ins]
    parts = [v if at is ... else jax.eval_shape(lambda x, at=at: x[at], v) for v, at in ins]

    def is_small(v):
        return v.size * v.dtype.itemsize <= small

    plain = [is_small(v) and at is ... for v, at in ins] + [is_small(v) for v in outs]
    kept = [v for v, p in zip((*parts, *outs), plain) if not p]

    def body(*refs):
        refs = list(refs)
        numbers = [refs.pop(0) for _ in scalars]
        outside = [refs.pop(0) for _ in plain]
        inside = [refs.pop(0) for _ in kept]
        sems, rest, count = refs[-1], refs[:-1], [0]
        arrays = []
        for k, (ref, p) in enumerate(zip(outside, plain)):
            kind = Held if k < len(ins) else Result
            arrays.append(kind(None, ref, sems, count) if p else kind(ref, inside.pop(0), sems, count))
        held, results = arrays[: len(ins)], arrays[len(ins) :]
        for v, (_, at) in zip(held, ins):
            if v.outside is not None:
                v.copy(v.outside.at[at], v.inside)
        kernel(*numbers, *held, *results, *rest)
        for v in results:
            if not v.pending:
                v.send()
        for v in arrays:
            v.wait()

    specs = [pl.BlockSpec(memory_space=pltpu.VMEM if p else pl.ANY) for p in plain]
    return pl.pallas_call(
        body,
        in_specs=[pl.BlockSpec(memory_space=pltpu.SMEM)] * len(scalars) + specs[: len(ins)],
        out_specs=specs[len(ins) :],
        out_shape=list(outs),
        scratch_shapes=[pltpu.VMEM(v.shape, v.dtype) for v in kept]
        + list(scratch)
        + [pltpu.SemaphoreType.DMA((len(kept) + sends + 1,))],
        compiler_params=pltpu.CompilerParams(vmem_limit_bytes=limit * 1024 * 1024),
    )(*scalars, *[v for v, _ in ins])


def out(shape, dtype):
    return jax.ShapeDtypeStruct(shape, dtype)


def block(b, size=256):
    return slice(b * size, (b + 1) * size)


def packed_at(shape, b):
    size, half = shape[0] // 2, shape[1] // 2
    return (block(b // 2, size), slice(half * (b % 2), half * (b % 2 + 1)))


def unpack(ref, b):
    return ref[packed_at(ref.shape, b)]


def pack(ref, b, value):
    ref[packed_at(ref.shape, b)] = value


def by_head(parts, head):
    return jnp.concatenate([pick(parts, head ^ a) for a in range(4)], axis=1)


def chunks_by_head(value, head):
    hw = value.shape[1] // 4
    blocks = [value[:, a * hw : (a + 1) * hw] for a in range(4)]
    return [pick(blocks, head ^ j) for j in range(4)]


def staggered(stages, tasks):
    done = [None] * len(tasks)
    for t in range(len(tasks) + len(stages) - 1):
        for k, stage in enumerate(stages):
            if 0 <= t - k < len(tasks):
                done[t - k] = stage(*tasks[t - k]) if k == 0 else stage(*tasks[t - k], done[t - k])
    return done


def of_head(values, hd):
    lane = lax.broadcasted_iota(jnp.int32, (1, values.shape[1]), 1) // HD
    return jnp.where(lane == hd, values, 0)


def softmax_columns(keys, queries, values_t, p_ref, inv_ref, visible=None):
    heads = keys.shape[1] // HD
    own_keys = [of_head(keys, hd) for hd in range(heads)]

    def scores(b, hd):
        return mm(own_keys[hd], queries[b], 1, 1)

    def weights(b, hd, st):
        if visible is not None:
            st = jnp.where(visible, st, -1e30)
        e = jnp.exp(st - jnp.max(st, axis=0, keepdims=True))
        inv = 1.0 / jnp.sum(e, axis=0, keepdims=True)
        low = e.astype(BF)
        p_ref[hd, :, block(b)] = low
        inv_ref[hd : hd + 1, block(b)] = inv
        return low, inv

    def mixed(b, hd, done):
        result = mm(values_t[hd * HD : (hd + 1) * HD, :], done[0]) * done[1]
        if hd == heads - 1:
            p_ref.send((slice(None), slice(None), block(b)))
        return result

    parts = staggered((scores, weights, mixed), [(b, hd) for b in range(len(queries)) for hd in range(heads)])
    return [
        jnp.concatenate(parts[b * heads : (b + 1) * heads], axis=0).T.astype(BF) for b in range(len(queries))
    ]


def softmax_back(keys, values, queries, p_ref, inv_ref, results, grads, ds_ref):
    heads = keys.shape[1] // HD
    keys_t = keys.astype(F32).T.astype(BF)
    own_values = [of_head(values, hd) for hd in range(heads)]
    count = len(grads)
    scaled, inner = [], []
    for b in range(count):
        go_t, o_t = grads[b].T, results[b].astype(F32).T
        parts = []
        for hd in range(heads):
            at = slice(hd * HD, (hd + 1) * HD)
            parts.append(go_t[at, :] * inv_ref[hd : hd + 1, block(b)])
            inner.append(jnp.sum(parts[-1] * o_t[at, :], axis=0, keepdims=True))
        scaled.append(jnp.concatenate(parts, axis=0).T.astype(BF))

    def dprob(b, hd):
        return mm(own_values[hd], scaled[b], 1, 1)

    def dscore(b, hd, dp):
        ds = (p_ref[hd, :, block(b)].astype(F32) * (dp - inner[b * heads + hd])).astype(BF)
        ds_ref[hd, :, block(b)] = ds
        return ds

    def dquery(b, hd, ds):
        return mm(keys_t[hd * HD : (hd + 1) * HD, :], ds)

    parts = staggered((dprob, dscore, dquery), [(b, hd) for b in range(count) for hd in range(heads)])
    dq = [
        (jnp.concatenate(parts[b * heads : (b + 1) * heads], axis=0).T * 0.125).astype(BF) for b in range(count)
    ]
    everything = jnp.concatenate(scaled, axis=0)
    dk = sum(of_head(mm(ds_ref[hd], queries), hd) for hd in range(heads))
    dv = sum(of_head(mm(p_ref[hd], everything), hd) for hd in range(heads))
    return dq, dk.astype(BF), dv.astype(BF)


BLOCKS = range(4)


def self_forward(x0, x1, x2, x3, mod, w, n_ref, qkv_ref, sm_ref, p_ref, inv_ref):
    width = x0.shape[1]
    hw = sm_ref.shape[1] // 2
    norms = [stats(x[...].astype(F32))[0] for x in (x0, x1, x2, x3)]
    scale, shift = 1.0 + mod[:, width : 2 * width], mod[:, :width]
    firsts = [(n * scale + shift).astype(BF) for n in norms]
    weights = w[:, 2 * hw :]
    joints = [mm(first, weights) for first in firsts]
    for b in BLOCKS:
        n_ref[block(b), :] = norms[b].astype(BF)
    n_ref.send()
    queries = [(joint[:, :hw] * 0.125).astype(BF) for joint in joints]
    keys = jnp.concatenate([joint[:, hw : 2 * hw].astype(BF) for joint in joints], axis=0)
    for b in BLOCKS:
        qkv_ref[0, block(b), :] = queries[b]
        qkv_ref[2, block(b), :] = joints[b][:, 2 * hw :].astype(BF)
    qkv_ref[1] = keys
    qkv_ref.send()
    values_t = jnp.concatenate([joint[:, 2 * hw :].T.astype(BF) for joint in joints], axis=1)
    for b, result in enumerate(softmax_columns(keys, queries, values_t, p_ref, inv_ref)):
        pack(sm_ref, b, result)


def cross_forward(
    head, length, x0, x1, x2, x3, w0, w1, w2, w3, sm0, sm1, sm2, sm3, mod, out_bias, gain, w_later, caption,
    sm_ref, wout_ref, proj_ref, after_ref, second_ref, cq_ref, pair_ref, cm_ref, p_ref, inv_ref,
):
    h = head[0]
    width = x0.shape[1]
    hw = cq_ref.shape[1]
    w_out = by_head([w[:, :hw] for w in (w0, w1, w2, w3)], h)
    wout_ref[...] = w_out
    wout_ref.send()
    mixed = [by_head([unpack(p, b ^ j) for j, p in enumerate((sm0, sm1, sm2, sm3))], h) for b in BLOCKS]
    projs = [mm(m, w_out) + out_bias[...] for m in mixed]
    pair = mm(caption[...], w_later[:, hw:])
    keys, values = pair[:, :hw].astype(BF), pair[:, hw:]
    pair_ref[0] = keys
    pair_ref[1] = values.astype(BF)
    afters, seconds = [], []
    for b, x in enumerate((x0, x1, x2, x3)):
        sm_ref[block(b), :] = mixed[b]
        proj_ref[block(b), :] = projs[b].astype(BF)
        after = x[...].astype(F32) + mod[:, 2 * width : 3 * width] * projs[b]
        after_ref[block(b), :] = after
        seconds.append((stats(after)[0] * gain[...]).astype(BF))
        second_ref[block(b), :] = seconds[b]
    for ref in (sm_ref, proj_ref, after_ref, second_ref):
        ref.send()
    queries = [(mm(second, w_later[:, :hw]) * 0.125).astype(BF) for second in seconds]
    for b in BLOCKS:
        cq_ref[block(b), :] = queries[b]
    slots = lax.broadcasted_iota(jnp.int32, (caption.shape[0], 1), 0)
    results = softmax_columns(keys, queries, values.T.astype(BF), p_ref, inv_ref, slots < length[0])
    for b, result in enumerate(results):
        pack(cm_ref, b, result)


def feed_both(
    head, cm0, w0, w1, w2, w3, cm1, cm2, cm3, after, co_bias, mod, w_up, up_bias, w_down, g0, g1, g2, g3,
    cm_ref, wc_ref, across_ref, third_ref, hidden_ref, gup_ref, gfeed_ref, ga_ref, c0, c1, c2, c3, vec_ref,
):
    h = head[0]
    width = after.shape[1]
    hw = width // 4
    ff = w_up.shape[1]
    w_cross = by_head([w[:, hw:] for w in (w0, w1, w2, w3)], h)
    wc_ref[...] = w_cross
    wc_ref.send()
    mixed = [by_head([unpack(p, b ^ j) for j, p in enumerate((cm0, cm1, cm2, cm3))], h) for b in BLOCKS]
    across = [after[block(b), :] + mm(mixed[b], w_cross) + co_bias[...] for b in BLOCKS]
    across_ref[...] = across[0]
    across_ref.send()
    scale, shift = 1.0 + mod[:, 4 * width : 5 * width], mod[:, 3 * width : 4 * width]
    norms = [stats(v) for v in across]
    thirds = [(n * scale + shift).astype(BF) for n, _ in norms]
    for b in BLOCKS:
        cm_ref[block(b), :] = mixed[b]
        third_ref[block(b), :] = thirds[b]
    cm_ref.send()
    third_ref.send()
    ups = [mm(third, w_up[...]) + up_bias[...].astype(F32) for third in thirds]
    cots = [g[...].astype(F32) for g in (g0, g1, g2, g3)]
    feeds = [(mod[:, 5 * width :] * cot).astype(BF) for cot in cots]
    hiddens = [mm(feed, w_down[...]) for feed in feeds]
    gups = []
    for b in BLOCKS:
        v = ups[b]
        t = jnp.tanh(0.7978845608028654 * (v + 0.044715 * v * v * v))
        hidden_ref[block(b), :] = (0.5 * v * (1.0 + t)).astype(BF)
        slope = 0.5 * (1.0 + t) + 0.5 * v * (1.0 - t * t) * (0.7978845608028654 * (1.0 + 0.134145 * v * v))
        gups.append((hiddens[b] * slope).astype(BF))
        gup_ref[block(b), :] = gups[b]
        gfeed_ref[block(b), :] = feeds[b]
    for ref in (hidden_ref, gup_ref, gfeed_ref):
        ref.send()
    gthirds = [mm(gup, w_up[...], 1, 1) for gup in gups]
    gas = [normback(*norms[b], scale * gthirds[b]) for b in BLOCKS]
    gas[0] = gas[0] + cots[0]
    lows = [ga.astype(BF) for ga in gas]
    for b in BLOCKS:
        ga_ref[block(b), :] = lows[b]
    ga_ref.send()
    for b in BLOCKS:
        chunks = chunks_by_head(mm(lows[b], w_cross, 1, 1).astype(BF), h)
        for j, (ref, chunk) in enumerate(zip((c0, c1, c2, c3), chunks)):
            pack(ref, b ^ j, chunk)

    def over_rows(values):
        return sum(jnp.sum(v, axis=0, keepdims=True) for v in values)

    vec_ref[...] = jnp.concatenate(
        [
            over_rows(gthirds),
            over_rows([gthirds[b] * norms[b][0] for b in BLOCKS]),
            over_rows(gas),
            over_rows([gup.astype(F32) for gup in gups]),
            over_rows([feeds[0].astype(F32)]),
            jnp.zeros((3, width), F32),
        ],
        axis=0,
    )


def cross_back(
    head, a0, a1, a2, cm, inv, pair, cq, p, w_later, ga, after, gain, mod, proj, wout,
    dq_ref, dpair_ref, gas_ref, gproj_ref, c0, c1, c2, c3, vec_ref, ds_ref,
):
    h = head[0]
    width = after.shape[1]
    hw = cq.shape[1]
    grads = [sum(unpack(a, b).astype(F32) for a in (a0, a1, a2)) for b in BLOCKS]
    results = [unpack(cm, b) for b in BLOCKS]
    dqs, dk, dv = softmax_back(pair[0], pair[1], cq[...], p, inv, results, grads, ds_ref)
    dpair_ref[0] = dk
    dpair_ref[1] = dv
    for b in BLOCKS:
        dq_ref[block(b), :] = dqs[b]
    gseconds = [mm(dq, w_later[:, :hw], 1, 1) for dq in dqs]
    norms = [stats(after[block(b), :]) for b in BLOCKS]
    gas = [ga[block(b), :].astype(F32) + normback(*norms[b], gain[...] * gseconds[b]) for b in BLOCKS]
    gprojs = [(mod[:, 2 * width : 3 * width] * v).astype(BF) for v in gas]
    for b in BLOCKS:
        gas_ref[block(b), :] = gas[b].astype(BF)
        gproj_ref[block(b), :] = gprojs[b]
    gas_ref.send()
    gproj_ref.send()
    for b in BLOCKS:
        chunks = chunks_by_head(mm(gprojs[b], wout[...], 1, 1).astype(BF), h)
        for j, (ref, chunk) in enumerate(zip((c0, c1, c2, c3), chunks)):
            pack(ref, b ^ j, chunk)

    def over_rows(values):
        return sum(jnp.sum(v, axis=0, keepdims=True) for v in values)

    vec_ref[...] = jnp.concatenate(
        [
            over_rows([gas[b] * proj[block(b), :].astype(F32) for b in BLOCKS]),
            over_rows([gseconds[b] * norms[b][0] for b in BLOCKS]),
            over_rows([gproj.astype(F32) for gproj in gprojs]),
            jnp.zeros((5, width), F32),
        ],
        axis=0,
    )


def self_back(
    place, a0, a1, a2, sm, inv, qkv, p, n_one, w, mod, vec_c, vec_d, gate, grads_ref, near_ref, far_ref, vec_ref, ds_ref, whole_ref,
    *, kr,
):
    hw = qkv.shape[2]
    width = w.shape[0]
    grads = [sum(unpack(a, b).astype(F32) for a in (a0, a1, a2)) for b in BLOCKS]
    results = [unpack(sm, b) for b in BLOCKS]
    dqs, dk, dv = softmax_back(qkv[1], qkv[2], qkv[0], p, inv, results, grads, ds_ref)
    joint = jnp.concatenate([jnp.concatenate(dqs, axis=0), dk, dv], axis=1)
    grads_ref[...] = joint
    grads_ref.send()
    product = mm(n_one[...], joint, 0, 0)
    sums = jnp.sum(joint.astype(F32), axis=0, keepdims=True)
    weights = w[...].astype(F32)
    grad = (1.0 + mod[:, width : 2 * width]).T * product + mod[:, :width].T * sums
    empty = jnp.zeros((width, near_ref.shape[-1] - 3 * hw), BF)
    whole_ref[...] = jnp.concatenate([grad.astype(BF), empty], axis=1)
    part_rows(whole_ref, place, near_ref, far_ref, kr)
    shift_one = jnp.sum(weights * sums, axis=1, keepdims=True).T
    scale_one = jnp.sum(weights * product, axis=1, keepdims=True).T
    rows = [shift_one, scale_one, vec_d[0:1], vec_c[0:1], vec_c[1:2], gate[...], vec_d[2:3], vec_d[1:2]]
    rows += [vec_c[2:3], vec_c[4:5], vec_c[3:4], jnp.zeros((5, width), F32)]
    vec_ref[...] = jnp.concatenate(rows, axis=0)


def out_rows(place, o0, o1, o2, near_ref, far_ref, cap_ref, whole_ref, *, kr):
    hw = o0.shape[1] // 4
    rows = o0.shape[0]
    total = sum(o[...].astype(F32) for o in (o0, o1, o2))
    cap_ref[0] = total[:, 3 * hw :]
    low = total[:, : 3 * hw].astype(BF)
    for k in range(3):
        whole_ref[block(k, rows), :] = low[:, k * hw : (k + 1) * hw]
    part_rows(whole_ref, place, near_ref, far_ref, kr, out_third=kr // 3)


def first_back(x0, x1, x2, x3, grads, w, mod, gas, *frame_refs):
    width = x0.shape[1]
    weights = w[:, w.shape[1] - grads.shape[1] :]
    gfirsts = [mm(grads[block(b), :], weights, 1, 1) for b in BLOCKS]
    scale = 1.0 + mod[:, width : 2 * width]
    for b, x in enumerate((x0, x1, x2, x3)):
        ga = normback(*stats(x[...].astype(F32)), scale * gfirsts[b])
        frame_refs[b][...] = (gas[block(b), :].astype(F32) + ga).astype(BF)


def own_columns(head, *refs, hw):
    sources, target = refs[:-1], refs[-1]
    t = 0
    for ref in sources:
        for base in range(0, ref.shape[1], 4 * hw):
            part = pick([ref[:, base + a * hw : base + (a + 1) * hw] for a in range(4)], head[0])
            if len(target.shape) == 2:
                target[:, t * hw : (t + 1) * hw] = part
            else:
                for d in range(target.shape[0]):
                    target[d, :, t * hw : (t + 1) * hw] = part
            t += 1


def feed_weights(head, cm, ga, hidden, w_down, third, gup, gfeed, c0, c1, c2, c3, both_ref):
    width = ga.shape[1]
    hw = width // 4
    rows = hidden.shape[0] // 4
    chunks = chunks_by_head(mm(cm[...], ga[...], 0, 0).astype(BF), head[0])
    for j, ref in enumerate((c0, c1, c2, c3)):
        ref[:, :width] = mm(hidden[block(j, rows), :], w_down[...], 1, 1).astype(BF)
        for k in range(3):
            ref[:, width + k * hw : width + (k + 1) * hw] = chunks[j][k * rows : (k + 1) * rows]
        ref[:, width + 3 * hw :] = jnp.zeros((rows, ref.shape[1] - width - 3 * hw), BF)
        ref.send()
    both_ref[:, : gup.shape[1]] = mm(third[...], gup[...], 0, 0).astype(BF)
    both_ref[:, gup.shape[1] :] = mm(gfeed[...], hidden[...], 0, 0).astype(BF)


def part_rows(value, place, near_ref, far_ref, kr, out_third=0):
    if kr % 16:
        near_ref[...] = value[...]
        far_ref[...] = value[...]
        return
    for j in range(near_ref.shape[0]):
        first = ((place[1] >> 1) ^ j) * 2
        for ref, index in ((near_ref, first + (place[1] & 1)), (far_ref, first + 1 - (place[1] & 1))):
            block_rows = value[pl.ds(pl.multiple_of(index * kr, kr), kr), :]
            if out_third:
                hw = block_rows.shape[1]
                for k in range(3):
                    ref[j, :, k * hw : (k + 1) * hw] = block_rows[k * out_third : (k + 1) * out_third]
                ref[j, :, 3 * hw :] = jnp.zeros((out_third, ref.shape[2] - 3 * hw), BF)
            else:
                ref[j] = block_rows


def mid_weights(
    place, f0, f1, f2, across, cot, mod, dn_bias, sm, gproj, caption, dpair, w_later, second, dq,
    near_ref, far_ref, c0, c1, c2, c3, output_ref, gate_ref, whole_ref, *, kr,
):
    hw, width = dq.shape[1], sm.shape[1]
    rows = f0.shape[0]
    total = sum(f[...].astype(F32) for f in (f0, f1, f2))
    feed = total[:, :width] + dn_bias[...]
    output_ref[...] = (across[...] + mod[:, 5 * width :] * feed).astype(BF)
    gate_ref[...] = jnp.sum(cot[...].astype(F32) * feed, axis=0, keepdims=True)
    out_chunks = chunks_by_head(mm(sm[...], gproj[...], 0, 0).astype(BF), place[0])
    cap = mm(dpair[0], w_later[:, hw : 2 * hw], 1, 1) + mm(dpair[1], w_later[:, 2 * hw :], 1, 1)
    cap_chunks = chunks_by_head(cap.astype(BF), place[0])
    for ref, out_chunk, cap_chunk in zip((c0, c1, c2, c3), out_chunks, cap_chunks):
        for k in range(3):
            ref[:, k * hw : (k + 1) * hw] = out_chunk[k * rows : (k + 1) * rows]
        ref[:, 3 * hw :] = cap_chunk
    low = total[:, width:].astype(BF)
    cross = jnp.concatenate([low[:, k * hw : (k + 1) * hw] for k in range(3)], axis=0)
    parts = [mm(second[...], dq[...], 0, 0)] + [mm(caption[...], dpair[t], 0, 0) for t in range(2)]
    whole_ref[...] = jnp.concatenate([cross] + [p.astype(BF) for p in parts], axis=1)
    part_rows(whole_ref, place, near_ref, far_ref, kr)


def column_chunks(head, mid, last, third_rows, *refs):
    own = refs[0].shape[0]
    hw = mid.shape[1] // 4
    kr = 4 * own

    outs = third_rows[...]
    if outs.shape[1] > hw:
        outs = jnp.concatenate([outs[:, k * hw : (k + 1) * hw] for k in range(3)], axis=0)
    value = jnp.concatenate([mid[...], outs, last[:kr, : 3 * hw]], axis=1)
    for j, ref in enumerate(refs):
        ref[...] = pick([value[a * own : (a + 1) * own] for a in range(4)], head[0] ^ j).astype(BF)


def spread_columns(head, p0, p1, p2, p3, cross_ref, query_ref, pair_ref, out_ref, self_ref):
    hw = p0.shape[1] // 8
    got = [p[...].astype(F32) for p in (p0, p1, p2, p3)]
    for a in range(4):
        rows = pick(got, head[0] ^ a)
        for t, (ref, base) in enumerate(
            ((cross_ref, 0), (query_ref, 0), (pair_ref, 0), (pair_ref, 4), (out_ref, 0), (self_ref, 0), (self_ref, 4), (self_ref, 8))
        ):
            ref[:, (base + a) * hw : (base + a + 1) * hw] = rows[:, t * hw : (t + 1) * hw]


def on_device(
    frames,
    condition,
    captions,
    caption_lengths,
    modulation_weight,
    modulation_bias,
    self_weight,
    self_out,
    self_bias,
    cross_gain,
    cross_query,
    cross_pair,
    cross_out,
    cross_bias,
    up_weight,
    up_bias,
    down_weight,
    down_bias,
    cotangent,
):
    n = lax.axis_size("seq")
    h = lax.axis_index("head")
    s = lax.axis_index("seq")
    rows, width = frames.shape
    hw = width // 4
    kr = self_weight.shape[0]
    own = kr // 4
    total = rows * 4

    ff = up_weight.shape[1]
    head = h.astype(jnp.int32)[None]

    def columns(weights, shape):
        return call(partial(own_columns, hw=hw), [head], weights, [out(shape, BF)])[0]

    w_own = columns((self_out, cross_out, self_weight), (kr, 5 * hw))
    condition, w_own, later = lax.optimization_barrier((condition, w_own, (cross_query, cross_pair)))
    w_later = columns(later, (n, kr, 3 * hw))
    w_own = lax.all_gather(w_own, "seq", axis=0, tiled=True)
    x = head_rel(frames)
    biases = jnp.concatenate([self_bias, cross_bias, cross_gain, down_bias])[None]
    got = exchange(jnp.concatenate([condition.reshape(n, kr), jnp.broadcast_to(biases, (n, 4 * kr))], axis=1))
    cond_own = jax.nn.silu(got[:, :kr].astype(F32)).astype(BF)
    vectors = got[:, kr:].astype(F32).reshape(n, 4, kr).transpose(1, 0, 2).reshape(4, width)
    out_bias, co_bias, gain, dn_bias = vectors[0], vectors[1], vectors[2], vectors[3]
    mod_part = mm(cond_own, modulation_weight) + lax.dynamic_update_slice(
        jnp.zeros((n * modulation_bias.shape[0],), F32),
        modulation_bias.astype(F32),
        (s * modulation_bias.shape[0],),
    )
    g = head_rel(cotangent)
    mod_part, x = lax.optimization_barrier((mod_part, x))
    mod = exchange(mod_part).sum(0, keepdims=True)
    w_own = after(w_own, (mod, w_later, g))
    updown = after((up_weight, down_weight), (mod, g))
    updown = jnp.concatenate([updown[0], updown[1].T], axis=1)
    updown = lax.all_gather(updown, "seq", axis=0, tiled=True)
    w_up = (updown, (slice(None), slice(0, ff)))
    w_down = (updown, (slice(None), slice(ff, 2 * ff)))
    w_later = exchange(after(w_later, mod)).reshape(width, 3 * hw)
    w_parts = w_own[:, : 2 * hw]
    mod, w_parts = lax.optimization_barrier((mod, w_parts))
    w_parts = head_rel(w_parts)
    caption = captions[0]
    slots = caption.shape[0]
    heads = hw // HD
    packed = (total // 2, 2 * hw)
    pad = -3 * hw % 128
    deep = out((total, width), BF)
    n_one, qkv, sm_own, probs, inv = call(
        self_forward,
        [],
        [*x, mod, w_own],
        [deep, out((3, total, hw), BF), out(packed, BF), out((heads, total, total), BF), out((heads, total), F32)],
        sends=4,
    )
    sm_parts = head_rel(sm_own)
    sm, w_out, proj, after_self, second, cq, pair, cm_own, cprobs, cinv = call(
        cross_forward,
        [head, caption_lengths],
        [*x, *w_parts, *sm_parts, mod, out_bias[None], gain[None], w_later, caption],
        [
            deep,
            out((width, width), BF),
            deep,
            out((total, width), F32),
            deep,
            out((total, hw), BF),
            out((2, slots, hw), BF),
            out(packed, BF),
            out((heads, slots, total), BF),
            out((heads, total), F32),
        ],
        sends=4,
    )
    cm_parts = head_rel(cm_own)
    cm, w_cross, across, third, hidden, g_up, g_feed, ga, *chunks, vec_c = call(
        feed_both,
        [head],
        [cm_parts[0], *w_parts, *cm_parts[1:], after_self, co_bias[None], mod]
        + [w_up, up_bias[None], w_down, *g],
        [deep, out((width, width), BF), out((rows, width), F32), deep]
        + [out((total, ff), BF), out((total, ff), BF), deep, deep]
        + [out(packed, BF) for _ in range(4)]
        + [out((8, width), F32)],
    )

    def near_terms(chunks):
        a, b = swap(chunks[1], 1), swap(chunks[3], 1)
        return chunks[0], a, (chunks[2].astype(F32) + b.astype(F32)).astype(BF)

    mine, near, other = near_terms(chunks)
    far = swap(other, 2)
    place = jnp.stack([h, s]).astype(jnp.int32)

    def halves(columns):
        shape = (width, columns) if kr % 16 else (n // 2, kr, columns)
        return [out(shape, BF) for _ in range(2)]

    def parted(near_rows, far_rows):
        if kr % 16 == 0:
            return near_rows, far_rows
        v = near_rows.reshape(n, kr, -1)
        for bit in (1 << b for b in range(n.bit_length() - 1)):
            pairs = v.reshape(n // (2 * bit), 2, bit, kr, -1)
            v = jnp.where((s & bit) != 0, pairs[:, ::-1], pairs).reshape(n, kr, -1)
        return v[0::2], v[1::2]

    *feed_chunks, both = call(
        feed_weights,
        [head],
        [after(cm, other), ga, hidden, w_down, third, g_up, g_feed],
        [out((rows, width + 3 * hw + pad), BF) for _ in range(4)] + [out((width, 2 * ff), BF)],
    )
    both = exchange(after(both, far).reshape(n, kr, 2 * ff))
    feed_mine, feed_near, feed_other = near_terms(after(tuple(feed_chunks), far))
    far, feed_other = lax.optimization_barrier((far, feed_other))
    feed_far = swap(feed_other, 2)
    dq, dpair, gas, g_proj, *chunks, vec_d = call(
        cross_back,
        [head],
        [mine, near, far, cm_own, cinv, pair, cq, cprobs, w_later, ga, after_self, gain[None], mod, proj, w_out],
        [out((total, hw), BF), out((2, slots, hw), BF), deep, deep]
        + [out(packed, BF) for _ in range(4)]
        + [out((8, width), F32)],
        [pltpu.VMEM((heads, slots, total), BF)],
    )
    mine, near, other = near_terms(chunks)
    other, feed_far = lax.optimization_barrier((other, feed_far))
    far = swap(other, 2)
    *mid, out0, out1, out2, out3, output_frames, gv_gate2 = call(
        partial(mid_weights, kr=kr),
        [place],
        [feed_mine, feed_near, feed_far, across, cotangent, mod, dn_bias[None]]
        + [after(sm, other), g_proj, caption, dpair, w_later, second, dq],
        halves(4 * hw)
        + [out((rows, 4 * hw), BF) for _ in range(4)]
        + [out((rows, width), BF), out((1, width), F32)],
        [pltpu.VMEM((width, 4 * hw), BF)],
    )
    out_mine, out_near, out_other = near_terms(after((out0, out1, out2, out3), far))
    far, mid, out_other = lax.optimization_barrier((far, mid, out_other))
    out_far = swap(out_other, 2)
    mid = half_reduce(*parted(*mid))
    g_joint, *last, vec = call(
        partial(self_back, kr=kr),
        [place],
        [mine, near, far, sm_own, inv, qkv, probs, n_one, (w_own, (slice(None), slice(2 * hw, 5 * hw)))]
        + [mod, vec_c, vec_d, gv_gate2],
        [out((total, 3 * hw), BF)] + halves(3 * hw + pad) + [out((16, width), F32)],
        [pltpu.VMEM((heads, total, total), BF), pltpu.VMEM((width, 3 * hw + pad), BF)],
    )
    vec, mid, both, out_far = lax.optimization_barrier((vec, mid, both, out_far))
    near_rows, far_rows = parted(*last)
    last = half_reduce(near_rows, after(far_rows, mid))
    last_y = last
    shared = vec + swap(vec, 1)
    shared = shared + swap(shared, 2)
    vec = jnp.where(jnp.arange(16)[:, None] == 10, vec, shared).astype(BF)
    mid_y = mid
    sent_mid = []
    mid = rest_reduce(mid, sent_mid)
    third_shape = (width, hw) if kr % 16 else (n // 2, kr // 3, 3 * hw + pad)
    *outs, grad_captions = call(
        partial(out_rows, kr=kr),
        [place],
        [out_mine, out_near, out_far],
        [out(third_shape, BF) for _ in range(2)] + [out((1, slots, hw), F32)],
        [pltpu.VMEM((width, hw), BF)],
    )
    near_rows, far_rows = parted(*outs)
    if kr % 16:
        near_rows, far_rows = (
            jnp.pad(
                v.reshape(n // 2, 3, kr // 3, hw).transpose(0, 2, 1, 3).reshape(n // 2, kr // 3, 3 * hw),
                ((0, 0), (0, 0), (0, pad)),
            )
            for v in (near_rows, far_rows)
        )
    outs = half_reduce(near_rows, far_rows)
    vec = exchange(jnp.broadcast_to(after(vec, last_y)[None], (n, *vec.shape))).astype(F32)
    sent = []
    last = rest_reduce(jnp.concatenate([last, outs], axis=1), sent)
    outs = last[kr:]
    gf = call(first_back, [], [*x, g_joint, w_own, mod, after(gas, sent_mid[-1])], [out((rows, width), BF)] * 4)
    if kr % 16:
        outs = outs[:, : 3 * hw].reshape(own * 4 // 3, 3, hw).transpose(1, 0, 2).reshape(kr, hw)
    frame_mine, frame_near, frame_other = near_terms(gf)

    g_mod = vec[:, :6].reshape(n, 6 * width)
    g_cond = lax.dot_general(
        g_mod,
        modulation_weight.astype(F32),
        (((1,), (1,)), ((), ())),
        precision=lax.Precision.HIGHEST,
        preferred_element_type=F32,
    )
    g_silu = exchange(after(g_cond, frame_other)).reshape(width)
    g_cond = jax.vjp(jax.nn.silu, condition[0].astype(F32))[1](g_silu)[0]
    grad_condition = lax.dynamic_slice_in_dim(g_cond, h * hw, hw, 0)[None]
    cond_rows = lax.dynamic_slice_in_dim(cond_own, h * own, own, 1).astype(F32)
    grad_mod_weight = lax.dot_general(
        cond_rows, g_mod, (((0,), (0,)), ((), ())), precision=lax.Precision.HIGHEST, preferred_element_type=F32
    )
    sums = vec.sum(0)
    index = s * 4 + h
    mb = 6 * width // (4 * n)
    grad_mod_bias = lax.dynamic_slice_in_dim(sums[:6].reshape(6 * width), index * mb, mb, 0)

    def own_vec(i):
        return lax.dynamic_slice_in_dim(sums[6 + i], index * own, own, 0)

    both = both.astype(F32).sum(0)
    tiny = dict(small=1 << 20, limit=8)
    cols = call(column_chunks, [head], [mid, last, outs], [out((own, 8 * hw), BF) for _ in range(4)], **tiny)
    frame_far = swap(frame_other, 2)
    grad_frames = frame_mine.astype(F32) + frame_near.astype(F32) + frame_far.astype(F32)
    cols = [cols[0]] + [
        lax.ppermute(cols[j], "head", [(i, i ^ j) for i in range(4)]) for j in range(1, 4)
    ]
    grad_cross, grad_query, grad_pair, grad_out, grad_self = call(
        spread_columns, [head], cols, [out((own, k * width), F32) for k in (1, 1, 2, 1, 3)], **tiny
    )
    return (
        output_frames,
        grad_frames,
        grad_condition,
        grad_captions,
        grad_mod_weight,
        grad_mod_bias,
        grad_self,
        grad_out,
        own_vec(0),
        own_vec(1),
        grad_query,
        grad_pair,
        grad_cross,
        own_vec(2),
        both[:, :ff],
        sums[10],
        both[:, ff:].T,
        own_vec(3),
    )


def solution(mesh):
    both = ("seq", "head")
    return jax.shard_map(
        on_device,
        mesh=mesh,
        in_specs=(
            P(both, None),
            P("seq", None),
            P("seq", None, None),
            P("seq"),
            P("seq", None),
            P("seq"),
            P("seq", None),
            P("seq", None),
            P("seq"),
            P("seq"),
            P("seq", None),
            P("seq", None),
            P("seq", None),
            P("seq"),
            P("seq", "head"),
            P("head"),
            P("head", "seq"),
            P("seq"),
            P(both, None),
        ),
        out_specs=(
            P(both, None),
            P(both, None),
            P("seq", "head"),
            P("seq", None, "head"),
            P(both, None),
            P(both),
            P(both, None),
            P(both, None),
            P(both),
            P(both),
            P(both, None),
            P(both, None),
            P(both, None),
            P(both),
            P("seq", "head"),
            P("head"),
            P("head", "seq"),
            P(both),
        ),
        check_vma=False,
    )
```

```python
from functools import partial

import jax
import jax.numpy as jnp
from jax import lax
from jax.experimental import pallas as pl
from jax.experimental.pallas import tpu as pltpu
from jax.sharding import PartitionSpec as P

HD = 64
BF = jnp.bfloat16
F32 = jnp.float32


def mm(a, b, ca=1, cb=0):
    return lax.dot_general(a, b, (((ca,), (cb,)), ((), ())), preferred_element_type=F32)


def swap(x, bit):
    return lax.ppermute(x, "head", [(i, i ^ bit) for i in range(4)])


def swap_rows(x, bit):
    blocks = jnp.split(swap(x, bit), 4, axis=0)
    return jnp.concatenate([blocks[i ^ bit] for i in range(4)], axis=0)


def head_rel(x, swap=swap):
    near = swap(x, 1)
    far = swap(x, 2)
    return [x, near, far, swap(far, 1)]


def pick(parts, index):
    low, high = (index & 1) == 1, (index & 2) == 2
    return jnp.where(
        high, jnp.where(low, parts[3], parts[2]), jnp.where(low, parts[1], parts[0])
    )


def after(values, ready):
    return lax.optimization_barrier((values, ready))[0]


def seq_swap(x, bit):
    return lax.ppermute(x, "seq", [(i, i ^ bit) for i in range(lax.axis_size("seq"))])


def exchange(x):
    return lax.all_to_all(x, "seq", split_axis=0, concat_axis=0, tiled=True)


def half_reduce(near, far):
    return (near.astype(F32) + seq_swap(far, 1).astype(F32)).astype(BF)


def rest_reduce(x, sent=None):
    x, bit = x.astype(F32), 2
    while x.shape[0] > 1:
        send = x[1::2].astype(BF)
        if sent is not None:
            sent.append(send)
        x, bit = x[0::2] + seq_swap(send, bit).astype(F32), 2 * bit
    return x[0]


def stats(v):
    mean = jnp.mean(v, axis=-1, keepdims=True)
    center = v - mean
    r = lax.rsqrt(jnp.mean(center * center, axis=-1, keepdims=True) + 1e-6)
    return center * r, r


def normback(n, r, e):
    return r * (
        e - jnp.mean(e, axis=-1, keepdims=True) - n * jnp.mean(e * n, axis=-1, keepdims=True)
    )


class Held:
    def __init__(self, outside, inside, sems, count):
        self.outside, self.inside, self.sems, self.count = outside, inside, sems, count
        self.pending = []
        self.shape, self.dtype = inside.shape, inside.dtype

    def copy(self, source, target):
        copy = pltpu.make_async_copy(source, target, self.sems.at[self.count[0]])
        self.count[0] += 1
        copy.start()
        self.pending.append(copy)

    def send(self, at=...):
        if self.outside is not None:
            self.copy(self.inside.at[at], self.outside.at[at])

    def wait(self):
        for copy in self.pending:
            copy.wait()
        self.pending = []

    def __getitem__(self, at):
        self.wait()
        return self.inside[at]

    def __setitem__(self, at, value):
        self.inside[at] = value


class Result(Held):
    def __getitem__(self, at):
        return self.inside[at]


def call(kernel, scalars, ins, outs, scratch=(), sends=0, small=0, limit=58):
    ins = [v if isinstance(v, tuple) else (v, ...) for v in ins]
    parts = [v if at is ... else jax.eval_shape(lambda x, at=at: x[at], v) for v, at in ins]

    def is_small(v):
        return v.size * v.dtype.itemsize <= small

    plain = [is_small(v) and at is ... for v, at in ins] + [is_small(v) for v in outs]
    kept = [v for v, p in zip((*parts, *outs), plain) if not p]

    def body(*refs):
        refs = list(refs)
        numbers = [refs.pop(0) for _ in scalars]
        outside = [refs.pop(0) for _ in plain]
        inside = [refs.pop(0) for _ in kept]
        sems, rest, count = refs[-1], refs[:-1], [0]
        arrays = []
        for k, (ref, p) in enumerate(zip(outside, plain)):
            kind = Held if k < len(ins) else Result
            arrays.append(kind(None, ref, sems, count) if p else kind(ref, inside.pop(0), sems, count))
        held, results = arrays[: len(ins)], arrays[len(ins) :]
        for v, (_, at) in zip(held, ins):
            if v.outside is not None:
                v.copy(v.outside.at[at], v.inside)
        kernel(*numbers, *held, *results, *rest)
        for v in results:
            if not v.pending:
                v.send()
        for v in arrays:
            v.wait()

    specs = [pl.BlockSpec(memory_space=pltpu.VMEM if p else pl.ANY) for p in plain]
    return pl.pallas_call(
        body,
        in_specs=[pl.BlockSpec(memory_space=pltpu.SMEM)] * len(scalars) + specs[: len(ins)],
        out_specs=specs[len(ins) :],
        out_shape=list(outs),
        scratch_shapes=[pltpu.VMEM(v.shape, v.dtype) for v in kept]
        + list(scratch)
        + [pltpu.SemaphoreType.DMA((len(kept) + sends + 1,))],
        compiler_params=pltpu.CompilerParams(vmem_limit_bytes=limit * 1024 * 1024),
    )(*scalars, *[v for v, _ in ins])


def out(shape, dtype):
    return jax.ShapeDtypeStruct(shape, dtype)


def block(b, size=256):
    return slice(b * size, (b + 1) * size)


def packed_at(shape, b):
    size, half = shape[0] // 2, shape[1] // 2
    return (block(b // 2, size), slice(half * (b % 2), half * (b % 2 + 1)))


def unpack(ref, b):
    return ref[packed_at(ref.shape, b)]


def pack(ref, b, value):
    ref[packed_at(ref.shape, b)] = value


def by_head(parts, head):
    return jnp.concatenate([pick(parts, head ^ a) for a in range(4)], axis=1)


def chunks_by_head(value, head):
    hw = value.shape[1] // 4
    blocks = [value[:, a * hw : (a + 1) * hw] for a in range(4)]
    return [pick(blocks, head ^ j) for j in range(4)]


def staggered(stages, tasks):
    done = [None] * len(tasks)
    for t in range(len(tasks) + len(stages) - 1):
        for k, stage in enumerate(stages):
            if 0 <= t - k < len(tasks):
                done[t - k] = stage(*tasks[t - k]) if k == 0 else stage(*tasks[t - k], done[t - k])
    return done


def of_head(values, hd):
    lane = lax.broadcasted_iota(jnp.int32, (1, values.shape[1]), 1) // HD
    return jnp.where(lane == hd, values, 0)


def softmax_columns(keys, queries, values_t, p_ref, inv_ref, visible=None):
    heads = keys.shape[1] // HD
    own_keys = [of_head(keys, hd) for hd in range(heads)]

    def scores(b, hd):
        return mm(own_keys[hd], queries[b], 1, 1)

    def weights(b, hd, st):
        if visible is not None:
            st = jnp.where(visible, st, -1e30)
        e = jnp.exp(st - jnp.max(st, axis=0, keepdims=True))
        inv = 1.0 / jnp.sum(e, axis=0, keepdims=True)
        low = e.astype(BF)
        p_ref[hd, :, block(b)] = low
        inv_ref[hd : hd + 1, block(b)] = inv
        return low, inv

    def mixed(b, hd, done):
        result = mm(values_t[hd * HD : (hd + 1) * HD, :], done[0]) * done[1]
        if hd == heads - 1:
            p_ref.send((slice(None), slice(None), block(b)))
        return result

    parts = staggered((scores, weights, mixed), [(b, hd) for b in range(len(queries)) for hd in range(heads)])
    return [
        jnp.concatenate(parts[b * heads : (b + 1) * heads], axis=0).T.astype(BF) for b in range(len(queries))
    ]


def softmax_back(keys, values, queries, p_ref, inv_ref, results, grads, ds_ref):
    heads = keys.shape[1] // HD
    keys_t = keys.astype(F32).T.astype(BF)
    own_values = [of_head(values, hd) for hd in range(heads)]
    count = len(grads)
    scaled, inner = [], []
    for b in range(count):
        go_t, o_t = grads[b].T, results[b].astype(F32).T
        parts = []
        for hd in range(heads):
            at = slice(hd * HD, (hd + 1) * HD)
            parts.append(go_t[at, :] * inv_ref[hd : hd + 1, block(b)])
            inner.append(jnp.sum(parts[-1] * o_t[at, :], axis=0, keepdims=True))
        scaled.append(jnp.concatenate(parts, axis=0).T.astype(BF))

    def dprob(b, hd):
        return mm(own_values[hd], scaled[b], 1, 1)

    def dscore(b, hd, dp):
        ds = (p_ref[hd, :, block(b)].astype(F32) * (dp - inner[b * heads + hd])).astype(BF)
        ds_ref[hd, :, block(b)] = ds
        return ds

    def dquery(b, hd, ds):
        return mm(keys_t[hd * HD : (hd + 1) * HD, :], ds)

    parts = staggered((dprob, dscore, dquery), [(b, hd) for b in range(count) for hd in range(heads)])
    dq = [
        (jnp.concatenate(parts[b * heads : (b + 1) * heads], axis=0).T * 0.125).astype(BF) for b in range(count)
    ]
    everything = jnp.concatenate(scaled, axis=0)
    dk = sum(of_head(mm(ds_ref[hd], queries), hd) for hd in range(heads))
    dv = sum(of_head(mm(p_ref[hd], everything), hd) for hd in range(heads))
    return dq, dk.astype(BF), dv.astype(BF)


BLOCKS = range(4)


def self_forward(x0, x1, x2, x3, mod, w, n_ref, qkv_ref, sm_ref, p_ref, inv_ref):
    width = x0.shape[1]
    hw = sm_ref.shape[1] // 2
    norms = [stats(x[...].astype(F32))[0] for x in (x0, x1, x2, x3)]
    scale, shift = 1.0 + mod[:, width : 2 * width], mod[:, :width]
    firsts = [(n * scale + shift).astype(BF) for n in norms]
    weights = w[:, 2 * hw :]
    joints = [mm(first, weights) for first in firsts]
    for b in BLOCKS:
        n_ref[block(b), :] = norms[b].astype(BF)
    n_ref.send()
    queries = [(joint[:, :hw] * 0.125).astype(BF) for joint in joints]
    keys = jnp.concatenate([joint[:, hw : 2 * hw].astype(BF) for joint in joints], axis=0)
    for b in BLOCKS:
        qkv_ref[0, block(b), :] = queries[b]
        qkv_ref[2, block(b), :] = joints[b][:, 2 * hw :].astype(BF)
    qkv_ref[1] = keys
    qkv_ref.send()
    values_t = jnp.concatenate([joint[:, 2 * hw :].T.astype(BF) for joint in joints], axis=1)
    for b, result in enumerate(softmax_columns(keys, queries, values_t, p_ref, inv_ref)):
        pack(sm_ref, b, result)


def cross_forward(
    head, length, x0, x1, x2, x3, w0, w1, w2, w3, sm0, sm1, sm2, sm3, mod, out_bias, gain, w_later, caption,
    sm_ref, wout_ref, proj_ref, after_ref, second_ref, cq_ref, pair_ref, cm_ref, p_ref, inv_ref,
):
    h = head[0]
    width = x0.shape[1]
    hw = cq_ref.shape[1]
    w_out = by_head([w[:, :hw] for w in (w0, w1, w2, w3)], h)
    wout_ref[...] = w_out
    wout_ref.send()
    mixed = [by_head([unpack(p, b ^ j) for j, p in enumerate((sm0, sm1, sm2, sm3))], h) for b in BLOCKS]
    projs = [mm(m, w_out) + out_bias[...] for m in mixed]
    pair = mm(caption[...], w_later[:, hw:])
    keys, values = pair[:, :hw].astype(BF), pair[:, hw:]
    pair_ref[0] = keys
    pair_ref[1] = values.astype(BF)
    afters, seconds = [], []
    for b, x in enumerate((x0, x1, x2, x3)):
        sm_ref[block(b), :] = mixed[b]
        proj_ref[block(b), :] = projs[b].astype(BF)
        after = x[...].astype(F32) + mod[:, 2 * width : 3 * width] * projs[b]
        after_ref[block(b), :] = after
        seconds.append((stats(after)[0] * gain[...]).astype(BF))
        second_ref[block(b), :] = seconds[b]
    for ref in (sm_ref, proj_ref, after_ref, second_ref):
        ref.send()
    queries = [(mm(second, w_later[:, :hw]) * 0.125).astype(BF) for second in seconds]
    for b in BLOCKS:
        cq_ref[block(b), :] = queries[b]
    slots = lax.broadcasted_iota(jnp.int32, (caption.shape[0], 1), 0)
    results = softmax_columns(keys, queries, values.T.astype(BF), p_ref, inv_ref, slots < length[0])
    for b, result in enumerate(results):
        pack(cm_ref, b, result)


def feed_both(
    head, cm0, w0, w1, w2, w3, cm1, cm2, cm3, after, co_bias, mod, w_up, up_bias, w_down, g0, g1, g2, g3,
    cm_ref, wc_ref, across_ref, third_ref, hidden_ref, gup_ref, gfeed_ref, ga_ref, c0, c1, c2, c3, vec_ref,
):
    h = head[0]
    width = after.shape[1]
    hw = width // 4
    ff = w_up.shape[1]
    w_cross = by_head([w[:, hw:] for w in (w0, w1, w2, w3)], h)
    wc_ref[...] = w_cross
    wc_ref.send()
    mixed = [by_head([unpack(p, b ^ j) for j, p in enumerate((cm0, cm1, cm2, cm3))], h) for b in BLOCKS]
    across = [after[block(b), :] + mm(mixed[b], w_cross) + co_bias[...] for b in BLOCKS]
    across_ref[...] = across[0]
    across_ref.send()
    scale, shift = 1.0 + mod[:, 4 * width : 5 * width], mod[:, 3 * width : 4 * width]
    norms = [stats(v) for v in across]
    thirds = [(n * scale + shift).astype(BF) for n, _ in norms]
    for b in BLOCKS:
        cm_ref[block(b), :] = mixed[b]
        third_ref[block(b), :] = thirds[b]
    cm_ref.send()
    third_ref.send()
    ups = [mm(third, w_up[...]) + up_bias[...].astype(F32) for third in thirds]
    cots = [g[...].astype(F32) for g in (g0, g1, g2, g3)]
    feeds = [(mod[:, 5 * width :] * cot).astype(BF) for cot in cots]
    hiddens = [mm(feed, w_down[...]) for feed in feeds]
    gups = []
    for b in BLOCKS:
        v = ups[b]
        t = jnp.tanh(0.7978845608028654 * (v + 0.044715 * v * v * v))
        hidden_ref[block(b), :] = (0.5 * v * (1.0 + t)).astype(BF)
        slope = 0.5 * (1.0 + t) + 0.5 * v * (1.0 - t * t) * (0.7978845608028654 * (1.0 + 0.134145 * v * v))
        gups.append((hiddens[b] * slope).astype(BF))
        gup_ref[block(b), :] = gups[b]
        gfeed_ref[block(b), :] = feeds[b]
    for ref in (hidden_ref, gup_ref, gfeed_ref):
        ref.send()
    gthirds = [mm(gup, w_up[...], 1, 1) for gup in gups]
    gas = [normback(*norms[b], scale * gthirds[b]) for b in BLOCKS]
    gas[0] = gas[0] + cots[0]
    lows = [ga.astype(BF) for ga in gas]
    for b in BLOCKS:
        ga_ref[block(b), :] = lows[b]
    ga_ref.send()
    for b in BLOCKS:
        chunks = chunks_by_head(mm(lows[b], w_cross, 1, 1).astype(BF), h)
        for j, (ref, chunk) in enumerate(zip((c0, c1, c2, c3), chunks)):
            pack(ref, b ^ j, chunk)

    def over_rows(values):
        return sum(jnp.sum(v, axis=0, keepdims=True) for v in values)

    vec_ref[...] = jnp.concatenate(
        [
            over_rows(gthirds),
            over_rows([gthirds[b] * norms[b][0] for b in BLOCKS]),
            over_rows(gas),
            over_rows([gup.astype(F32) for gup in gups]),
            over_rows([feeds[0].astype(F32)]),
            jnp.zeros((3, width), F32),
        ],
        axis=0,
    )


def cross_back(
    head, a0, a1, a2, cm, inv, pair, cq, p, w_later, ga, after, gain, mod, proj, wout,
    dq_ref, dpair_ref, gas_ref, gproj_ref, c0, c1, c2, c3, vec_ref, ds_ref,
):
    h = head[0]
    width = after.shape[1]
    hw = cq.shape[1]
    grads = [sum(unpack(a, b).astype(F32) for a in (a0, a1, a2)) for b in BLOCKS]
    results = [unpack(cm, b) for b in BLOCKS]
    dqs, dk, dv = softmax_back(pair[0], pair[1], cq[...], p, inv, results, grads, ds_ref)
    dpair_ref[0] = dk
    dpair_ref[1] = dv
    for b in BLOCKS:
        dq_ref[block(b), :] = dqs[b]
    gseconds = [mm(dq, w_later[:, :hw], 1, 1) for dq in dqs]
    norms = [stats(after[block(b), :]) for b in BLOCKS]
    gas = [ga[block(b), :].astype(F32) + normback(*norms[b], gain[...] * gseconds[b]) for b in BLOCKS]
    gprojs = [(mod[:, 2 * width : 3 * width] * v).astype(BF) for v in gas]
    for b in BLOCKS:
        gas_ref[block(b), :] = gas[b].astype(BF)
        gproj_ref[block(b), :] = gprojs[b]
    gas_ref.send()
    gproj_ref.send()
    for b in BLOCKS:
        chunks = chunks_by_head(mm(gprojs[b], wout[...], 1, 1).astype(BF), h)
        for j, (ref, chunk) in enumerate(zip((c0, c1, c2, c3), chunks)):
            pack(ref, b ^ j, chunk)

    def over_rows(values):
        return sum(jnp.sum(v, axis=0, keepdims=True) for v in values)

    vec_ref[...] = jnp.concatenate(
        [
            over_rows([gas[b] * proj[block(b), :].astype(F32) for b in BLOCKS]),
            over_rows([gseconds[b] * norms[b][0] for b in BLOCKS]),
            over_rows([gproj.astype(F32) for gproj in gprojs]),
            jnp.zeros((5, width), F32),
        ],
        axis=0,
    )


def self_back(
    place, a0, a1, a2, sm, inv, qkv, p, n_one, w, mod, vec_c, vec_d, gate, grads_ref, near_ref, far_ref, vec_ref, ds_ref, whole_ref,
    *, kr,
):
    hw = qkv.shape[2]
    width = w.shape[0]
    grads = [sum(unpack(a, b).astype(F32) for a in (a0, a1, a2)) for b in BLOCKS]
    results = [unpack(sm, b) for b in BLOCKS]
    dqs, dk, dv = softmax_back(qkv[1], qkv[2], qkv[0], p, inv, results, grads, ds_ref)
    joint = jnp.concatenate([jnp.concatenate(dqs, axis=0), dk, dv], axis=1)
    grads_ref[...] = joint
    grads_ref.send()
    product = mm(n_one[...], joint, 0, 0)
    sums = jnp.sum(joint.astype(F32), axis=0, keepdims=True)
    weights = w[...].astype(F32)
    grad = (1.0 + mod[:, width : 2 * width]).T * product + mod[:, :width].T * sums
    empty = jnp.zeros((width, near_ref.shape[-1] - 3 * hw), BF)
    whole_ref[...] = jnp.concatenate([grad.astype(BF), empty], axis=1)
    part_rows(whole_ref, place, near_ref, far_ref, kr)
    shift_one = jnp.sum(weights * sums, axis=1, keepdims=True).T
    scale_one = jnp.sum(weights * product, axis=1, keepdims=True).T
    rows = [shift_one, scale_one, vec_d[0:1], vec_c[0:1], vec_c[1:2], gate[...], vec_d[2:3], vec_d[1:2]]
    rows += [vec_c[2:3], vec_c[4:5], vec_c[3:4], jnp.zeros((5, width), F32)]
    vec_ref[...] = jnp.concatenate(rows, axis=0)


def out_rows(place, o0, o1, o2, near_ref, far_ref, cap_ref, whole_ref, *, kr):
    hw = o0.shape[1] // 4
    rows = o0.shape[0]
    total = sum(o[...].astype(F32) for o in (o0, o1, o2))
    cap_ref[0] = total[:, 3 * hw :]
    low = total[:, : 3 * hw].astype(BF)
    for k in range(3):
        whole_ref[block(k, rows), :] = low[:, k * hw : (k + 1) * hw]
    part_rows(whole_ref, place, near_ref, far_ref, kr, out_third=kr // 3)


def first_back(x0, x1, x2, x3, grads, w, mod, gas, *frame_refs):
    width = x0.shape[1]
    weights = w[:, w.shape[1] - grads.shape[1] :]
    gfirsts = [mm(grads[block(b), :], weights, 1, 1) for b in BLOCKS]
    scale = 1.0 + mod[:, width : 2 * width]
    for b, x in enumerate((x0, x1, x2, x3)):
        ga = normback(*stats(x[...].astype(F32)), scale * gfirsts[b])
        frame_refs[b][...] = (gas[block(b), :].astype(F32) + ga).astype(BF)


def own_columns(head, *refs, hw):
    sources, target = refs[:-1], refs[-1]
    t = 0
    for ref in sources:
        for base in range(0, ref.shape[1], 4 * hw):
            part = pick([ref[:, base + a * hw : base + (a + 1) * hw] for a in range(4)], head[0])
            if len(target.shape) == 2:
                target[:, t * hw : (t + 1) * hw] = part
            else:
                for d in range(target.shape[0]):
                    target[d, :, t * hw : (t + 1) * hw] = part
            t += 1


def feed_weights(head, cm, ga, hidden, w_down, third, gup, gfeed, c0, c1, c2, c3, both_ref):
    width = ga.shape[1]
    hw = width // 4
    rows = hidden.shape[0] // 4
    chunks = chunks_by_head(mm(cm[...], ga[...], 0, 0).astype(BF), head[0])
    for j, ref in enumerate((c0, c1, c2, c3)):
        ref[:, :width] = mm(hidden[block(j, rows), :], w_down[...], 1, 1).astype(BF)
        for k in range(3):
            ref[:, width + k * hw : width + (k + 1) * hw] = chunks[j][k * rows : (k + 1) * rows]
        ref[:, width + 3 * hw :] = jnp.zeros((rows, ref.shape[1] - width - 3 * hw), BF)
        ref.send()
    both_ref[:, : gup.shape[1]] = mm(third[...], gup[...], 0, 0).astype(BF)
    both_ref[:, gup.shape[1] :] = mm(gfeed[...], hidden[...], 0, 0).astype(BF)


def part_rows(value, place, near_ref, far_ref, kr, out_third=0):
    if kr % 16:
        near_ref[...] = value[...]
        far_ref[...] = value[...]
        return
    for j in range(near_ref.shape[0]):
        first = ((place[1] >> 1) ^ j) * 2
        for ref, index in ((near_ref, first + (place[1] & 1)), (far_ref, first + 1 - (place[1] & 1))):
            block_rows = value[pl.ds(pl.multiple_of(index * kr, kr), kr), :]
            if out_third:
                hw = block_rows.shape[1]
                for k in range(3):
                    ref[j, :, k * hw : (k + 1) * hw] = block_rows[k * out_third : (k + 1) * out_third]
                ref[j, :, 3 * hw :] = jnp.zeros((out_third, ref.shape[2] - 3 * hw), BF)
            else:
                ref[j] = block_rows


def mid_weights(
    place, f0, f1, f2, across, cot, mod, dn_bias, sm, gproj, caption, dpair, w_later, second, dq,
    near_ref, far_ref, c0, c1, c2, c3, output_ref, gate_ref, whole_ref, *, kr,
):
    hw, width = dq.shape[1], sm.shape[1]
    rows = f0.shape[0]
    total = sum(f[...].astype(F32) for f in (f0, f1, f2))
    feed = total[:, :width] + dn_bias[...]
    output_ref[...] = (across[...] + mod[:, 5 * width :] * feed).astype(BF)
    gate_ref[...] = jnp.sum(cot[...].astype(F32) * feed, axis=0, keepdims=True)
    out_chunks = chunks_by_head(mm(sm[...], gproj[...], 0, 0).astype(BF), place[0])
    cap = mm(dpair[0], w_later[:, hw : 2 * hw], 1, 1) + mm(dpair[1], w_later[:, 2 * hw :], 1, 1)
    cap_chunks = chunks_by_head(cap.astype(BF), place[0])
    for ref, out_chunk, cap_chunk in zip((c0, c1, c2, c3), out_chunks, cap_chunks):
        for k in range(3):
            ref[:, k * hw : (k + 1) * hw] = out_chunk[k * rows : (k + 1) * rows]
        ref[:, 3 * hw :] = cap_chunk
    low = total[:, width:].astype(BF)
    cross = jnp.concatenate([low[:, k * hw : (k + 1) * hw] for k in range(3)], axis=0)
    parts = [mm(second[...], dq[...], 0, 0)] + [mm(caption[...], dpair[t], 0, 0) for t in range(2)]
    whole_ref[...] = jnp.concatenate([cross] + [p.astype(BF) for p in parts], axis=1)
    part_rows(whole_ref, place, near_ref, far_ref, kr)


def column_chunks(head, mid, last, third_rows, *refs):
    own = refs[0].shape[0]
    hw = mid.shape[1] // 4
    kr = 4 * own

    outs = third_rows[...]
    if outs.shape[1] > hw:
        outs = jnp.concatenate([outs[:, k * hw : (k + 1) * hw] for k in range(3)], axis=0)
    value = jnp.concatenate([mid[...], outs, last[:kr, : 3 * hw]], axis=1)
    for j, ref in enumerate(refs):
        ref[...] = pick([value[a * own : (a + 1) * own] for a in range(4)], head[0] ^ j).astype(BF)


def spread_columns(head, p0, p1, p2, p3, cross_ref, query_ref, pair_ref, out_ref, self_ref):
    hw = p0.shape[1] // 8
    got = [p[...].astype(F32) for p in (p0, p1, p2, p3)]
    for a in range(4):
        rows = pick(got, head[0] ^ a)
        for t, (ref, base) in enumerate(
            ((cross_ref, 0), (query_ref, 0), (pair_ref, 0), (pair_ref, 4), (out_ref, 0), (self_ref, 0), (self_ref, 4), (self_ref, 8))
        ):
            ref[:, (base + a) * hw : (base + a + 1) * hw] = rows[:, t * hw : (t + 1) * hw]


def on_device(
    frames,
    condition,
    captions,
    caption_lengths,
    modulation_weight,
    modulation_bias,
    self_weight,
    self_out,
    self_bias,
    cross_gain,
    cross_query,
    cross_pair,
    cross_out,
    cross_bias,
    up_weight,
    up_bias,
    down_weight,
    down_bias,
    cotangent,
):
    n = lax.axis_size("seq")
    h = lax.axis_index("head")
    s = lax.axis_index("seq")
    rows, width = frames.shape
    hw = width // 4
    kr = self_weight.shape[0]
    own = kr // 4
    total = rows * 4

    ff = up_weight.shape[1]
    head = h.astype(jnp.int32)[None]

    def columns(weights, shape):
        return call(partial(own_columns, hw=hw), [head], weights, [out(shape, BF)])[0]

    w_own = columns((self_out, cross_out, self_weight), (kr, 5 * hw))
    condition, w_own, later = lax.optimization_barrier((condition, w_own, (cross_query, cross_pair)))
    w_later = columns(later, (n, kr, 3 * hw))
    w_own = lax.all_gather(w_own, "seq", axis=0, tiled=True)
    x = head_rel(frames)
    biases = jnp.concatenate([self_bias, cross_bias, cross_gain, down_bias])[None]
    got = exchange(jnp.concatenate([condition.reshape(n, kr), jnp.broadcast_to(biases, (n, 4 * kr))], axis=1))
    cond_own = jax.nn.silu(got[:, :kr].astype(F32)).astype(BF)
    vectors = got[:, kr:].astype(F32).reshape(n, 4, kr).transpose(1, 0, 2).reshape(4, width)
    out_bias, co_bias, gain, dn_bias = vectors[0], vectors[1], vectors[2], vectors[3]
    mod_part = mm(cond_own, modulation_weight) + lax.dynamic_update_slice(
        jnp.zeros((n * modulation_bias.shape[0],), F32),
        modulation_bias.astype(F32),
        (s * modulation_bias.shape[0],),
    )
    g = head_rel(cotangent)
    mod_part, x = lax.optimization_barrier((mod_part, x))
    mod = exchange(mod_part).sum(0, keepdims=True)
    w_own = after(w_own, (mod, w_later, g))
    updown = after((up_weight, down_weight), (mod, g))
    updown = jnp.concatenate([updown[0], updown[1].T], axis=1)
    updown = lax.all_gather(updown, "seq", axis=0, tiled=True)
    w_up = (updown, (slice(None), slice(0, ff)))
    w_down = (updown, (slice(None), slice(ff, 2 * ff)))
    w_later = exchange(after(w_later, mod)).reshape(width, 3 * hw)
    w_parts = w_own[:, : 2 * hw]
    mod, w_parts = lax.optimization_barrier((mod, w_parts))
    w_parts = head_rel(w_parts)
    caption = captions[0]
    slots = caption.shape[0]
    heads = hw // HD
    packed = (total // 2, 2 * hw)
    pad = -3 * hw % 128
    deep = out((total, width), BF)
    n_one, qkv, sm_own, probs, inv = call(
        self_forward,
        [],
        [*x, mod, w_own],
        [deep, out((3, total, hw), BF), out(packed, BF), out((heads, total, total), BF), out((heads, total), F32)],
        sends=4,
    )
    sm_parts = head_rel(sm_own)
    sm, w_out, proj, after_self, second, cq, pair, cm_own, cprobs, cinv = call(
        cross_forward,
        [head, caption_lengths],
        [*x, *w_parts, *sm_parts, mod, out_bias[None], gain[None], w_later, caption],
        [
            deep,
            out((width, width), BF),
            deep,
            out((total, width), F32),
            deep,
            out((total, hw), BF),
            out((2, slots, hw), BF),
            out(packed, BF),
            out((heads, slots, total), BF),
            out((heads, total), F32),
        ],
        sends=4,
    )
    cm_parts = head_rel(cm_own)
    cm, w_cross, across, third, hidden, g_up, g_feed, ga, *chunks, vec_c = call(
        feed_both,
        [head],
        [cm_parts[0], *w_parts, *cm_parts[1:], after_self, co_bias[None], mod]
        + [w_up, up_bias[None], w_down, *g],
        [deep, out((width, width), BF), out((rows, width), F32), deep]
        + [out((total, ff), BF), out((total, ff), BF), deep, deep]
        + [out(packed, BF) for _ in range(4)]
        + [out((8, width), F32)],
    )

    def near_terms(chunks):
        a, b = swap(chunks[1], 1), swap(chunks[3], 1)
        return chunks[0], a, (chunks[2].astype(F32) + b.astype(F32)).astype(BF)

    mine, near, other = near_terms(chunks)
    far = swap(other, 2)
    place = jnp.stack([h, s]).astype(jnp.int32)

    def halves(columns):
        shape = (width, columns) if kr % 16 else (n // 2, kr, columns)
        return [out(shape, BF) for _ in range(2)]

    def parted(near_rows, far_rows):
        if kr % 16 == 0:
            return near_rows, far_rows
        v = near_rows.reshape(n, kr, -1)
        for bit in (1 << b for b in range(n.bit_length() - 1)):
            pairs = v.reshape(n // (2 * bit), 2, bit, kr, -1)
            v = jnp.where((s & bit) != 0, pairs[:, ::-1], pairs).reshape(n, kr, -1)
        return v[0::2], v[1::2]

    *feed_chunks, both = call(
        feed_weights,
        [head],
        [after(cm, other), ga, hidden, w_down, third, g_up, g_feed],
        [out((rows, width + 3 * hw + pad), BF) for _ in range(4)] + [out((width, 2 * ff), BF)],
    )
    both = exchange(after(both, far).reshape(n, kr, 2 * ff))
    feed_mine, feed_near, feed_other = near_terms(after(tuple(feed_chunks), far))
    far, feed_other = lax.optimization_barrier((far, feed_other))
    feed_far = swap(feed_other, 2)
    dq, dpair, gas, g_proj, *chunks, vec_d = call(
        cross_back,
        [head],
        [mine, near, far, cm_own, cinv, pair, cq, cprobs, w_later, ga, after_self, gain[None], mod, proj, w_out],
        [out((total, hw), BF), out((2, slots, hw), BF), deep, deep]
        + [out(packed, BF) for _ in range(4)]
        + [out((8, width), F32)],
        [pltpu.VMEM((heads, slots, total), BF)],
    )
    mine, near, other = near_terms(chunks)
    other, feed_far = lax.optimization_barrier((other, feed_far))
    far = swap(other, 2)
    *mid, out0, out1, out2, out3, output_frames, gv_gate2 = call(
        partial(mid_weights, kr=kr),
        [place],
        [feed_mine, feed_near, feed_far, across, cotangent, mod, dn_bias[None]]
        + [after(sm, other), g_proj, caption, dpair, w_later, second, dq],
        halves(4 * hw)
        + [out((rows, 4 * hw), BF) for _ in range(4)]
        + [out((rows, width), BF), out((1, width), F32)],
        [pltpu.VMEM((width, 4 * hw), BF)],
    )
    out_mine, out_near, out_other = near_terms(after((out0, out1, out2, out3), far))
    far, mid, out_other = lax.optimization_barrier((far, mid, out_other))
    out_far = swap(out_other, 2)
    mid = half_reduce(*parted(*mid))
    g_joint, *last, vec = call(
        partial(self_back, kr=kr),
        [place],
        [mine, near, far, sm_own, inv, qkv, probs, n_one, (w_own, (slice(None), slice(2 * hw, 5 * hw)))]
        + [mod, vec_c, vec_d, gv_gate2],
        [out((total, 3 * hw), BF)] + halves(3 * hw + pad) + [out((16, width), F32)],
        [pltpu.VMEM((heads, total, total), BF), pltpu.VMEM((width, 3 * hw + pad), BF)],
    )
    vec, mid, both, out_far = lax.optimization_barrier((vec, mid, both, out_far))
    near_rows, far_rows = parted(*last)
    last = half_reduce(near_rows, after(far_rows, mid))
    last_y = last
    shared = vec + swap(vec, 1)
    shared = shared + swap(shared, 2)
    vec = jnp.where(jnp.arange(16)[:, None] == 10, vec, shared).astype(BF)
    mid_y = mid
    sent_mid = []
    mid = rest_reduce(mid, sent_mid)
    third_shape = (width, hw) if kr % 16 else (n // 2, kr // 3, 3 * hw + pad)
    *outs, grad_captions = call(
        partial(out_rows, kr=kr),
        [place],
        [out_mine, out_near, after(out_far, vec)],
        [out(third_shape, BF) for _ in range(2)] + [out((1, slots, hw), F32)],
        [pltpu.VMEM((width, hw), BF)],
    )
    near_rows, far_rows = parted(*outs)
    if kr % 16:
        near_rows, far_rows = (
            jnp.pad(
                v.reshape(n // 2, 3, kr // 3, hw).transpose(0, 2, 1, 3).reshape(n // 2, kr // 3, 3 * hw),
                ((0, 0), (0, 0), (0, pad)),
            )
            for v in (near_rows, far_rows)
        )
    outs = half_reduce(near_rows, far_rows)
    vec = exchange(jnp.broadcast_to(after(vec, last_y)[None], (n, *vec.shape))).astype(F32)
    sent = []
    last = rest_reduce(jnp.concatenate([last, outs], axis=1), sent)
    outs = last[kr:]
    gf = call(first_back, [], [*x, g_joint, w_own, mod, after(gas, sent_mid[-1])], [out((rows, width), BF)] * 4)
    if kr % 16:
        outs = outs[:, : 3 * hw].reshape(own * 4 // 3, 3, hw).transpose(1, 0, 2).reshape(kr, hw)
    frame_mine, frame_near, frame_other = near_terms(gf)

    g_mod = vec[:, :6].reshape(n, 6 * width)
    g_cond = lax.dot_general(
        g_mod,
        modulation_weight.astype(F32),
        (((1,), (1,)), ((), ())),
        precision=lax.Precision.HIGHEST,
        preferred_element_type=F32,
    )
    g_silu = exchange(after(g_cond, frame_other)).reshape(width)
    g_cond = jax.vjp(jax.nn.silu, condition[0].astype(F32))[1](g_silu)[0]
    grad_condition = lax.dynamic_slice_in_dim(g_cond, h * hw, hw, 0)[None]
    cond_rows = lax.dynamic_slice_in_dim(cond_own, h * own, own, 1).astype(F32)
    grad_mod_weight = lax.dot_general(
        cond_rows, g_mod, (((0,), (0,)), ((), ())), precision=lax.Precision.HIGHEST, preferred_element_type=F32
    )
    sums = vec.sum(0)
    index = s * 4 + h
    mb = 6 * width // (4 * n)
    grad_mod_bias = lax.dynamic_slice_in_dim(sums[:6].reshape(6 * width), index * mb, mb, 0)

    def own_vec(i):
        return lax.dynamic_slice_in_dim(sums[6 + i], index * own, own, 0)

    both = both.astype(F32).sum(0)
    tiny = dict(small=1 << 20, limit=8)
    cols = call(column_chunks, [head], [mid, last, outs], [out((own, 8 * hw), BF) for _ in range(4)], **tiny)
    frame_far = swap(frame_other, 2)
    grad_frames = frame_mine.astype(F32) + frame_near.astype(F32) + frame_far.astype(F32)
    cols = [cols[0]] + [
        lax.ppermute(cols[j], "head", [(i, i ^ j) for i in range(4)]) for j in range(1, 4)
    ]
    grad_cross, grad_query, grad_pair, grad_out, grad_self = call(
        spread_columns, [head], cols, [out((own, k * width), F32) for k in (1, 1, 2, 1, 3)], **tiny
    )
    return (
        output_frames,
        grad_frames,
        grad_condition,
        grad_captions,
        grad_mod_weight,
        grad_mod_bias,
        grad_self,
        grad_out,
        own_vec(0),
        own_vec(1),
        grad_query,
        grad_pair,
        grad_cross,
        own_vec(2),
        both[:, :ff],
        sums[10],
        both[:, ff:].T,
        own_vec(3),
    )


def solution(mesh):
    both = ("seq", "head")
    return jax.shard_map(
        on_device,
        mesh=mesh,
        in_specs=(
            P(both, None),
            P("seq", None),
            P("seq", None, None),
            P("seq"),
            P("seq", None),
            P("seq"),
            P("seq", None),
            P("seq", None),
            P("seq"),
            P("seq"),
            P("seq", None),
            P("seq", None),
            P("seq", None),
            P("seq"),
            P("seq", "head"),
            P("head"),
            P("head", "seq"),
            P("seq"),
            P(both, None),
        ),
        out_specs=(
            P(both, None),
            P(both, None),
            P("seq", "head"),
            P("seq", None, "head"),
            P(both, None),
            P(both),
            P(both, None),
            P(both, None),
            P(both),
            P(both),
            P(both, None),
            P(both, None),
            P(both, None),
            P(both),
            P("seq", "head"),
            P("head"),
            P("head", "seq"),
            P(both),
        ),
        check_vma=False,
    )
```
